256 devices in a mesh: group: 2 (over x_hi), seq: 16 (over x_lo, z), tensor: 8 (over y, core).
Axes of the slice: x: 4 (x_hi: 2, x_lo: 2; x = x_hi * 2 + x_lo), y: 4, z: 8, core: 2. Of those that a mesh axis runs over, the one named last changes fastest.
Arguments:
- tokens: bfloat16 [2, 2048, 8192], P('group', 'seq', 'tensor'), may hold values from -6 to 6
- frame_feats: bfloat16 [2, 512, 1280], P('group', 'seq'), may hold values from -6 to 6
- w_proj: bfloat16 [1280, 8192], P(None, 'tensor'), may hold values from -0.15625 to 0.15625
- frame_pos: int32 [2, 512], P('group', 'seq'), may hold values from 0 to 2047, as said below
- segments: int32 [2, 2048], P('group', 'seq'), may hold values from 0 to 3, never falling along the last dimension, each value on 1 to 1024 neighbouring positions
- signs: int32 [2, 2048], P('group', 'seq'), may hold values from 0 to 1
- w_x: bfloat16 [8192, 8192], P(('group', 'seq'), 'tensor'), may hold values from -0.0625 to 0.0625
- w_bc: bfloat16 [8192, 2048], P(('group', 'seq'), 'tensor'), may hold values from -0.0625 to 0.0625
- w_dt: bfloat16 [8192, 128], P(('group', 'seq'), 'tensor'), may hold values from -0.0625 to 0.0625
- dt_bias: float32 [128], P('tensor'), may hold values from -4 to -2
- decay_rate: float32 [128], P('tensor'), may hold values from 0.0001 to 1
- skip_gain: float32 [128], P('tensor'), may hold values from 0.5 to 6
- probe: bfloat16 [2, 2048, 8192], P('group', 'seq', 'tensor'), may hold values from -6 to 6
Outputs:
- adv_tokens: bfloat16 [2, 2048, 8192], P('group', 'seq', 'tensor')
- adv_frames: bfloat16 [2, 512, 8192], P('group', 'seq', 'tensor')
The draws below stay inside these ranges and needn't reach their ends.
Inputs may be any that keep to these rules, and one draw needn't show every extreme that they name: `frame_pos`: within a sample the positions are distinct; frame token k * 32 + b * 2 + i (0 <= i < 2) lies in positions b * 128 to (b + 1) * 128 - 1. `segments`: document ids never fall along a sample.
All inputs are finite; a program needn't handle non-finite values.
Results may differ from the reference program's by a relative error of at most 0.0095.
Values may be sent and summed in bfloat16 or wider, within the bound.
No kernel may reach another device: no remote copies, remote signals or barrier semaphores. Data moves between devices by JAX's collectives and lax.ppermute only.
A program may use at most 128 MiB of HBM per device.

```python
import math
import jax
import jax.numpy as jnp
import numpy as np
from jax import lax

D = 8192
HEADS = 128
HEAD_DIM = 64
STATE = 128
GROUPS = 8
DV = 1280
TOK_DEV = 128
FB = 2
SEQ_LEN = 2048
F_DEV = 32
FRAMES = 512
SAMPLES = 2
N_TENSOR = 8


def draw_frame_pos(key, part):
    shards = F_DEV // FB
    keys = jax.random.split(jax.random.fold_in(key, 11), SAMPLES * shards)

    def one_shard(shard_key):
        return jax.random.permutation(shard_key, TOK_DEV)[:F_DEV].astype(jnp.int32)
    slots = jax.vmap(one_shard)(keys).reshape(SAMPLES, shards, shards, FB)
    offset = (jnp.arange(shards, dtype=jnp.int32) * TOK_DEV)[None, :, None, None]
    placed = slots + offset
    return jnp.transpose(placed, (0, 2, 1, 3)).reshape(SAMPLES, FRAMES).astype(jnp.int32)


def place_ends(values, rng, low, largest):
    dims = values.shape
    spot = [jax.random.randint(jax.random.fold_in(rng, axis), (), 0, dims[axis]) for axis in range(len(dims))]
    values = values.at[tuple(spot)].set(low)
    longest = dims.index(max(dims))
    spot[longest] = (spot[longest] + 1) % dims[longest]
    return values.at[tuple(spot)].set(largest)


def block_scale(key, shape, pieces, low, high):
    def one(dim, parts):
        steps = jax.random.uniform(jax.random.fold_in(jax.random.fold_in(key, 6), dim), (parts,), jnp.float32, low / len(pieces), high / len(pieces))
        return jnp.repeat(jnp.exp(steps), shape[dim] // parts).reshape((-1,) + (1,) * (len(shape) - dim - 1))

    gain = one(*pieces[0])
    for cut in pieces[1:]:
        gain = gain * one(*cut)
    return gain


def length_profile(count, total, limit, lean):
    weights = [(1 << 20) // math.isqrt(grade ** lean) + 1 for grade in range(2, count + 1)]
    surplus, holding = total - limit - (count - 1), [1] * (count - 1)
    while surplus > 0:
        candidates = [i for i in range(count - 1) if holding[i] < limit]
        mass, budget = sum([weights[i] for i in candidates]), surplus
        for i in candidates:
            extra = min(limit - holding[i], max(1, budget * weights[i] // mass), surplus)
            holding[i] = holding[i] + extra
            surplus = surplus - extra
    return np.array([limit] + holding)


def ragged_sizes(own_key, number_of, total, most, slope):
    if number_of == 2:
        one = jax.random.randint(own_key, (), max(1, total - most), min(most, total - 1) + 1)
        return jnp.stack([one, total - one])
    tallies = jnp.asarray(length_profile(number_of, total, most, slope), jnp.int32)
    couples = (number_of - 1) // 2
    giver, receiver = tallies[1:1 + 2 * couples:2], tallies[2:2 + 2 * couples:2]
    slack = jnp.minimum(giver - 1, most - receiver)
    moved = jax.random.randint(jax.random.fold_in(own_key, 1), (couples,), 0, 1 << 20) % (slack + 1)
    tallies = tallies.at[1:1 + 2 * couples:2].set(giver - moved).at[2:2 + 2 * couples:2].set(receiver + moved)
    return tallies[jax.random.permutation(jax.random.fold_in(own_key, 2), number_of)]


def noise(stream_key, extent, deviation, reach, pieces=(), held_as=jnp.bfloat16):
    loudness = block_scale(stream_key, extent, pieces, -0.22, 0.18) if pieces else 1.0
    values = jax.random.normal(stream_key, extent, jnp.float32) * deviation * loudness
    return jnp.minimum(jnp.maximum(values, -reach), reach).astype(held_as)


def setup_inputs(seed: int = 0) -> dict:
    seeds = jax.random.split(jax.random.key(seed), 14)
    return {
        "tokens": noise(seeds[0], (SAMPLES, SEQ_LEN, D), 1.0, 6.0, ((0, 2), (1, 16), (2, 8))),
        "frame_feats": noise(seeds[1], (SAMPLES, FRAMES, DV), 1.0, 6.0, ((0, 2), (1, 16))),
        "w_proj": noise(seeds[2], (DV, D), DV ** -0.5, 0.15625, ((1, 8),)),
        "frame_pos": draw_frame_pos(jax.random.fold_in(seeds[13], 71), 0),
        "segments": jax.vmap(lambda own: jnp.searchsorted(jnp.cumsum(ragged_sizes(own, 4, SEQ_LEN, SEQ_LEN // 2, 1)), jnp.arange(SEQ_LEN), side="right"))(jax.random.split(seeds[4], SAMPLES)).reshape((SAMPLES, SEQ_LEN)).astype(jnp.int32),
        "signs": place_ends(jax.random.randint(seeds[5], (SAMPLES, SEQ_LEN), 0, 2), jax.random.fold_in(seeds[5], 1), 0, 1).astype(jnp.int32),
        "w_x": noise(seeds[6], (D, HEADS * HEAD_DIM), D ** -0.5, 0.0625, ((0, 32), (1, 8))),
        "w_bc": noise(seeds[7], (D, GROUPS * 2 * STATE), D ** -0.5, 0.0625, ((0, 32), (1, 8))),
        "w_dt": noise(seeds[8], (D, HEADS), D ** -0.5, 0.0625, ((0, 32), (1, 8))),
        "dt_bias": jnp.clip(-4.0 + 2.0 * jax.random.uniform(seeds[9], (HEADS,), jnp.float32) ** block_scale(seeds[9], (HEADS,), ((0, 8),), -0.2, 0.2), -4.0, -2.0),
        "decay_rate": jnp.clip(jnp.exp(math.log(1.0) - 9.2103404 * jax.random.uniform(seeds[10], (HEADS,), jnp.float32) ** block_scale(seeds[10], (HEADS,), ((0, 8),), -0.2, 0.2)), 0.0001, 1.0),
        "skip_gain": jnp.clip(0.5 + 5.5 * jax.random.uniform(seeds[11], (HEADS,), jnp.float32) ** block_scale(seeds[11], (HEADS,), ((0, 8),), -0.2, 0.2), 0.5, 6.0),
        "probe": noise(seeds[12], (SAMPLES, SEQ_LEN, HEADS * HEAD_DIM), 1.0, 6.0, ((0, 2), (1, 16), (2, 8))),
    }


precise = lax.Precision.HIGHEST

def split_proj(proj_x, proj_bc, proj_dt, dt_bias):
    count = proj_x.shape[0]
    values = proj_x.reshape(count, -1, HEAD_DIM)
    pairs = proj_bc.reshape(count, -1, 2, STATE)
    step_sizes = jax.nn.softplus(proj_dt + dt_bias[None, :])
    return (values, pairs[:, :, 0], pairs[:, :, 1], step_sizes)

def block_state(proj_x, proj_bc, proj_dt, dt_bias, decay_rate, segment, seg_prev):
    values, b_proj, c_proj, step_sizes = split_proj(proj_x, proj_bc, proj_dt, dt_bias)
    repeat = values.shape[1] // b_proj.shape[1]
    log_decay = jnp.cumsum(-step_sizes * decay_rate[None, :], axis=0)
    end_decay = log_decay[-1]
    same_end = (segment == segment[-1])[:, None]
    tail_weight = jnp.where(same_end, jnp.exp(end_decay[None, :] - log_decay), 0.0) * step_sizes
    b_heads = jnp.repeat(b_proj, repeat, axis=1)
    end_states = jnp.einsum('sh,shp,shn->hpn', tail_weight, values, b_heads, precision=precise)
    carry_decay = jnp.where(segment[-1] == seg_prev, jnp.exp(end_decay), 0.0)
    return (end_states, carry_decay)

def block_loss(proj_x, proj_bc, proj_dt, dt_bias, decay_rate, skip_gain, segment, seg_prev, carried_in, probe):
    values, b_proj, c_proj, step_sizes = split_proj(proj_x, proj_bc, proj_dt, dt_bias)
    repeat = values.shape[1] // b_proj.shape[1]
    count = values.shape[0]
    log_decay = jnp.cumsum(-step_sizes * decay_rate[None, :], axis=0)
    position = jnp.arange(count)
    visible = (segment[:, None] == segment[None, :]) & (position[:, None] >= position[None, :])
    visible = visible[:, :, None]
    gap_decay = log_decay[:, None, :] - log_decay[None, :, :]
    decay = jnp.where(visible, jnp.exp(jnp.where(visible, gap_decay, 0.0)), 0.0)
    scores = jnp.einsum('tgn,sgn->tsg', c_proj, b_proj, precision=precise)
    scores = jnp.repeat(scores, repeat, axis=2)
    mixed = decay * scores * step_sizes[None, :, :]
    within = jnp.einsum('tsh,shp->thp', mixed, values, precision=precise)
    c_heads = jnp.repeat(c_proj, repeat, axis=1)
    carry_scale = jnp.where((segment == seg_prev)[:, None], jnp.exp(log_decay), 0.0)
    carried = jnp.einsum('thn,hpn->thp', c_heads, carried_in, precision=precise) * carry_scale[:, :, None]
    result = within + carried + skip_gain[None, :, None] * values
    return jnp.sum(result.reshape(count, -1) * probe.astype(jnp.float32))

def sample_step(tokens, frame_feats, w_proj, frame_pos, segments, sign_bits, w_x, w_bc, w_dt, dt_bias, decay_rate, skip_gain, probe):
    frame_emb = jnp.dot(frame_feats, w_proj, preferred_element_type=jnp.float32).astype(jnp.bfloat16)
    merged = tokens.at[frame_pos].set(frame_emb)
    proj_x = jnp.dot(merged, w_x, preferred_element_type=jnp.float32)
    proj_bc = jnp.dot(merged, w_bc, preferred_element_type=jnp.float32)
    proj_dt = jnp.dot(merged, w_dt, preferred_element_type=jnp.float32)
    blocks = SEQ_LEN // TOK_DEV
    seg_blocks = segments.reshape(blocks, TOK_DEV)
    seg_prev = jnp.concatenate([jnp.zeros((1,), jnp.int32), seg_blocks[:-1, -1].astype(jnp.int32)])
    probe_blocks = probe.reshape(blocks, TOK_DEV, -1)

    def total(px, pbc, pdt):
        bx = px.reshape(blocks, TOK_DEV, -1)
        bbc = pbc.reshape(blocks, TOK_DEV, -1)
        bdt = pdt.reshape(blocks, TOK_DEV, -1)

        def state_item(item):
            return block_state(item[0], item[1], item[2], dt_bias, decay_rate, item[3], item[4])
        end_states, decays = lax.map(state_item, (bx, bbc, bdt, seg_blocks, seg_prev))

        def advance(state, item):
            return (item[0][:, None, None] * state + item[1], state)
        _, entering = lax.scan(advance, jnp.zeros(end_states.shape[1:], jnp.float32), (decays, end_states))

        def loss_item(item):
            return block_loss(item[0], item[1], item[2], dt_bias, decay_rate, skip_gain, item[3], item[4], item[5], item[6])
        losses = lax.map(jax.checkpoint(loss_item), (bx, bbc, bdt, seg_blocks, seg_prev, entering, probe_blocks))
        return jnp.sum(losses)
    _, pull = jax.vjp(total, proj_x, proj_bc, proj_dt)
    grad_x, grad_bc, grad_dt = pull(jnp.ones((), jnp.float32))
    grad_x = grad_x.astype(jnp.bfloat16)
    grad_bc = grad_bc.astype(jnp.bfloat16)
    grad_dt = grad_dt.astype(jnp.bfloat16)
    width_x = grad_x.shape[1] // N_TENSOR
    width_bc = grad_bc.shape[1] // N_TENSOR
    width_dt = grad_dt.shape[1] // N_TENSOR
    gradient = jnp.zeros(merged.shape, jnp.float32)
    for j in range(N_TENSOR):
        part = jnp.dot(grad_x[:, j * width_x:(j + 1) * width_x], w_x[:, j * width_x:(j + 1) * width_x].T, preferred_element_type=jnp.float32)
        part = part + jnp.dot(grad_bc[:, j * width_bc:(j + 1) * width_bc], w_bc[:, j * width_bc:(j + 1) * width_bc].T, preferred_element_type=jnp.float32)
        part = part + jnp.dot(grad_dt[:, j * width_dt:(j + 1) * width_dt], w_dt[:, j * width_dt:(j + 1) * width_dt].T, preferred_element_type=jnp.float32)
        gradient = gradient + lax.optimization_barrier(part.astype(jnp.bfloat16)).astype(jnp.float32)
    grad_scale = jnp.sqrt(jnp.mean(gradient * gradient) + 1e-06)
    direction = (2 * sign_bits - 1).astype(jnp.float32)[:, None]
    adv = (merged.astype(jnp.float32) + 0.5 * direction * gradient / grad_scale).astype(jnp.bfloat16)
    return (adv, adv[frame_pos])

def reference(tokens, frame_feats, w_proj, frame_pos, segments, signs, w_x, w_bc, w_dt, dt_bias, decay_rate, skip_gain, probe):
    token_outs = []
    frame_outs = []
    for sample in range(SAMPLES):
        adv, frames = sample_step(tokens[sample], frame_feats[sample], w_proj, frame_pos[sample], segments[sample], signs[sample], w_x, w_bc, w_dt, dt_bias, decay_rate, skip_gain, probe[sample])
        token_outs.append(adv)
        frame_outs.append(frames)
    return (jnp.stack(token_outs), jnp.stack(frame_outs))
```

```python
import jax
import jax.numpy as jnp
from jax import lax
from jax.sharding import Mesh, PartitionSpec as P

HEAD_DIM = 64
SEQ = ("x_lo", "z")
TENSOR = ("y", "core")
STATE = 128


precise = lax.Precision.HIGHEST


def from_behind(x, axis, by):
    size = lax.axis_size(axis)
    pairs = [(i, i + by) for i in range(size) if 0 <= i + by < size]
    return lax.ppermute(x, axis, pairs)


def carried_in(x, axis, later):
    size, mine = (lax.axis_size(axis), lax.axis_index(axis))
    decays, states = jax.tree.map(lambda part: lax.all_gather(part.astype(jnp.bfloat16), axis), x)
    decays = decays.astype(jnp.float32)
    weights = [None] * size
    run = jnp.ones_like(decays[0])
    for k in range(size) if later else reversed(range(size)):
        reached = (k > mine) if later else (k < mine)
        weights[k] = jnp.where(reached, run, 0.0)
        run = jnp.where(reached, run * decays[k], run)
    weights = jnp.stack(weights)
    return jnp.sum(weights[:, :, None, None] * states.astype(jnp.float32), axis=0)


def split_proj(proj_x, proj_bc, proj_dt, dt_bias):
    count = proj_x.shape[0]
    values = proj_x.reshape(count, -1, HEAD_DIM)
    pairs = proj_bc.reshape(count, -1, 2, STATE)
    step_sizes = jax.nn.softplus(proj_dt + dt_bias[None, :])
    return (values, pairs[:, :, 0], pairs[:, :, 1], step_sizes)


def block_state(proj_x, proj_bc, proj_dt, dt_bias, decay_rate, segment, seg_prev):
    values, b_proj, c_proj, step_sizes = split_proj(proj_x, proj_bc, proj_dt, dt_bias)
    repeat = values.shape[1] // b_proj.shape[1]
    log_decay = jnp.cumsum(-step_sizes * decay_rate[None, :], axis=0)
    end_decay = log_decay[-1]
    same_end = (segment == segment[-1])[:, None]
    tail_weight = jnp.where(same_end, jnp.exp(end_decay[None, :] - log_decay), 0.0) * step_sizes
    b_heads = jnp.repeat(b_proj, repeat, axis=1)
    end_states = jnp.einsum("sh,shp,shn->hpn", tail_weight, values, b_heads, precision=precise)
    carry_decay = jnp.where(segment[-1] == seg_prev, jnp.exp(end_decay), 0.0)
    return (end_states, carry_decay)


def block_loss(
    proj_x, proj_bc, proj_dt, dt_bias, decay_rate, skip_gain, segment, seg_prev, carried_in, probe
):
    values, b_proj, c_proj, step_sizes = split_proj(proj_x, proj_bc, proj_dt, dt_bias)
    repeat = values.shape[1] // b_proj.shape[1]
    count = values.shape[0]
    log_decay = jnp.cumsum(-step_sizes * decay_rate[None, :], axis=0)
    position = jnp.arange(count)
    visible = (segment[:, None] == segment[None, :]) & (position[:, None] >= position[None, :])
    visible = visible[:, :, None]
    gap_decay = log_decay[:, None, :] - log_decay[None, :, :]
    decay = jnp.where(visible, jnp.exp(jnp.where(visible, gap_decay, 0.0)), 0.0)
    scores = jnp.einsum("tgn,sgn->tsg", c_proj, b_proj, precision=precise)
    scores = jnp.repeat(scores, repeat, axis=2)
    mixed = decay * scores * step_sizes[None, :, :]
    within = jnp.einsum("tsh,shp->thp", mixed, values, precision=precise)
    c_heads = jnp.repeat(c_proj, repeat, axis=1)
    carry_scale = jnp.where((segment == seg_prev)[:, None], jnp.exp(log_decay), 0.0)
    carried = (
        jnp.einsum("thn,hpn->thp", c_heads, carried_in, precision=precise) * carry_scale[:, :, None]
    )
    result = within + carried + skip_gain[None, :, None] * values
    return jnp.sum(result.reshape(count, -1) * probe.astype(jnp.float32))


def body(
    tokens,
    frame_feats,
    w_proj,
    frame_pos,
    segments,
    signs,
    w_x,
    w_bc,
    w_dt,
    dt_bias,
    decay_rate,
    skip_gain,
    probe,
):
    rows = tokens.shape[1]
    seq_count = lax.axis_size(SEQ)
    own_index = lax.axis_index(SEQ)
    frame_emb = jnp.dot(frame_feats[0], w_proj, preferred_element_type=jnp.float32).astype(
        jnp.bfloat16
    )
    arrived, arrived_pos = (
        lax.all_to_all(frame_emb, SEQ, split_axis=0, concat_axis=0, tiled=True),
        lax.all_to_all(frame_pos[0], SEQ, split_axis=0, concat_axis=0, tiled=True),
    )
    local_pos = arrived_pos - own_index * rows
    merged = tokens[0].at[local_pos].set(arrived)
    segment = segments[0]
    edge_ids = from_behind(segment[-1:], SEQ, 1)
    seg_prev = edge_ids[0]
    features = lax.all_gather(merged, TENSOR, axis=1, tiled=True)
    whole_x, whole_bc, whole_dt = (
        lax.all_gather(w_x, ("x_hi",) + SEQ, axis=0, tiled=True),
        lax.all_gather(w_bc, ("x_hi",) + SEQ, axis=0, tiled=True),
        lax.all_gather(w_dt, ("x_hi",) + SEQ, axis=0, tiled=True),
    )
    proj_x = jnp.dot(features, whole_x, preferred_element_type=jnp.float32)
    proj_bc = jnp.dot(features, whole_bc, preferred_element_type=jnp.float32)
    proj_dt = jnp.dot(features, whole_dt, preferred_element_type=jnp.float32)

    def state_of(part_x, part_bc, part_dt):
        return block_state(part_x, part_bc, part_dt, dt_bias, decay_rate, segment, seg_prev)

    (end_states, carry_decay), pull_state = jax.vjp(state_of, proj_x, proj_bc, proj_dt)
    entering = carried_in((carry_decay, end_states), SEQ, False)

    def loss_of(part_x, part_bc, part_dt, carried_in):
        return block_loss(
            part_x,
            part_bc,
            part_dt,
            dt_bias,
            decay_rate,
            skip_gain,
            segment,
            seg_prev,
            carried_in,
            probe[0],
        )

    _, pull_loss = jax.vjp(loss_of, proj_x, proj_bc, proj_dt, entering)
    loss_gx, loss_gbc, loss_gdt, local_grad = pull_loss(jnp.ones((), jnp.float32))
    leaving_grad = carried_in((carry_decay, local_grad), SEQ, True)
    decay_grad = jnp.sum(leaving_grad * entering, axis=(1, 2))
    state_gx, state_gbc, state_gdt = pull_state((leaving_grad, decay_grad))
    grad_x = (loss_gx + state_gx).astype(jnp.bfloat16)
    grad_bc = (loss_gbc + state_gbc).astype(jnp.bfloat16)
    grad_dt = (loss_gdt + state_gdt).astype(jnp.bfloat16)
    partial_value = jnp.dot(grad_x, whole_x.T, preferred_element_type=jnp.float32)
    partial_value = partial_value + jnp.dot(grad_bc, whole_bc.T, preferred_element_type=jnp.float32)
    partial_value = partial_value + jnp.dot(grad_dt, whole_dt.T, preferred_element_type=jnp.float32)
    gradient = lax.psum_scatter(
        partial_value.astype(jnp.bfloat16), TENSOR, scatter_dimension=1, tiled=True
    ).astype(jnp.float32)
    entries = rows * seq_count * gradient.shape[1] * lax.axis_size(TENSOR)
    squares = jnp.sum(gradient * gradient)
    for axis in ("core", "y", "z", "x_lo"):
        squares = lax.psum(squares, axis)
    grad_scale = jnp.sqrt(squares / entries + 1e-06)
    direction = (2 * signs[0] - 1).astype(jnp.float32)[:, None]
    adv = (merged.astype(jnp.float32) + 0.5 * direction * gradient / grad_scale).astype(
        jnp.bfloat16
    )
    picked = adv[local_pos]
    returned = lax.all_to_all(picked, SEQ, split_axis=0, concat_axis=0, tiled=True)
    return (adv[None], returned[None])


def solution(mesh):
    mesh = Mesh(mesh.devices.reshape(2, 2, 8, 4, 2), ("x_hi", "x_lo", "z", "y", "core"))
    return jax.shard_map(
        body,
        mesh=mesh,
        in_specs=(
            P("x_hi", SEQ, TENSOR),
            P("x_hi", SEQ, None),
            P(None, TENSOR),
            P("x_hi", SEQ),
            P("x_hi", SEQ),
            P("x_hi", SEQ),
            P(("x_hi",) + SEQ, TENSOR),
            P(("x_hi",) + SEQ, TENSOR),
            P(("x_hi",) + SEQ, TENSOR),
            P(TENSOR),
            P(TENSOR),
            P(TENSOR),
            P("x_hi", SEQ, TENSOR),
        ),
        out_specs=(P("x_hi", SEQ, TENSOR), P("x_hi", SEQ, TENSOR)),
        check_vma=False,
    )
```

```python
import jax
import jax.numpy as jnp
from jax import lax
from jax.experimental import pallas as pl
from jax.experimental.pallas import tpu as pltpu
from jax.sharding import Mesh, PartitionSpec as P

F32, BF16 = jnp.float32, jnp.bfloat16
AXES = ("x_hi", "x_lo", "z", "y", "core")
X = ("x_hi", "x_lo")
SEQ = ("x_lo", "z")
TENSOR = ("y", "core")
CHUNK = 128
WIDE = 1408
HIGH = lax.Precision.HIGHEST
VMEM = pl.BlockSpec(memory_space=pltpu.VMEM)
SMEM = pl.BlockSpec(memory_space=pltpu.SMEM)


def linear(x, z, y, core):
    return ((x * 8 + z) * 4 + y) * 2 + core


def features_route():
    pairs = []
    for x in range(4):
        for z in range(8):
            for y in range(4):
                for core in range(2):
                    there = linear(y, 4 * (z // 4) + x, (z % 4 + x) % 4, core)
                    pairs.append((linear(x, z, y, core), there))
    return pairs


def probe_route():
    pairs = []
    for x in range(4):
        for z in range(8):
            pairs.append((x * 8 + z, (z % 4) * 8 + 4 * (z // 4) + x))
    return pairs


def quarter_route(k):
    pairs = []
    for z in range(8):
        sample, quarter = (z % 4) // 2, 2 * (z % 2) + z // 4
        to = (quarter + k) % 4
        pairs.append((z, 4 * (to % 2) + 2 * sample + to // 2))
    return pairs


def dot_nt(a, b):
    return lax.dot_general(a, b, (((1,), (1,)), ((), ())), preferred_element_type=F32)


def dot_tn(a, b):
    return lax.dot_general(a, b, (((0,), (0,)), ((), ())), preferred_element_type=F32)


def dot_nn(a, b):
    return jnp.dot(a, b, preferred_element_type=F32)


def iota(shape, dim):
    return lax.broadcasted_iota(jnp.int32, shape, dim)


def spread(columns):
    left = iota((CHUNK, 128), 1) < 64
    tiles = [
        jnp.where(left, jnp.broadcast_to(columns[2 * i], (CHUNK, 128)), jnp.broadcast_to(columns[2 * i + 1], (CHUNK, 128)))
        for i in range(2)
    ]
    return jnp.concatenate(tiles, axis=1)


def by_head_rows(values):
    rows = iota((256, 128), 0)
    out = jnp.broadcast_to(values[3], (256, 128))
    for h in (2, 1, 0):
        out = jnp.where(rows < 64 * (h + 1), jnp.broadcast_to(values[h], (256, 128)), out)
    return out


def lanes(row):
    return [row[:, h : h + 1] for h in range(4)]


def weights_of(rows, cols):
    seg = cols[:, 12:13]
    prev, last = rows[13:14, 127:128], rows[12:13, 127:128]
    end = cols[127:128, :]
    carry = jnp.where(seg == prev, jnp.exp(cols), 0.0)
    tail = jnp.where(seg == last, jnp.exp(end - cols), 0.0)
    through = jnp.where(last == prev, jnp.exp(end), 0.0)
    return carry, tail, through


def project_kernel(meta, own, oth, w, out, acc):
    i = pl.program_id(0)
    cols = pl.ds(pl.multiple_of(lax.rem(i, 4) * 256, 256), 256)

    def product(ref):
        rows = jnp.concatenate([ref[lax.rem(k + meta[1], 4), :, cols] for k in range(4)], axis=0)
        return dot_nn(rows, w[0])

    @pl.when(i == 0)
    def _():
        acc[...] = product(own)

    @pl.when((i > 0) & (i < 4))
    def _():
        acc[...] += product(own)

    @pl.when(i >= 4)
    def _():
        acc[...] += product(oth)

    @pl.when(i == 7)
    def _():
        steps = acc[:, 1280:1408].T
        for d in range(4):
            out[d, 0:512, 0:256] = acc[:, 256 * d : 256 * d + 256].astype(BF16)
            out[d, 0:512, 256:512] = acc[:, 1024:1280].astype(BF16)
            mine = jnp.concatenate([steps[4 * d : 4 * d + 4], jnp.zeros((12, 512), F32)], axis=0)
            out[d, 512:528, :] = mine.astype(BF16)


def project(meta, own, oth, w):
    whole = lambda i, m: (0, 0, 0)
    return pl.pallas_call(
        project_kernel,
        out_shape=jax.ShapeDtypeStruct((4, 528, 512), BF16),
        grid_spec=pltpu.PrefetchScalarGridSpec(
            num_scalar_prefetch=1,
            grid=(8,),
            in_specs=[
                pl.BlockSpec((4, 128, 1024), whole),
                pl.BlockSpec((4, 128, 1024), whole),
                pl.BlockSpec((1, 256, WIDE), lambda i, m: (lax.rem(m[0] + i // 4, 2) * 4 + lax.rem(i, 4), 0, 0)),
            ],
            out_specs=pl.BlockSpec((4, 528, 512), whole),
            scratch_shapes=[pltpu.VMEM((512, WIDE), F32)],
        ),
    )(meta, own, oth, w)


def prepare_kernel(meta, r, p, prm, pay, x, bc, rows_out, cols_out, t_out, q_out):
    total = r[0, 0:512, :].astype(F32)
    raw = r[0, 512:528, :].astype(F32)
    for d in range(1, 4):
        total += r[d, 0:512, :].astype(F32)
        raw += r[d, 512:528, :].astype(F32)
    x[...] = total[:, 0:256]
    bc[...] = total[:, 256:512].astype(BF16)
    upper = (iota((128, 128), 0) <= iota((128, 128), 1)).astype(F32)
    top = iota((8, 128), 0) < 4
    bias, rate = prm[0], prm[1]
    through = []
    for k in range(4):
        here = slice(128 * k, 128 * k + 128)
        z = raw[0:8, here] + bias
        dt = jnp.maximum(z, 0.0) + jnp.log1p(jnp.exp(-jnp.abs(z)))
        logs = jnp.dot(-dt * rate, upper, precision=HIGH, preferred_element_type=F32)
        seg = p[k, 128:144, 0:128].astype(F32)[0:8]
        rows = jnp.concatenate([jnp.where(top, logs, pltpu.roll(dt, 4, 0)), jnp.where(top, z, pltpu.roll(seg, 4, 0))], axis=0)
        cols = jnp.concatenate([rows, jnp.zeros((112, 128), F32)], axis=0).T
        rows_out[k] = rows
        cols_out[k] = cols
        carry, tail, thru = weights_of(rows, cols)
        through.append(thru)
        carry_x = spread(lanes(carry))
        tail_x = spread([tail[:, h : h + 1] * cols[:, 4 + h : 5 + h] for h in range(4)])
        b, c = bc[here, 0:128], bc[here, 128:256]
        t_out[k] = dot_tn((x[here, :] * tail_x).astype(BF16), b)
        q_out[k] = dot_tn((p[k, 0:128, :].astype(F32) * carry_x).astype(BF16), c)
    state = t_out[0]
    grad = q_out[3]
    whole = through[0]
    for k in range(1, 4):
        state = by_head_rows(lanes(through[k])) * state + t_out[k]
        grad = by_head_rows(lanes(through[3 - k])) * grad + q_out[3 - k]
        whole = whole * through[k]
    for k in range(1, 4):
        pay[k - 1, 0:256, :] = jnp.where(meta[2] + k < 4, state, grad).astype(BF16)
        pay[k - 1, 256:272, :] = jnp.broadcast_to(whole, (16, 128)).astype(BF16)


def prepare(meta, r, p, prm):
    return pl.pallas_call(
        prepare_kernel,
        in_specs=[SMEM, VMEM, VMEM, VMEM],
        out_specs=[VMEM] * 7,
        out_shape=[
            jax.ShapeDtypeStruct((3, 272, 128), BF16),
            jax.ShapeDtypeStruct((512, 256), F32),
            jax.ShapeDtypeStruct((512, 256), BF16),
            jax.ShapeDtypeStruct((4, 16, 128), F32),
            jax.ShapeDtypeStruct((4, 128, 128), F32),
            jax.ShapeDtypeStruct((4, 256, 128), F32),
            jax.ShapeDtypeStruct((4, 256, 128), F32),
        ],
    )(meta, r, p, prm)


def intra_kernel(x, bc, p, rows_in, cols_in, skip, dx, dbc, e):
    seen = iota((128, 128), 0) >= iota((128, 128), 1)
    lane = iota((128, 128), 1)
    for k in range(4):
        here = slice(128 * k, 128 * k + 128)
        b, c = bc[here, 0:128], bc[here, 128:256]
        rows, cols = rows_in[k], cols_in[k]
        scores = dot_nt(c, b)
        visible = (cols[:, 12:13] == rows[12:13, :]) & seen
        d_scores = jnp.zeros((128, 128), F32)
        by_row = jnp.zeros((128, 128), F32)
        sums = []
        for tile in range(2):
            part = slice(128 * tile, 128 * tile + 128)
            probe = p[k, 0:128, part].astype(F32)
            values = x[here, part].astype(BF16)
            d_values = skip[:, part] * probe
            for a in range(2):
                h = 2 * tile + a
                mine = jnp.where((lane < 64) if a == 0 else (lane >= 64), probe, 0.0).astype(BF16)
                pulled = dot_nt(mine, values)
                decay = jnp.exp(jnp.where(visible, cols[:, h : h + 1] - rows[h : h + 1, :], -1e30))
                steps = rows[4 + h : 5 + h, :]
                weighted = decay * pulled
                decayed = decay * scores
                plain = weighted * scores
                sums.append(jnp.sum(plain, axis=0, keepdims=True))
                by_row = jnp.where(lane == h, jnp.sum(plain * steps, axis=1, keepdims=True), by_row)
                d_scores += weighted * steps
                d_values += dot_tn((decayed * steps).astype(BF16), mine)
            dx[here, part] = d_values
        d_scores = d_scores.astype(BF16)
        dbc[here, 0:128] = dot_tn(d_scores, c)
        dbc[here, 128:256] = dot_nn(d_scores, b)
        sub = iota((8, 128), 0)
        down = jnp.zeros((8, 128), F32)
        for h in range(4):
            down = jnp.where(sub == h, jnp.broadcast_to(sums[h], (8, 128)), down)
        dt = pltpu.roll(rows[0:8], 4, 0)
        e[k, 0:8, :] = down
        e[k, 8:16, :] = by_row.T[0:8] - dt * down


def intra(x, bc, p, rows, cols, skip):
    return pl.pallas_call(
        intra_kernel,
        in_specs=[VMEM] * 6,
        out_specs=[VMEM] * 3,
        out_shape=[
            jax.ShapeDtypeStruct((512, 256), F32),
            jax.ShapeDtypeStruct((512, 256), F32),
            jax.ShapeDtypeStruct((4, 16, 128), F32),
        ],
    )(x, bc, p, rows, cols, skip)


def finish_kernel(meta, r1, r2, r3, x, bc, p, rows_in, cols_in, t_in, q_in, dx, dbc, e, prm, out):
    quarter = meta[2]
    got = (r1, r2, r3)
    parts = [ref[0:256, :].astype(F32) for ref in got]
    decays = [by_head_rows(lanes(ref[256:272, :].astype(F32)[0:1])) for ref in got]

    def total(order):
        out_sum = jnp.zeros((256, 128), F32)
        run = jnp.ones((256, 128), F32)
        for index, valid in order:
            out_sum += jnp.where(valid, run * parts[index], 0.0)
            run = jnp.where(valid, run * decays[index], run)
        return out_sum

    entering = total([(k - 1, quarter - k >= 0) for k in (1, 2, 3)])
    leaving = total([(3 - m, quarter + m <= 3) for m in (1, 2, 3)])
    weights = [weights_of(rows_in[k], cols_in[k]) for k in range(4)]
    through = [by_head_rows(lanes(weights[k][2])) for k in range(4)]
    states, grads = [entering], [leaving]
    for k in range(3):
        states.append(through[k] * states[k] + t_in[k])
        grads.append(through[3 - k] * grads[k] + q_in[3 - k])
    grads = grads[::-1]
    indicator = (iota((8, 256), 1) // 64 == iota((8, 256), 0)).astype(F32)
    lower = (iota((128, 128), 0) >= iota((128, 128), 1)).astype(F32)
    sub, lane = iota((8, 128), 0), iota((8, 128), 1)
    rate = prm[1]

    def by_head(product):
        dims = (((1,), (1,)), ((), ()))
        return lax.dot_general(indicator, product, dims, precision=HIGH, preferred_element_type=F32)

    for k in range(4):
        here = slice(128 * k, 128 * k + 128)
        rows, cols = rows_in[k], cols_in[k]
        carry, tail, thru = weights[k]
        b, c = bc[here, 0:128], bc[here, 128:256]
        carry_x = spread(lanes(carry))
        tail_x = spread(lanes(tail))
        step_x = spread([cols[:, 4 + h : 5 + h] for h in range(4)])
        state, grad = states[k].astype(BF16), grads[k].astype(BF16)
        probe = p[k, 0:128, :].astype(F32) * carry_x
        values = x[here, :] * tail_x
        carried = probe * dot_nt(c, state)
        pulled = dot_nt(b, grad)
        out[here, 0:256] = (dx[here, :] + tail_x * step_x * pulled).astype(BF16)
        d_b = dbc[here, 0:128] + dot_nn((values * step_x).astype(BF16), grad)
        d_c = dbc[here, 128:256] + dot_nn(probe.astype(BF16), state)
        out[here, 256:384] = d_b.astype(BF16)
        out[here, 384:512] = d_c.astype(BF16)
        from_carry = by_head(carried)
        from_tail = by_head(values * pulled)
        dt = pltpu.roll(rows[0:8], 4, 0)
        d_log = e[k, 8:16, :] + from_carry - dt * from_tail
        both = jnp.sum(grads[k] * states[k], axis=1, keepdims=True)
        end = jnp.sum(jnp.where(sub < 4, dt * from_tail, 0.0), axis=1, keepdims=True)
        for h in range(4):
            own = jnp.sum(both[64 * h : 64 * h + 64], axis=0, keepdims=True) * thru[:, h : h + 1]
            end = jnp.where(sub[:, 0:1] == h, end + own, end)
        d_log = jnp.where(lane == 127, d_log + end, d_log)
        d_step = jnp.dot(d_log, lower, precision=HIGH, preferred_element_type=F32)
        d_dt = e[k, 0:8, :] + from_tail - rate * d_step
        z = rows[8:16]
        d_z = jnp.where(sub < 4, d_dt / (1.0 + jnp.exp(-z)), 0.0)
        out[512:528, here] = jnp.concatenate([d_z, jnp.zeros((8, 128), F32)], axis=0).astype(BF16)


def finish(meta, *args):
    return pl.pallas_call(
        finish_kernel,
        in_specs=[SMEM] + [VMEM] * len(args),
        out_specs=VMEM,
        out_shape=jax.ShapeDtypeStruct((528, 512), BF16),
    )(meta, *args)


def pull_kernel(meta, g, w, oth, own, full):
    i = pl.program_id(0)

    @pl.when(i == 0)
    def _():
        shared = g[0, 0:512, 256:512].astype(F32)
        for d in range(4):
            full[:, 256 * d : 256 * d + 256] = g[d, 0:512, 0:256]
            if d:
                shared += g[d, 0:512, 256:512].astype(F32)
        full[:, 1024:1280] = shared.astype(BF16)
        top = iota((8, 512), 0) < 4
        steps = [g[d, 512:528, :].astype(F32)[0:8] for d in range(4)]
        pairs = [jnp.where(top, steps[2 * j], pltpu.roll(steps[2 * j + 1], 4, 0)) for j in range(2)]
        tall = jnp.concatenate(pairs + [jnp.zeros((112, 512), F32)], axis=0)
        full[:, 1280:1408] = tall.T.astype(BF16)

    part = dot_nt(full[...], w[0]).astype(BF16)
    cols = pl.ds(pl.multiple_of(lax.rem(i, 4) * 256, 256), 256)

    def put(ref):
        for k in range(4):
            ref[lax.rem(k + meta[1], 4), :, cols] = part[128 * k : 128 * k + 128]

    @pl.when(i < 4)
    def _():
        put(oth)

    @pl.when(i >= 4)
    def _():
        put(own)


def pull(meta, g, w):
    whole = lambda i, m: (0, 0, 0)
    return pl.pallas_call(
        pull_kernel,
        out_shape=[jax.ShapeDtypeStruct((4, 128, 1024), BF16)] * 2,
        grid_spec=pltpu.PrefetchScalarGridSpec(
            num_scalar_prefetch=1,
            grid=(8,),
            in_specs=[
                pl.BlockSpec((4, 528, 512), whole),
                pl.BlockSpec((1, 256, WIDE), lambda i, m: (lax.rem(m[0] + 1 + i // 4, 2) * 4 + lax.rem(i, 4), 0, 0)),
            ],
            out_specs=[pl.BlockSpec((4, 128, 1024), whole)] * 2,
            scratch_shapes=[pltpu.VMEM((512, WIDE), BF16)],
        ),
    )(meta, g, w)


def to_all(x, axis):
    return lax.all_to_all(jnp.broadcast_to(x[None], (4,) + x.shape), axis, split_axis=0, concat_axis=0)


def shifted(x, axis, k):
    return lax.ppermute(x, axis, [(i, (i + k) % 4) for i in range(4)])


def sum_of_four(x, axis):
    return x + shifted(x, axis, 1) + shifted(x, axis, 2) + shifted(x, axis, 3)


SWAP = [(0, 1), (1, 0)]


def body(tokens, frame_feats, w_proj, frame_pos, segments, signs, w_x, w_bc, w_dt, dt_bias, decay_rate, skip_gain, probe):
    x_at, z_at, core_at = lax.axis_index(X), lax.axis_index("z"), lax.axis_index("core")
    quarter = 2 * lax.rem(z_at, 2) + z_at // 4
    meta = jnp.stack([core_at, lax.rem(z_at, 4), quarter]).astype(jnp.int32)

    w_all = jnp.concatenate([w_x, w_bc, w_dt, jnp.zeros((256, 112), BF16)], axis=1)
    weights = lax.all_gather(w_all, "z")

    frame_emb = jnp.dot(frame_feats[0], w_proj, preferred_element_type=F32).astype(BF16)
    slot = frame_pos[0] - CHUNK * (jnp.arange(32, dtype=jnp.int32) // 2)
    tagged = jnp.concatenate([frame_emb, jnp.broadcast_to(slot.astype(BF16)[:, None], (32, 128))], axis=1)
    arrived = lax.all_to_all(tagged, SEQ, split_axis=0, concat_axis=0, tiled=True)
    local_pos = arrived[:, 1024].astype(jnp.int32)
    merged = tokens[0].at[local_pos].set(arrived[:, :1024])

    moved = lax.ppermute(merged, AXES, features_route())
    own = to_all(moved, "y")
    oth = lax.ppermute(own, "core", SWAP)

    segment = segments[0]
    before = lax.ppermute(segment[-1:], X + ("z",), [(i, i + 1) for i in range(31)])
    ids = jnp.concatenate([segment[None], jnp.broadcast_to(before[None], (15, CHUNK))]).astype(BF16)
    probe_ids = jnp.concatenate([probe[0], jnp.tile(ids, (1, 8))], axis=0)
    probe_ids = lax.ppermute(probe_ids, X + ("z",), probe_route())
    probe_ids = probe_ids.reshape(144, 4, 256).transpose(1, 0, 2)
    probe_ids = lax.all_to_all(probe_ids, X, split_axis=0, concat_axis=0)

    def four(v):
        return lax.dynamic_slice(v, (4 * x_at,), (4,))

    prm = jnp.stack([four(dt_bias), four(decay_rate)])
    prm = jnp.concatenate([prm, jnp.zeros((2, 4), F32)], axis=1)
    prm = jnp.broadcast_to(prm[:, :, None], (2, 8, 128))
    skip = jnp.repeat(four(skip_gain), 64)[None, :]

    partial_proj = project(meta, own, oth, weights)
    received = lax.all_to_all(partial_proj, X, split_axis=0, concat_axis=0)
    pay, values, bc, rows, cols, t_all, q_all = prepare(meta, received, probe_ids, prm)
    got = [lax.ppermute(pay[k - 1], "z", quarter_route(k)) for k in (1, 2, 3)]
    dx, dbc, e = intra(values, bc, probe_ids, rows, cols, skip)
    grads = finish(meta, *got, values, bc, probe_ids, rows, cols, t_all, q_all, dx, dbc, e, prm)
    everyone = to_all(grads, X)
    oth_part, own_part = pull(meta, everyone, weights)
    swapped = lax.ppermute(oth_part, "core", SWAP)
    both = (own_part.astype(F32) + swapped.astype(F32)).astype(BF16)
    pieces = lax.all_to_all(both, "y", split_axis=0, concat_axis=0)
    away = jnp.sum(pieces.astype(F32), axis=0)
    squares = jnp.broadcast_to(jnp.sum(away * away), (8, 128))
    back = [(b, a) for a, b in features_route()]
    gradient = lax.ppermute(away.astype(BF16), AXES, back)
    squares = squares + lax.ppermute(squares, "core", SWAP)
    squares = sum_of_four(squares, X)
    squares = lax.ppermute(squares, AXES, back)[0, 0]

    direction = (2 * signs[0] - 1).astype(F32)[:, None]
    step = 0.5 * direction * gradient.astype(F32)
    picked = (direction.astype(BF16) * gradient)[local_pos]
    high = squares.astype(BF16)
    low = (squares - high.astype(F32)).astype(BF16)
    lane = jnp.arange(128)[None, :]
    tail = jnp.broadcast_to(jnp.where(lane < 64, high, low), (32, 128))
    returned = lax.all_to_all(jnp.concatenate([picked, tail], axis=1), SEQ, split_axis=0, concat_axis=0, tiled=True)
    sums = returned[::2, 1024:].astype(F32)
    entries = 2048 * 8192
    grad_scale = jnp.sqrt((jnp.sum(sums[:, 0]) + jnp.sum(sums[:, 64])) / entries + 1e-06)
    adv = (merged.astype(F32) + step / grad_scale).astype(BF16)
    adv_frames = (frame_emb.astype(F32) + 0.5 * returned[:, :1024].astype(F32) / grad_scale).astype(BF16)
    return (adv[None], adv_frames[None])


def solution(mesh):
    mesh = Mesh(mesh.devices.reshape(2, 2, 8, 4, 2), AXES)
    return jax.shard_map(
        body,
        mesh=mesh,
        in_specs=(
            P("x_hi", SEQ, TENSOR),
            P("x_hi", SEQ, None),
            P(None, TENSOR),
            P("x_hi", SEQ),
            P("x_hi", SEQ),
            P("x_hi", SEQ),
            P(("x_hi",) + SEQ, TENSOR),
            P(("x_hi",) + SEQ, TENSOR),
            P(("x_hi",) + SEQ, TENSOR),
            P(TENSOR),
            P(TENSOR),
            P(TENSOR),
            P("x_hi", SEQ, TENSOR),
        ),
        out_specs=(P("x_hi", SEQ, TENSOR), P("x_hi", SEQ, TENSOR)),
        check_vma=False,
    )
```

```python
import jax
import jax.numpy as jnp
from jax import lax
from jax.experimental import pallas as pl
from jax.experimental.pallas import tpu as pltpu
from jax.sharding import Mesh, PartitionSpec as P

F32, BF16 = jnp.float32, jnp.bfloat16
AXES = ("x_hi", "x_lo", "z", "y", "core")
X = ("x_hi", "x_lo")
SEQ = ("x_lo", "z")
TENSOR = ("y", "core")
CHUNK = 128
WIDE = 1408
HIGH = lax.Precision.HIGHEST
VMEM = pl.BlockSpec(memory_space=pltpu.VMEM)
SMEM = pl.BlockSpec(memory_space=pltpu.SMEM)


def linear(x, z, y, core):
    return ((x * 8 + z) * 4 + y) * 2 + core


def features_route():
    pairs = []
    for x in range(4):
        for z in range(8):
            for y in range(4):
                for core in range(2):
                    there = linear(y, 4 * (z // 4) + x, (z % 4 + x) % 4, core)
                    pairs.append((linear(x, z, y, core), there))
    return pairs


def probe_route():
    pairs = []
    for x in range(4):
        for z in range(8):
            pairs.append((x * 8 + z, (z % 4) * 8 + 4 * (z // 4) + x))
    return pairs


def quarter_route(k):
    pairs = []
    for z in range(8):
        sample, quarter = (z % 4) // 2, 2 * (z % 2) + z // 4
        to = (quarter + k) % 4
        pairs.append((z, 4 * (to % 2) + 2 * sample + to // 2))
    return pairs


def dot_nt(a, b):
    return lax.dot_general(a, b, (((1,), (1,)), ((), ())), preferred_element_type=F32)


def dot_tn(a, b):
    return lax.dot_general(a, b, (((0,), (0,)), ((), ())), preferred_element_type=F32)


def dot_nn(a, b):
    return jnp.dot(a, b, preferred_element_type=F32)


def iota(shape, dim):
    return lax.broadcasted_iota(jnp.int32, shape, dim)


def spread(columns):
    left = iota((CHUNK, 128), 1) < 64
    tiles = [
        jnp.where(left, jnp.broadcast_to(columns[2 * i], (CHUNK, 128)), jnp.broadcast_to(columns[2 * i + 1], (CHUNK, 128)))
        for i in range(2)
    ]
    return jnp.concatenate(tiles, axis=1)


def by_head_rows(values):
    rows = iota((256, 128), 0)
    out = jnp.broadcast_to(values[3], (256, 128))
    for h in (2, 1, 0):
        out = jnp.where(rows < 64 * (h + 1), jnp.broadcast_to(values[h], (256, 128)), out)
    return out


def lanes(row):
    return [row[:, h : h + 1] for h in range(4)]


def weights_of(rows, cols):
    seg = cols[:, 12:13]
    prev, last = rows[13:14, 127:128], rows[12:13, 127:128]
    end = cols[127:128, :]
    carry = jnp.where(seg == prev, jnp.exp(cols), 0.0)
    tail = jnp.where(seg == last, jnp.exp(end - cols), 0.0)
    through = jnp.where(last == prev, jnp.exp(end), 0.0)
    return carry, tail, through


def ring_source(meta, i):
    offset = (0, 7, 1, 6, 2, 5, 3, 4)[i]
    return lax.rem(meta[3] + offset, 8)


def start_copies(blocks, buf, sems):
    copies = []
    for i, ref in enumerate(blocks[:7]):
        copies.append([pltpu.make_async_copy(ref, buf.at[i], sems.at[i])])
    if len(blocks) == 9:
        halves = [pltpu.make_async_copy(blocks[7 + n], buf.at[7, pl.ds(128 * n, 128)], sems.at[7 + n]) for n in range(2)]
        copies.append(halves)
    for group in copies:
        for copy in group:
            copy.start()
    return copies


def feature_columns(meta, own, oth, place):
    half, cols = place // 4, pl.ds(pl.multiple_of(lax.rem(place, 4) * 256, 256), 256)
    mine = half == meta[0]
    parts = []
    for k in range(4):
        at = lax.rem(k + meta[1], 4)
        parts.append(jnp.where(mine, own[at, :, cols].astype(F32), oth[at, :, cols].astype(F32)).astype(BF16))
    return jnp.concatenate(parts, axis=0)


TILES = [(256 * t, min(256 * t + 256, WIDE)) for t in range(6)]


def project_most_kernel(meta, own, oth, *rest):
    blocks, acc, (buf, rows, sems) = rest[:7], rest[7], rest[8:]
    copies = start_copies(blocks, buf, sems)
    for i in range(7):
        rows[i] = feature_columns(meta, own, oth, ring_source(meta, i))
    for group in copies:
        group[0].wait()
    for lo, hi in TILES:
        total = dot_nn(rows[0], buf[0, :, lo:hi])
        for i in range(1, 7):
            total += dot_nn(rows[i], buf[i, :, lo:hi])
        acc[:, lo:hi] = total


def project_most(meta, own, oth, blocks):
    return pl.pallas_call(
        project_most_kernel,
        in_specs=[SMEM, VMEM, VMEM] + [pl.BlockSpec(memory_space=pl.ANY)] * 7,
        out_specs=VMEM,
        out_shape=jax.ShapeDtypeStruct((512, WIDE), F32),
        scratch_shapes=[
            pltpu.VMEM((7, 256, WIDE), BF16),
            pltpu.VMEM((7, 512, 256), BF16),
            pltpu.SemaphoreType.DMA((7,)),
        ],
    )(meta, own, oth, *blocks)


def project_last_kernel(meta, own, oth, acc, upper, lower, out):
    rows = feature_columns(meta, own, oth, ring_source(meta, 7))
    for t, (lo, hi) in enumerate(TILES):
        total = acc[:, lo:hi] + dot_nn(rows[:, 0:128], upper[:, lo:hi]) + dot_nn(rows[:, 128:256], lower[:, lo:hi])
        if t < 4:
            out[t, 0:512, 0:256] = total.astype(BF16)
        elif t == 4:
            for d in range(4):
                out[d, 0:512, 256:512] = total.astype(BF16)
        else:
            steps = total.T
            for d in range(4):
                mine = jnp.concatenate([steps[4 * d : 4 * d + 4], jnp.zeros((12, 512), F32)], axis=0)
                out[d, 512:528, :] = mine.astype(BF16)


def project_last(meta, own, oth, acc, upper, lower):
    return pl.pallas_call(
        project_last_kernel,
        in_specs=[SMEM] + [VMEM] * 5,
        out_specs=VMEM,
        out_shape=jax.ShapeDtypeStruct((4, 528, 512), BF16),
    )(meta, own, oth, acc, upper, lower)


def prepare_kernel(meta, r, p, prm, pay, x, bc, rows_out, cols_out, t_out, q_out):
    total = r[0, 0:512, :].astype(F32)
    raw = r[0, 512:528, :].astype(F32)
    for d in range(1, 4):
        total += r[d, 0:512, :].astype(F32)
        raw += r[d, 512:528, :].astype(F32)
    x[...] = total[:, 0:256]
    bc[...] = total[:, 256:512].astype(BF16)
    upper = (iota((128, 128), 0) <= iota((128, 128), 1)).astype(F32)
    top = iota((8, 128), 0) < 4
    bias, rate = prm[0], prm[1]
    through = []
    for k in range(4):
        here = slice(128 * k, 128 * k + 128)
        z = raw[0:8, here] + bias
        dt = jnp.maximum(z, 0.0) + jnp.log1p(jnp.exp(-jnp.abs(z)))
        logs = jnp.dot(-dt * rate, upper, precision=HIGH, preferred_element_type=F32)
        seg = p[k, 128:144, 0:128].astype(F32)[0:8]
        rows = jnp.concatenate([jnp.where(top, logs, pltpu.roll(dt, 4, 0)), jnp.where(top, z, pltpu.roll(seg, 4, 0))], axis=0)
        cols = jnp.concatenate([rows, jnp.zeros((112, 128), F32)], axis=0).T
        rows_out[k] = rows
        cols_out[k] = cols
        carry, tail, thru = weights_of(rows, cols)
        through.append(thru)
        carry_x = spread(lanes(carry))
        tail_x = spread([tail[:, h : h + 1] * cols[:, 4 + h : 5 + h] for h in range(4)])
        b, c = bc[here, 0:128], bc[here, 128:256]
        t_out[k] = dot_tn((x[here, :] * tail_x).astype(BF16), b)
        q_out[k] = dot_tn((p[k, 0:128, :].astype(F32) * carry_x).astype(BF16), c)
    state = t_out[0]
    grad = q_out[3]
    whole = through[0]
    for k in range(1, 4):
        state = by_head_rows(lanes(through[k])) * state + t_out[k]
        grad = by_head_rows(lanes(through[3 - k])) * grad + q_out[3 - k]
        whole = whole * through[k]
    for k in range(1, 4):
        pay[k - 1, 0:256, :] = jnp.where(meta[2] + k < 4, state, grad).astype(BF16)
        pay[k - 1, 256:272, :] = jnp.broadcast_to(whole, (16, 128)).astype(BF16)


def prepare(meta, r, p, prm):
    return pl.pallas_call(
        prepare_kernel,
        in_specs=[SMEM, VMEM, VMEM, VMEM],
        out_specs=[VMEM] * 7,
        out_shape=[
            jax.ShapeDtypeStruct((3, 272, 128), BF16),
            jax.ShapeDtypeStruct((512, 256), F32),
            jax.ShapeDtypeStruct((512, 256), BF16),
            jax.ShapeDtypeStruct((4, 16, 128), F32),
            jax.ShapeDtypeStruct((4, 128, 128), F32),
            jax.ShapeDtypeStruct((4, 256, 128), F32),
            jax.ShapeDtypeStruct((4, 256, 128), F32),
        ],
    )(meta, r, p, prm)


def intra_kernel(x, bc, p, rows_in, cols_in, skip, dx, dbc, e):
    seen = iota((128, 128), 0) >= iota((128, 128), 1)
    lane = iota((128, 128), 1)
    for k in range(4):
        here = slice(128 * k, 128 * k + 128)
        b, c = bc[here, 0:128], bc[here, 128:256]
        rows, cols = rows_in[k], cols_in[k]
        scores = dot_nt(c, b)
        visible = (cols[:, 12:13] == rows[12:13, :]) & seen
        d_scores = jnp.zeros((128, 128), F32)
        by_row = jnp.zeros((128, 128), F32)
        sums = []
        for tile in range(2):
            part = slice(128 * tile, 128 * tile + 128)
            probe = p[k, 0:128, part].astype(F32)
            values = x[here, part].astype(BF16)
            d_values = skip[:, part] * probe
            for a in range(2):
                h = 2 * tile + a
                mine = jnp.where((lane < 64) if a == 0 else (lane >= 64), probe, 0.0).astype(BF16)
                pulled = dot_nt(mine, values)
                decay = jnp.exp(jnp.where(visible, cols[:, h : h + 1] - rows[h : h + 1, :], -1e30))
                steps = rows[4 + h : 5 + h, :]
                weighted = decay * pulled
                decayed = decay * scores
                plain = weighted * scores
                sums.append(jnp.sum(plain, axis=0, keepdims=True))
                by_row = jnp.where(lane == h, jnp.sum(plain * steps, axis=1, keepdims=True), by_row)
                d_scores += weighted * steps
                d_values += dot_tn((decayed * steps).astype(BF16), mine)
            dx[here, part] = d_values
        d_scores = d_scores.astype(BF16)
        dbc[here, 0:128] = dot_tn(d_scores, c)
        dbc[here, 128:256] = dot_nn(d_scores, b)
        sub = iota((8, 128), 0)
        down = jnp.zeros((8, 128), F32)
        for h in range(4):
            down = jnp.where(sub == h, jnp.broadcast_to(sums[h], (8, 128)), down)
        dt = pltpu.roll(rows[0:8], 4, 0)
        e[k, 0:8, :] = down
        e[k, 8:16, :] = by_row.T[0:8] - dt * down


def intra(x, bc, p, rows, cols, skip):
    return pl.pallas_call(
        intra_kernel,
        in_specs=[VMEM] * 6,
        out_specs=[VMEM] * 3,
        out_shape=[
            jax.ShapeDtypeStruct((512, 256), F32),
            jax.ShapeDtypeStruct((512, 256), F32),
            jax.ShapeDtypeStruct((4, 16, 128), F32),
        ],
    )(x, bc, p, rows, cols, skip)


def finish_kernel(meta, r1, r2, r3, x, bc, p, rows_in, cols_in, t_in, q_in, dx, dbc, e, prm, out):
    quarter = meta[2]
    got = (r1, r2, r3)
    parts = [ref[0:256, :].astype(F32) for ref in got]
    decays = [by_head_rows(lanes(ref[256:272, :].astype(F32)[0:1])) for ref in got]

    def total(order):
        out_sum = jnp.zeros((256, 128), F32)
        run = jnp.ones((256, 128), F32)
        for index, valid in order:
            out_sum += jnp.where(valid, run * parts[index], 0.0)
            run = jnp.where(valid, run * decays[index], run)
        return out_sum

    entering = total([(k - 1, quarter - k >= 0) for k in (1, 2, 3)])
    leaving = total([(3 - m, quarter + m <= 3) for m in (1, 2, 3)])
    weights = [weights_of(rows_in[k], cols_in[k]) for k in range(4)]
    through = [by_head_rows(lanes(weights[k][2])) for k in range(4)]
    states, grads = [entering], [leaving]
    for k in range(3):
        states.append(through[k] * states[k] + t_in[k])
        grads.append(through[3 - k] * grads[k] + q_in[3 - k])
    grads = grads[::-1]
    indicator = (iota((8, 256), 1) // 64 == iota((8, 256), 0)).astype(F32)
    lower = (iota((128, 128), 0) >= iota((128, 128), 1)).astype(F32)
    sub, lane = iota((8, 128), 0), iota((8, 128), 1)
    rate = prm[1]

    def by_head(product):
        dims = (((1,), (1,)), ((), ()))
        return lax.dot_general(indicator, product, dims, precision=HIGH, preferred_element_type=F32)

    for k in range(4):
        here = slice(128 * k, 128 * k + 128)
        rows, cols = rows_in[k], cols_in[k]
        carry, tail, thru = weights[k]
        b, c = bc[here, 0:128], bc[here, 128:256]
        carry_x = spread(lanes(carry))
        tail_x = spread(lanes(tail))
        step_x = spread([cols[:, 4 + h : 5 + h] for h in range(4)])
        state, grad = states[k].astype(BF16), grads[k].astype(BF16)
        probe = p[k, 0:128, :].astype(F32) * carry_x
        values = x[here, :] * tail_x
        carried = probe * dot_nt(c, state)
        pulled = dot_nt(b, grad)
        out[here, 0:256] = (dx[here, :] + tail_x * step_x * pulled).astype(BF16)
        d_b = dbc[here, 0:128] + dot_nn((values * step_x).astype(BF16), grad)
        d_c = dbc[here, 128:256] + dot_nn(probe.astype(BF16), state)
        out[here, 256:384] = d_b.astype(BF16)
        out[here, 384:512] = d_c.astype(BF16)
        from_carry = by_head(carried)
        from_tail = by_head(values * pulled)
        dt = pltpu.roll(rows[0:8], 4, 0)
        d_log = e[k, 8:16, :] + from_carry - dt * from_tail
        both = jnp.sum(grads[k] * states[k], axis=1, keepdims=True)
        end = jnp.sum(jnp.where(sub < 4, dt * from_tail, 0.0), axis=1, keepdims=True)
        for h in range(4):
            own = jnp.sum(both[64 * h : 64 * h + 64], axis=0, keepdims=True) * thru[:, h : h + 1]
            end = jnp.where(sub[:, 0:1] == h, end + own, end)
        d_log = jnp.where(lane == 127, d_log + end, d_log)
        d_step = jnp.dot(d_log, lower, precision=HIGH, preferred_element_type=F32)
        d_dt = e[k, 0:8, :] + from_tail - rate * d_step
        z = rows[8:16]
        d_z = jnp.where(sub < 4, d_dt / (1.0 + jnp.exp(-z)), 0.0)
        out[512:528, here] = jnp.concatenate([d_z, jnp.zeros((8, 128), F32)], axis=0).astype(BF16)


def finish(meta, *args):
    return pl.pallas_call(
        finish_kernel,
        in_specs=[SMEM] + [VMEM] * len(args),
        out_specs=VMEM,
        out_shape=jax.ShapeDtypeStruct((528, 512), BF16),
    )(meta, *args)


def pull_kernel(meta, g, *rest):
    blocks, oth, own, (buf, full, sems) = rest[:9], rest[9], rest[10], rest[11:]
    copies = start_copies(blocks, buf, sems)
    shared = g[0, 0:512, 256:512].astype(F32)
    for d in range(4):
        full[256 * d : 256 * d + 256, :] = g[d, 0:512, 0:256].astype(F32).T.astype(BF16)
        if d:
            shared += g[d, 0:512, 256:512].astype(F32)
    full[1024:1280, :] = shared.T.astype(BF16)
    top = iota((8, 512), 0) < 4
    steps = [g[d, 512:528, :].astype(F32)[0:8] for d in range(4)]
    pairs = [jnp.where(top, steps[2 * j], pltpu.roll(steps[2 * j + 1], 4, 0)) for j in range(2)]
    full[1280:1408, :] = jnp.concatenate(pairs + [jnp.zeros((112, 512), F32)], axis=0).astype(BF16)
    for i in range(8):
        for copy in copies[i]:
            copy.wait()
        place = ring_source(meta, i)
        part = dot_nn(buf[i], full[...]).T.astype(BF16)
        cols = pl.ds(pl.multiple_of(lax.rem(place, 4) * 256, 256), 256)
        mine = place // 4 == meta[0]

        def put(ref):
            for k in range(4):
                ref[lax.rem(k + meta[1], 4), :, cols] = part[128 * k : 128 * k + 128]

        @pl.when(mine)
        def _():
            put(own)

        @pl.when(jnp.logical_not(mine))
        def _():
            put(oth)


def pull(meta, g, blocks):
    return pl.pallas_call(
        pull_kernel,
        in_specs=[SMEM, VMEM] + [pl.BlockSpec(memory_space=pl.ANY)] * 9,
        out_specs=[VMEM] * 2,
        out_shape=[jax.ShapeDtypeStruct((4, 128, 1024), BF16)] * 2,
        scratch_shapes=[
            pltpu.VMEM((8, 256, WIDE), BF16),
            pltpu.VMEM((WIDE, 512), BF16),
            pltpu.SemaphoreType.DMA((9,)),
        ],
    )(meta, g, *blocks)


def to_all(x, axis):
    return lax.all_to_all(jnp.broadcast_to(x[None], (4,) + x.shape), axis, split_axis=0, concat_axis=0)


def shifted(x, axis, k):
    return lax.ppermute(x, axis, [(i, (i + k) % 4) for i in range(4)])


def sum_of_four(x, axis):
    return x + shifted(x, axis, 1) + shifted(x, axis, 2) + shifted(x, axis, 3)


SWAP = [(0, 1), (1, 0)]


def body(tokens, frame_feats, w_proj, frame_pos, segments, signs, w_x, w_bc, w_dt, dt_bias, decay_rate, skip_gain, probe):
    x_at, z_at, core_at = lax.axis_index(X), lax.axis_index("z"), lax.axis_index("core")
    quarter = 2 * lax.rem(z_at, 2) + z_at // 4
    meta = jnp.stack([core_at, lax.rem(z_at, 4), quarter, z_at]).astype(jnp.int32)

    w_all = jnp.concatenate([w_x, w_bc, w_dt, jnp.zeros((256, 112), BF16)], axis=1)

    def right(v):
        return lax.ppermute(v, "z", [(i, (i + 1) % 8) for i in range(8)])

    def left(v):
        return lax.ppermute(v, "z", [(i, (i + 7) % 8) for i in range(8)])

    r1, l1 = right(w_all), left(w_all)
    frame_emb = jnp.dot(frame_feats[0], w_proj, preferred_element_type=F32).astype(BF16)
    slot = frame_pos[0] - CHUNK * (jnp.arange(32, dtype=jnp.int32) // 2)
    tagged = jnp.concatenate([frame_emb, jnp.broadcast_to(slot.astype(BF16)[:, None], (32, 128))], axis=1)
    arrived = lax.all_to_all(tagged, SEQ, split_axis=0, concat_axis=0, tiled=True)
    local_pos = arrived[:, 1024].astype(jnp.int32)
    merged = tokens[0].at[local_pos].set(arrived[:, :1024])
    segment = segments[0]
    before = lax.ppermute(segment[-1:], X + ("z",), [(i, i + 1) for i in range(31)])
    ids = jnp.concatenate([segment[None], jnp.broadcast_to(before[None], (15, CHUNK))]).astype(BF16)
    probe_ids = jnp.concatenate([probe[0], jnp.tile(ids, (1, 8))], axis=0)

    merged, r1, l1, probe_ids = lax.optimization_barrier((merged, r1, l1, probe_ids))
    r2, l2 = right(r1), left(l1)
    moved = lax.ppermute(merged, AXES, features_route())
    moved, r2, l2 = lax.optimization_barrier((moved, r2, l2))
    r3, l3 = right(r2), left(l2)
    own = to_all(moved, "y")
    own, r3, l3, probe_ids = lax.optimization_barrier((own, r3, l3, probe_ids))
    r4, l4 = right(r3[:128]), left(l3[128:])
    oth = lax.ppermute(own, "core", SWAP)
    probe_ids = lax.ppermute(probe_ids, X + ("z",), probe_route())
    probe_ids = probe_ids.reshape(144, 4, 256).transpose(1, 0, 2)
    probe_ids = lax.all_to_all(probe_ids, X, split_axis=0, concat_axis=0)

    def four(v):
        return lax.dynamic_slice(v, (4 * x_at,), (4,))

    prm = jnp.stack([four(dt_bias), four(decay_rate)])
    prm = jnp.concatenate([prm, jnp.zeros((2, 4), F32)], axis=1)
    prm = jnp.broadcast_to(prm[:, :, None], (2, 8, 128))
    skip = jnp.repeat(four(skip_gain), 64)[None, :]

    blocks = [w_all, r1, l1, r2, l2, r3, l3]
    acc = project_most(meta, own, oth, blocks)
    partial_proj = project_last(meta, own, oth, acc, r4, l4)
    received = lax.all_to_all(partial_proj, X, split_axis=0, concat_axis=0)
    pay, values, bc, rows, cols, t_all, q_all = prepare(meta, received, probe_ids, prm)
    got = [lax.ppermute(pay[k - 1], "z", quarter_route(k)) for k in (1, 2, 3)]
    dx, dbc, e = intra(values, bc, probe_ids, rows, cols, skip)
    grads = finish(meta, *got, values, bc, probe_ids, rows, cols, t_all, q_all, dx, dbc, e, prm)
    everyone = to_all(grads, X)
    oth_part, own_part = pull(meta, everyone, blocks + [r4, l4])
    swapped = lax.ppermute(oth_part, "core", SWAP)
    both = (own_part.astype(F32) + swapped.astype(F32)).astype(BF16)
    pieces = lax.all_to_all(both, "y", split_axis=0, concat_axis=0)
    away = jnp.sum(pieces.astype(F32), axis=0)
    squares = jnp.broadcast_to(jnp.sum(away * away), (8, 128))
    back = [(b, a) for a, b in features_route()]
    gradient = lax.ppermute(away.astype(BF16), AXES, back)
    squares = squares + lax.ppermute(squares, "core", SWAP)
    squares = sum_of_four(squares, X)
    squares = lax.ppermute(squares, AXES, back)[0, 0]

    direction = (2 * signs[0] - 1).astype(F32)[:, None]
    step = 0.5 * direction * gradient.astype(F32)
    picked = (direction.astype(BF16) * gradient)[local_pos]
    high = squares.astype(BF16)
    low = (squares - high.astype(F32)).astype(BF16)
    lane = jnp.arange(128)[None, :]
    tail = jnp.broadcast_to(jnp.where(lane < 64, high, low), (32, 128))
    returned = lax.all_to_all(jnp.concatenate([picked, tail], axis=1), SEQ, split_axis=0, concat_axis=0, tiled=True)
    sums = returned[::2, 1024:].astype(F32)
    entries = 2048 * 8192
    grad_scale = jnp.sqrt((jnp.sum(sums[:, 0]) + jnp.sum(sums[:, 64])) / entries + 1e-06)
    adv = (merged.astype(F32) + step / grad_scale).astype(BF16)
    adv_frames = (frame_emb.astype(F32) + 0.5 * returned[:, :1024].astype(F32) / grad_scale).astype(BF16)
    return (adv[None], adv_frames[None])


def solution(mesh):
    mesh = Mesh(mesh.devices.reshape(2, 2, 8, 4, 2), AXES)
    return jax.shard_map(
        body,
        mesh=mesh,
        in_specs=(
            P("x_hi", SEQ, TENSOR),
            P("x_hi", SEQ, None),
            P(None, TENSOR),
            P("x_hi", SEQ),
            P("x_hi", SEQ),
            P("x_hi", SEQ),
            P(("x_hi",) + SEQ, TENSOR),
            P(("x_hi",) + SEQ, TENSOR),
            P(("x_hi",) + SEQ, TENSOR),
            P(TENSOR),
            P(TENSOR),
            P(TENSOR),
            P("x_hi", SEQ, TENSOR),
        ),
        out_specs=(P("x_hi", SEQ, TENSOR), P("x_hi", SEQ, TENSOR)),
        check_vma=False,
    )
```

```python
import jax
import jax.numpy as jnp
from jax import lax
from jax.experimental import pallas as pl
from jax.experimental.pallas import tpu as pltpu
from jax.sharding import Mesh, PartitionSpec as P


F32, BF16 = jnp.float32, jnp.bfloat16
AXES = ("x_hi", "x_lo", "z", "y", "core")
X = ("x_hi", "x_lo")
SEQ = ("x_lo", "z")
TENSOR = ("y", "core")
CHUNK = 128
WIDE = 1408
PLACE = (0, 2, 1, 3)
HIGH = lax.Precision.HIGHEST
VMEM = pl.BlockSpec(memory_space=pltpu.VMEM)
SMEM = pl.BlockSpec(memory_space=pltpu.SMEM)


def linear(x, z, y, core):
    return ((x * 8 + z) * 4 + y) * 2 + core


def features_route():
    pairs = []
    for x in range(4):
        for z in range(8):
            for y in range(4):
                for core in range(2):
                    there = linear(y, 4 * (z // 4) + PLACE[x], (z % 4 + x) % 4, core)
                    pairs.append((linear(x, z, y, core), there))
    return pairs


def probe_route():
    pairs = []
    for x in range(4):
        for z in range(8):
            pairs.append((x * 8 + z, (z % 4 + x) % 4 * 8 + 4 * (z // 4) + PLACE[x]))
    return pairs


def quarter_route(k):
    pairs = []
    for z in range(8):
        home = PLACE[z % 4]
        to = (2 * (home % 2) + z // 4 + k) % 4
        pairs.append((z, 4 * (to % 2) + PLACE[home // 2 * 2 + to // 2]))
    return pairs


def dot_nt(a, b):
    return lax.dot_general(a, b, (((1,), (1,)), ((), ())), preferred_element_type=F32)


def dot_tn(a, b):
    return lax.dot_general(a, b, (((0,), (0,)), ((), ())), preferred_element_type=F32)


def dot_nn(a, b):
    return jnp.dot(a, b, preferred_element_type=F32)


def iota(shape, dim):
    return lax.broadcasted_iota(jnp.int32, shape, dim)


def spread(columns):
    left = iota((CHUNK, 128), 1) < 64
    tiles = [
        jnp.where(left, jnp.broadcast_to(columns[2 * i], (CHUNK, 128)), jnp.broadcast_to(columns[2 * i + 1], (CHUNK, 128)))
        for i in range(2)
    ]
    return jnp.concatenate(tiles, axis=1)


def by_head_rows(values):
    rows = iota((256, 128), 0)
    out = jnp.broadcast_to(values[3], (256, 128))
    for h in (2, 1, 0):
        out = jnp.where(rows < 64 * (h + 1), jnp.broadcast_to(values[h], (256, 128)), out)
    return out


def lanes(row):
    return [row[:, h : h + 1] for h in range(4)]


def weights_of(rows, cols):
    seg = cols[:, 12:13]
    prev, last = rows[13:14, 127:128], rows[12:13, 127:128]
    end = cols[127:128, :]
    carry = jnp.where(seg == prev, jnp.exp(cols), 0.0)
    tail = jnp.where(seg == last, jnp.exp(end - cols), 0.0)
    through = jnp.where(last == prev, jnp.exp(end), 0.0)
    return carry, tail, through


def pack_kernel(w_x, w_bc, w_dt, out):
    out[:, 0:1024] = w_x[...]
    out[:, 1024:1280] = w_bc[...]
    out[:, 1280:1408] = jnp.zeros((256, 128), BF16)
    out[:, 1280:1296] = w_dt[...]


def pack(*parts):
    return pl.pallas_call(
        pack_kernel, in_specs=[VMEM] * 3, out_specs=VMEM, out_shape=jax.ShapeDtypeStruct((256, WIDE), BF16)
    )(*parts)


def ring_source(meta, i):
    offset = (0, 7, 1, 6, 2, 5, 3, 4)[i]
    return lax.rem(meta[3] + offset, 8)


def start_copies(blocks, buf, sems):
    copies = []
    for i, ref in enumerate(blocks[:7]):
        copies.append([pltpu.make_async_copy(ref, buf.at[i], sems.at[i])])
    if len(blocks) == 9:
        halves = [pltpu.make_async_copy(blocks[7 + n], buf.at[7, pl.ds(128 * n, 128)], sems.at[7 + n]) for n in range(2)]
        copies.append(halves)
    for group in copies:
        for copy in group:
            copy.start()
    return copies


def feature_columns(meta, own, oth, place):
    half, cols = place // 4, pl.ds(pl.multiple_of(lax.rem(place, 4) * 256, 256), 256)
    mine = half == meta[0]
    parts = []
    for k in range(4):
        at = lax.rem(k + meta[1], 4)
        parts.append(jnp.where(mine, own[at, :, cols].astype(F32), oth[at, :, cols].astype(F32)).astype(BF16))
    return jnp.concatenate(parts, axis=0)


TILES = [(256 * t, min(256 * t + 256, WIDE)) for t in range(6)]


def project_most_kernel(meta, own, oth, *rest):
    blocks, (acc, last), (buf, rows, sems) = rest[:7], rest[7:9], rest[9:]
    copies = start_copies(blocks, buf, sems)
    for i in range(7):
        rows[i] = feature_columns(meta, own, oth, ring_source(meta, i))
    last[...] = feature_columns(meta, own, oth, ring_source(meta, 7))
    for group in copies:
        group[0].wait()
    for lo, hi in TILES:
        total = dot_nn(rows[0], buf[0, :, lo:hi])
        for i in range(1, 7):
            total += dot_nn(rows[i], buf[i, :, lo:hi])
        acc[:, lo:hi] = total


def project_most(meta, own, oth, blocks):
    return pl.pallas_call(
        project_most_kernel,
        in_specs=[SMEM, VMEM, VMEM] + [pl.BlockSpec(memory_space=pl.ANY)] * 7,
        out_specs=[VMEM] * 2,
        out_shape=[jax.ShapeDtypeStruct((512, WIDE), F32), jax.ShapeDtypeStruct((512, 256), BF16)],
        scratch_shapes=[
            pltpu.VMEM((7, 256, WIDE), BF16),
            pltpu.VMEM((7, 512, 256), BF16),
            pltpu.SemaphoreType.DMA((7,)),
        ],
    )(meta, own, oth, *blocks)


def project_last_kernel(rows, acc, upper, lower, probe, out):
    ids = probe[128:144, 0:512].astype(F32)[0:8]
    for d in range(4):
        part = slice(256 * d, 256 * d + 256)
        out[d, 528:592, 0:256] = probe[0:64, part]
        out[d, 528:592, 256:512] = probe[64:128, part]
    for t, (lo, hi) in enumerate(TILES):
        total = acc[:, lo:hi] + dot_nn(rows[:, 0:128], upper[:, lo:hi]) + dot_nn(rows[:, 128:256], lower[:, lo:hi])
        if t < 4:
            out[t, 0:512, 0:256] = total.astype(BF16)
        elif t == 4:
            for d in range(4):
                out[d, 0:512, 256:512] = total.astype(BF16)
        else:
            steps = total.T
            for d in range(4):
                mine = jnp.concatenate([steps[4 * d : 4 * d + 4], jnp.zeros((4, 512), F32), ids], axis=0)
                out[d, 512:528, :] = mine.astype(BF16)


def project_last(*args):
    return pl.pallas_call(
        project_last_kernel,
        in_specs=[VMEM] * 5,
        out_specs=VMEM,
        out_shape=jax.ShapeDtypeStruct((4, 592, 512), BF16),
    )(*args)


def prepare_kernel(meta, r, prm, pay, x, bc, rows_out, cols_out, t_out, q_out, p):
    total = r[0, 0:512, :].astype(F32)
    raw = r[0, 512:528, :].astype(F32)
    for d in range(1, 4):
        total += r[d, 0:512, :].astype(F32)
        raw += r[d, 512:528, :].astype(F32)
    x[...] = total[:, 0:256]
    bc[...] = total[:, 256:512].astype(BF16)
    upper = (iota((128, 128), 0) <= iota((128, 128), 1)).astype(F32)
    top = iota((8, 128), 0) < 4
    bias, rate = prm[0], prm[1]
    through = []
    for k in range(4):
        here = slice(128 * k, 128 * k + 128)
        z = raw[0:8, here] + bias
        dt = jnp.maximum(z, 0.0) + jnp.log1p(jnp.exp(-jnp.abs(z)))
        logs = jnp.dot(-dt * rate, upper, precision=HIGH, preferred_element_type=F32)
        source = lax.rem(k + meta[1], 4)
        p[k, 0:64, :] = r[source, 528:592, 0:256]
        p[k, 64:128, :] = r[source, 528:592, 256:512]
        seg = r[source, 512:528, 0:128].astype(F32)[8:16]
        rows = jnp.concatenate([jnp.where(top, logs, pltpu.roll(dt, 4, 0)), jnp.where(top, z, pltpu.roll(seg, 4, 0))], axis=0)
        cols = jnp.concatenate([rows, jnp.zeros((112, 128), F32)], axis=0).T
        rows_out[k] = rows
        cols_out[k] = cols
        carry, tail, thru = weights_of(rows, cols)
        through.append(thru)
        carry_x = spread(lanes(carry))
        tail_x = spread([tail[:, h : h + 1] * cols[:, 4 + h : 5 + h] for h in range(4)])
        b, c = bc[here, 0:128], bc[here, 128:256]
        t_out[k] = dot_tn((x[here, :] * tail_x).astype(BF16), b)
        q_out[k] = dot_tn((p[k, 0:128, :].astype(F32) * carry_x).astype(BF16), c)
    state = t_out[0]
    grad = q_out[3]
    whole = through[0]
    for k in range(1, 4):
        state = by_head_rows(lanes(through[k])) * state + t_out[k]
        grad = by_head_rows(lanes(through[3 - k])) * grad + q_out[3 - k]
        whole = whole * through[k]
    for k in range(1, 4):
        pay[k - 1, 0:256, :] = jnp.where(meta[2] + k < 4, state, grad).astype(BF16)
        pay[k - 1, 256:272, :] = jnp.broadcast_to(whole, (16, 128)).astype(BF16)


def prepare(meta, r, prm):
    return pl.pallas_call(
        prepare_kernel,
        in_specs=[SMEM, VMEM, VMEM],
        out_specs=[VMEM] * 8,
        out_shape=[
            jax.ShapeDtypeStruct((3, 272, 128), BF16),
            jax.ShapeDtypeStruct((512, 256), F32),
            jax.ShapeDtypeStruct((512, 256), BF16),
            jax.ShapeDtypeStruct((4, 16, 128), F32),
            jax.ShapeDtypeStruct((4, 128, 128), F32),
            jax.ShapeDtypeStruct((4, 256, 128), F32),
            jax.ShapeDtypeStruct((4, 256, 128), F32),
            jax.ShapeDtypeStruct((4, 128, 256), BF16),
        ],
    )(meta, r, prm)


def intra_kernel(x, bc, p, rows_in, cols_in, skip, dx, dbc, e):
    seen = iota((128, 128), 0) >= iota((128, 128), 1)
    lane = iota((128, 128), 1)
    for k in range(4):
        here = slice(128 * k, 128 * k + 128)
        b, c = bc[here, 0:128], bc[here, 128:256]
        rows, cols = rows_in[k], cols_in[k]
        scores = dot_nt(c, b)
        visible = (cols[:, 12:13] == rows[12:13, :]) & seen
        d_scores = jnp.zeros((128, 128), F32)
        by_row = jnp.zeros((128, 128), F32)
        sums = []
        for tile in range(2):
            part = slice(128 * tile, 128 * tile + 128)
            probe = p[k, 0:128, part].astype(F32)
            values = x[here, part].astype(BF16)
            d_values = skip[:, part] * probe
            for a in range(2):
                h = 2 * tile + a
                mine = jnp.where((lane < 64) if a == 0 else (lane >= 64), probe, 0.0).astype(BF16)
                pulled = dot_nt(mine, values)
                decay = jnp.exp(jnp.where(visible, cols[:, h : h + 1] - rows[h : h + 1, :], -1e30))
                steps = rows[4 + h : 5 + h, :]
                weighted = decay * pulled
                decayed = decay * scores
                plain = weighted * scores
                sums.append(jnp.sum(plain, axis=0, keepdims=True))
                by_row = jnp.where(lane == h, jnp.sum(plain * steps, axis=1, keepdims=True), by_row)
                d_scores += weighted * steps
                d_values += dot_tn((decayed * steps).astype(BF16), mine)
            dx[here, part] = d_values
        d_scores = d_scores.astype(BF16)
        dbc[here, 0:128] = dot_tn(d_scores, c)
        dbc[here, 128:256] = dot_nn(d_scores, b)
        sub = iota((8, 128), 0)
        down = jnp.zeros((8, 128), F32)
        for h in range(4):
            down = jnp.where(sub == h, jnp.broadcast_to(sums[h], (8, 128)), down)
        dt = pltpu.roll(rows[0:8], 4, 0)
        e[k, 0:8, :] = down
        e[k, 8:16, :] = by_row.T[0:8] - dt * down


def intra(x, bc, p, rows, cols, skip):
    return pl.pallas_call(
        intra_kernel,
        in_specs=[VMEM] * 6,
        out_specs=[VMEM] * 3,
        out_shape=[
            jax.ShapeDtypeStruct((512, 256), F32),
            jax.ShapeDtypeStruct((512, 256), F32),
            jax.ShapeDtypeStruct((4, 16, 128), F32),
        ],
    )(x, bc, p, rows, cols, skip)


def finish_kernel(meta, r1, r2, r3, x, bc, p, rows_in, cols_in, t_in, q_in, dx, dbc, e, prm, out):
    quarter = meta[2]
    got = (r1, r2, r3)
    parts = [ref[0:256, :].astype(F32) for ref in got]
    decays = [by_head_rows(lanes(ref[256:272, :].astype(F32)[0:1])) for ref in got]

    def total(order):
        out_sum = jnp.zeros((256, 128), F32)
        run = jnp.ones((256, 128), F32)
        for index, valid in order:
            out_sum += jnp.where(valid, run * parts[index], 0.0)
            run = jnp.where(valid, run * decays[index], run)
        return out_sum

    entering = total([(k - 1, quarter - k >= 0) for k in (1, 2, 3)])
    leaving = total([(3 - m, quarter + m <= 3) for m in (1, 2, 3)])
    weights = [weights_of(rows_in[k], cols_in[k]) for k in range(4)]
    through = [by_head_rows(lanes(weights[k][2])) for k in range(4)]
    states, grads = [entering], [leaving]
    for k in range(3):
        states.append(through[k] * states[k] + t_in[k])
        grads.append(through[3 - k] * grads[k] + q_in[3 - k])
    grads = grads[::-1]
    indicator = (iota((8, 256), 1) // 64 == iota((8, 256), 0)).astype(F32)
    lower = (iota((128, 128), 0) >= iota((128, 128), 1)).astype(F32)
    sub, lane = iota((8, 128), 0), iota((8, 128), 1)
    rate = prm[1]

    def by_head(product):
        dims = (((1,), (1,)), ((), ()))
        return lax.dot_general(indicator, product, dims, precision=HIGH, preferred_element_type=F32)

    for k in range(4):
        here = slice(128 * k, 128 * k + 128)
        rows, cols = rows_in[k], cols_in[k]
        carry, tail, thru = weights[k]
        b, c = bc[here, 0:128], bc[here, 128:256]
        carry_x = spread(lanes(carry))
        tail_x = spread(lanes(tail))
        step_x = spread([cols[:, 4 + h : 5 + h] for h in range(4)])
        state, grad = states[k].astype(BF16), grads[k].astype(BF16)
        probe = p[k, 0:128, :].astype(F32) * carry_x
        values = x[here, :] * tail_x
        carried = probe * dot_nt(c, state)
        pulled = dot_nt(b, grad)
        out[here, 0:256] = (dx[here, :] + tail_x * step_x * pulled).astype(BF16)
        d_b = dbc[here, 0:128] + dot_nn((values * step_x).astype(BF16), grad)
        d_c = dbc[here, 128:256] + dot_nn(probe.astype(BF16), state)
        out[here, 256:384] = d_b.astype(BF16)
        out[here, 384:512] = d_c.astype(BF16)
        from_carry = by_head(carried)
        from_tail = by_head(values * pulled)
        dt = pltpu.roll(rows[0:8], 4, 0)
        d_log = e[k, 8:16, :] + from_carry - dt * from_tail
        both = jnp.sum(grads[k] * states[k], axis=1, keepdims=True)
        end = jnp.sum(jnp.where(sub < 4, dt * from_tail, 0.0), axis=1, keepdims=True)
        for h in range(4):
            own = jnp.sum(both[64 * h : 64 * h + 64], axis=0, keepdims=True) * thru[:, h : h + 1]
            end = jnp.where(sub[:, 0:1] == h, end + own, end)
        d_log = jnp.where(lane == 127, d_log + end, d_log)
        d_step = jnp.dot(d_log, lower, precision=HIGH, preferred_element_type=F32)
        d_dt = e[k, 0:8, :] + from_tail - rate * d_step
        z = rows[8:16]
        d_z = jnp.where(sub < 4, d_dt / (1.0 + jnp.exp(-z)), 0.0)
        out[512:528, here] = jnp.concatenate([d_z, jnp.zeros((8, 128), F32)], axis=0).astype(BF16)


def finish(meta, *args):
    return pl.pallas_call(
        finish_kernel,
        in_specs=[SMEM] + [VMEM] * len(args),
        out_specs=VMEM,
        out_shape=jax.ShapeDtypeStruct((528, 512), BF16),
    )(meta, *args)


def pull_kernel(meta, g, *rest):
    blocks, oth, own, (buf, full, sems) = rest[:9], rest[9], rest[10], rest[11:]
    copies = start_copies(blocks, buf, sems)
    shared = g[0, 0:512, 256:512].astype(F32)
    for d in range(4):
        full[256 * d : 256 * d + 256, :] = g[d, 0:512, 0:256].astype(F32).T.astype(BF16)
        if d:
            shared += g[d, 0:512, 256:512].astype(F32)
    full[1024:1280, :] = shared.T.astype(BF16)
    top = iota((8, 512), 0) < 4
    steps = [g[d, 512:528, :].astype(F32)[0:8] for d in range(4)]
    pairs = [jnp.where(top, steps[2 * j], pltpu.roll(steps[2 * j + 1], 4, 0)) for j in range(2)]
    full[1280:1408, :] = jnp.concatenate(pairs + [jnp.zeros((112, 512), F32)], axis=0).astype(BF16)
    for i in range(8):
        for copy in copies[i]:
            copy.wait()
        place = ring_source(meta, i)
        part = dot_nn(buf[i], full[...]).T.astype(BF16)
        cols = pl.ds(pl.multiple_of(lax.rem(place, 4) * 256, 256), 256)
        mine = place // 4 == meta[0]

        def put(ref):
            for k in range(4):
                ref[lax.rem(k + meta[1], 4), :, cols] = part[128 * k : 128 * k + 128]

        @pl.when(mine)
        def _():
            put(own)

        @pl.when(jnp.logical_not(mine))
        def _():
            put(oth)


def pull(meta, g, blocks):
    return pl.pallas_call(
        pull_kernel,
        in_specs=[SMEM, VMEM] + [pl.BlockSpec(memory_space=pl.ANY)] * 9,
        out_specs=[VMEM] * 2,
        out_shape=[jax.ShapeDtypeStruct((4, 128, 1024), BF16)] * 2,
        scratch_shapes=[
            pltpu.VMEM((8, 256, WIDE), BF16),
            pltpu.VMEM((WIDE, 512), BF16),
            pltpu.SemaphoreType.DMA((9,)),
        ],
    )(meta, g, *blocks)


def to_all(x, axis):
    return lax.all_to_all(jnp.broadcast_to(x[None], (4,) + x.shape), axis, split_axis=0, concat_axis=0)


def shifted(x, axis, k):
    return lax.ppermute(x, axis, [(i, (i + k) % 4) for i in range(4)])


def sum_of_four(x, axis):
    return x + shifted(x, axis, 1) + shifted(x, axis, 2) + shifted(x, axis, 3)


SWAP = [(0, 1), (1, 0)]


def body(tokens, frame_feats, w_proj, frame_pos, segments, signs, w_x, w_bc, w_dt, dt_bias, decay_rate, skip_gain, probe):
    x_at, z_at, core_at = lax.axis_index(X), lax.axis_index("z"), lax.axis_index("core")
    across = lax.rem(z_at, 4)
    origin = 2 * lax.rem(across, 2) + across // 2
    quarter = 2 * lax.rem(origin, 2) + z_at // 4
    meta = jnp.stack([core_at, origin, quarter, z_at]).astype(jnp.int32)
    w_all = pack(w_x, w_bc, w_dt)

    def right(v):
        return lax.ppermute(v, "z", [(i, (i + 1) % 8) for i in range(8)])

    def left(v):
        return lax.ppermute(v, "z", [(i, (i + 7) % 8) for i in range(8)])

    frame_emb = jnp.dot(frame_feats[0], w_proj, preferred_element_type=F32).astype(BF16)
    slot = frame_pos[0] - CHUNK * (jnp.arange(32, dtype=jnp.int32) // 2)
    tagged = jnp.concatenate([frame_emb, jnp.broadcast_to(slot.astype(BF16)[:, None], (32, 128))], axis=1)
    arrived = lax.all_to_all(tagged, SEQ, split_axis=0, concat_axis=0, tiled=True)
    r1, l1 = right(w_all), left(w_all)
    local_pos = arrived[:, 1024].astype(jnp.int32)
    merged = tokens[0].at[local_pos].set(arrived[:, :1024])
    segment = segments[0]
    before = lax.ppermute(segment[-1:], X + ("z",), [(i, i + 1) for i in range(31)])

    merged, r1, l1 = lax.optimization_barrier((merged, r1, l1))
    moved = lax.ppermute(merged, AXES, features_route())
    r2, l2 = right(r1), left(l1)
    ids = jnp.concatenate([segment[None], jnp.broadcast_to(before[None], (15, CHUNK))]).astype(BF16)
    probe_ids = jnp.concatenate([probe[0], jnp.tile(ids, (1, 8))], axis=0)
    moved, r2, l2, probe_ids = lax.optimization_barrier((moved, r2, l2, probe_ids))
    r3, l3 = right(r2), left(l2)
    own = to_all(moved, "y")
    own, r3, l3, probe_ids = lax.optimization_barrier((own, r3, l3, probe_ids))
    r4, l4 = right(r3[:128]), left(l3[128:])
    probe_ids = lax.ppermute(probe_ids, X + ("z",), probe_route())
    oth = lax.ppermute(own, "core", SWAP)

    def four(v):
        return lax.dynamic_slice(v, (4 * x_at,), (4,))

    prm = jnp.stack([four(dt_bias), four(decay_rate)])
    prm = jnp.concatenate([prm, jnp.zeros((2, 4), F32)], axis=1)
    prm = jnp.broadcast_to(prm[:, :, None], (2, 8, 128))
    skip = jnp.repeat(four(skip_gain), 64)[None, :]

    blocks = [w_all, r1, l1, r2, l2, r3, l3]
    acc, last = project_most(meta, own, oth, blocks)
    partial_proj = project_last(last, acc, r4, l4, probe_ids)
    received = lax.all_to_all(partial_proj, X, split_axis=0, concat_axis=0)
    pay, values, bc, rows, cols, t_all, q_all, probes = prepare(meta, received, prm)
    got = [lax.ppermute(pay[k - 1], "z", quarter_route(k)) for k in (1, 2, 3)]
    dx, dbc, e = intra(values, bc, probes, rows, cols, skip)
    grads = finish(meta, *got, values, bc, probes, rows, cols, t_all, q_all, dx, dbc, e, prm)
    everyone = to_all(grads, X)
    oth_part, own_part = pull(meta, everyone, blocks + [r4, l4])
    swapped = lax.ppermute(oth_part, "core", SWAP)
    both = (own_part.astype(F32) + swapped.astype(F32)).astype(BF16)
    pieces = lax.all_to_all(both, "y", split_axis=0, concat_axis=0)
    away = jnp.sum(pieces.astype(F32), axis=0)
    squares = jnp.broadcast_to(jnp.sum(away * away), (8, 128))
    back = [(b, a) for a, b in features_route()]
    gradient = lax.ppermute(away.astype(BF16), AXES, back)
    squares = squares + lax.ppermute(squares, "core", SWAP)
    squares = sum_of_four(squares, X)
    squares = lax.ppermute(squares, AXES, back)[0, 0]

    direction = (2 * signs[0] - 1).astype(F32)[:, None]
    step = 0.5 * direction * gradient.astype(F32)
    picked = (direction.astype(BF16) * gradient)[local_pos]
    high = squares.astype(BF16)
    low = (squares - high.astype(F32)).astype(BF16)
    lane = jnp.arange(128)[None, :]
    tail = jnp.broadcast_to(jnp.where(lane < 64, high, low), (32, 128))
    returned = lax.all_to_all(jnp.concatenate([picked, tail], axis=1), SEQ, split_axis=0, concat_axis=0, tiled=True)
    sums = returned[::2, 1024:].astype(F32)
    entries = 2048 * 8192
    grad_scale = jnp.sqrt((jnp.sum(sums[:, 0]) + jnp.sum(sums[:, 64])) / entries + 1e-06)
    adv = (merged.astype(F32) + step / grad_scale).astype(BF16)
    adv_frames = (frame_emb.astype(F32) + 0.5 * returned[:, :1024].astype(F32) / grad_scale).astype(BF16)
    return (adv[None], adv_frames[None])


def solution(mesh):
    mesh = Mesh(mesh.devices.reshape(2, 2, 8, 4, 2), AXES)

    return jax.shard_map(
        body,
        mesh=mesh,
        in_specs=(
            P("x_hi", SEQ, TENSOR),
            P("x_hi", SEQ, None),
            P(None, TENSOR),
            P("x_hi", SEQ),
            P("x_hi", SEQ),
            P("x_hi", SEQ),
            P(("x_hi",) + SEQ, TENSOR),
            P(("x_hi",) + SEQ, TENSOR),
            P(("x_hi",) + SEQ, TENSOR),
            P(TENSOR),
            P(TENSOR),
            P(TENSOR),
            P("x_hi", SEQ, TENSOR),
        ),
        out_specs=(P("x_hi", SEQ, TENSOR), P("x_hi", SEQ, TENSOR)),
        check_vma=False,
    )
```

```python
import jax
import jax.numpy as jnp
from jax import lax
from jax.experimental import pallas as pl
from jax.experimental.pallas import tpu as pltpu
from jax.sharding import Mesh, PartitionSpec as P


F32, BF16 = jnp.float32, jnp.bfloat16
AXES = ("x_hi", "x_lo", "z", "y", "core")
X = ("x_hi", "x_lo")
SEQ = ("x_lo", "z")
TENSOR = ("y", "core")
CHUNK = 128
WIDE = 1408
PLACE = (0, 2, 1, 3)
HIGH = lax.Precision.HIGHEST
VMEM = pl.BlockSpec(memory_space=pltpu.VMEM)
SMEM = pl.BlockSpec(memory_space=pltpu.SMEM)


def linear(x, z, y, core):
    return ((x * 8 + z) * 4 + y) * 2 + core


def features_route():
    pairs = []
    for x in range(4):
        for z in range(8):
            for y in range(4):
                for core in range(2):
                    there = linear(y, 4 * (z // 4) + PLACE[x], (z % 4 + x) % 4, core)
                    pairs.append((linear(x, z, y, core), there))
    return pairs


def probe_route():
    pairs = []
    for x in range(4):
        for z in range(8):
            pairs.append((x * 8 + z, (z % 4 + x) % 4 * 8 + 4 * (z // 4) + PLACE[x]))
    return pairs


def quarter_route(k):
    pairs = []
    for z in range(8):
        home = PLACE[z % 4]
        to = (2 * (home % 2) + z // 4 + k) % 4
        pairs.append((z, 4 * (to % 2) + PLACE[home // 2 * 2 + to // 2]))
    return pairs


def dot_nt(a, b):
    return lax.dot_general(a, b, (((1,), (1,)), ((), ())), preferred_element_type=F32)


def dot_tn(a, b):
    return lax.dot_general(a, b, (((0,), (0,)), ((), ())), preferred_element_type=F32)


def dot_nn(a, b):
    return jnp.dot(a, b, preferred_element_type=F32)


def iota(shape, dim):
    return lax.broadcasted_iota(jnp.int32, shape, dim)


def spread(columns):
    left = iota((CHUNK, 128), 1) < 64
    tiles = [
        jnp.where(left, jnp.broadcast_to(columns[2 * i], (CHUNK, 128)), jnp.broadcast_to(columns[2 * i + 1], (CHUNK, 128)))
        for i in range(2)
    ]
    return jnp.concatenate(tiles, axis=1)


def by_head_rows(values):
    rows = iota((256, 128), 0)
    out = jnp.broadcast_to(values[3], (256, 128))
    for h in (2, 1, 0):
        out = jnp.where(rows < 64 * (h + 1), jnp.broadcast_to(values[h], (256, 128)), out)
    return out


def lanes(row):
    return [row[:, h : h + 1] for h in range(4)]


def weights_of(rows, cols):
    seg = cols[:, 12:13]
    prev, last = rows[13:14, 127:128], rows[12:13, 127:128]
    end = cols[127:128, :]
    carry = jnp.where(seg == prev, jnp.exp(cols), 0.0)
    tail = jnp.where(seg == last, jnp.exp(end - cols), 0.0)
    through = jnp.where(last == prev, jnp.exp(end), 0.0)
    return carry, tail, through


def pack_kernel(w_x, w_bc, w_dt, out):
    out[:, 0:1024] = w_x[...]
    out[:, 1024:1280] = w_bc[...]
    out[:, 1280:1408] = jnp.zeros((256, 128), BF16)
    out[:, 1280:1296] = w_dt[...]


def pack(*parts):
    return pl.pallas_call(
        pack_kernel, in_specs=[VMEM] * 3, out_specs=VMEM, out_shape=jax.ShapeDtypeStruct((256, WIDE), BF16)
    )(*parts)


TILES = [(256 * t, min(256 * t + 256, WIDE)) for t in range(6)]
ANY = pl.BlockSpec(memory_space=pl.ANY)


def project_kernel(meta, own, oth, w, probe, out, buf, rows, sems):
    copies = []
    for t, (lo, hi) in enumerate(TILES):
        for n in range(2):
            here = pl.ds(pl.multiple_of(lax.rem(meta[0] + n, 2) * 1024, 1024), 1024)
            there = buf.at[1024 * n : 1024 * n + 1024, lo:hi]
            copies.append(pltpu.make_async_copy(w.at[here, lo:hi], there, sems.at[2 * t + n]))
    for copy in copies:
        copy.start()
    for n, ref in enumerate((own, oth)):
        for k in range(4):
            rows[128 * k : 128 * k + 128, 1024 * n : 1024 * n + 1024] = ref[lax.rem(k + meta[1], 4)]
    ids = probe[128:144, 0:512].astype(F32)[0:8]
    for d in range(4):
        part = slice(256 * d, 256 * d + 256)
        out[d, 528:592, 0:256] = probe[0:64, part]
        out[d, 528:592, 256:512] = probe[64:128, part]
    for t, (lo, hi) in enumerate(TILES):
        copies[2 * t].wait()
        copies[2 * t + 1].wait()
        total = dot_nn(rows[...], buf[:, lo:hi])
        if t < 4:
            out[t, 0:512, 0:256] = total.astype(BF16)
        elif t == 4:
            for d in range(4):
                out[d, 0:512, 256:512] = total.astype(BF16)
        else:
            steps = total.T
            for d in range(4):
                mine = jnp.concatenate([steps[4 * d : 4 * d + 4], jnp.zeros((4, 512), F32), ids], axis=0)
                out[d, 512:528, :] = mine.astype(BF16)


def project(meta, own, oth, w, probe):
    return pl.pallas_call(
        project_kernel,
        in_specs=[SMEM, VMEM, VMEM, ANY, VMEM],
        out_specs=VMEM,
        out_shape=jax.ShapeDtypeStruct((4, 592, 512), BF16),
        scratch_shapes=[
            pltpu.VMEM((2048, WIDE), BF16),
            pltpu.VMEM((512, 2048), BF16),
            pltpu.SemaphoreType.DMA((12,)),
        ],
    )(meta, own, oth, w, probe)


def prepare_kernel(meta, r, prm, pay, x, bc, rows_out, cols_out, t_out, q_out, p):
    total = r[0, 0:512, :].astype(F32)
    raw = r[0, 512:528, :].astype(F32)
    for d in range(1, 4):
        total += r[d, 0:512, :].astype(F32)
        raw += r[d, 512:528, :].astype(F32)
    x[...] = total[:, 0:256]
    bc[...] = total[:, 256:512].astype(BF16)
    upper = (iota((128, 128), 0) <= iota((128, 128), 1)).astype(F32)
    top = iota((8, 128), 0) < 4
    bias, rate = prm[0], prm[1]
    through = []
    for k in range(4):
        here = slice(128 * k, 128 * k + 128)
        z = raw[0:8, here] + bias
        dt = jnp.maximum(z, 0.0) + jnp.log1p(jnp.exp(-jnp.abs(z)))
        logs = jnp.dot(-dt * rate, upper, precision=HIGH, preferred_element_type=F32)
        source = lax.rem(k + meta[1], 4)
        p[k, 0:64, :] = r[source, 528:592, 0:256]
        p[k, 64:128, :] = r[source, 528:592, 256:512]
        seg = r[source, 512:528, 0:128].astype(F32)[8:16]
        rows = jnp.concatenate([jnp.where(top, logs, pltpu.roll(dt, 4, 0)), jnp.where(top, z, pltpu.roll(seg, 4, 0))], axis=0)
        cols = jnp.concatenate([rows, jnp.zeros((112, 128), F32)], axis=0).T
        rows_out[k] = rows
        cols_out[k] = cols
        carry, tail, thru = weights_of(rows, cols)
        through.append(thru)
        carry_x = spread(lanes(carry))
        tail_x = spread([tail[:, h : h + 1] * cols[:, 4 + h : 5 + h] for h in range(4)])
        b, c = bc[here, 0:128], bc[here, 128:256]
        t_out[k] = dot_tn((x[here, :] * tail_x).astype(BF16), b)
        q_out[k] = dot_tn((p[k, 0:128, :].astype(F32) * carry_x).astype(BF16), c)
    state = t_out[0]
    grad = q_out[3]
    whole = through[0]
    for k in range(1, 4):
        state = by_head_rows(lanes(through[k])) * state + t_out[k]
        grad = by_head_rows(lanes(through[3 - k])) * grad + q_out[3 - k]
        whole = whole * through[k]
    for k in range(1, 4):
        pay[k - 1, 0:256, :] = jnp.where(meta[2] + k < 4, state, grad).astype(BF16)
        pay[k - 1, 256:272, :] = jnp.broadcast_to(whole, (16, 128)).astype(BF16)


def prepare(meta, r, prm):
    return pl.pallas_call(
        prepare_kernel,
        in_specs=[SMEM, VMEM, VMEM],
        out_specs=[VMEM] * 8,
        out_shape=[
            jax.ShapeDtypeStruct((3, 272, 128), BF16),
            jax.ShapeDtypeStruct((512, 256), F32),
            jax.ShapeDtypeStruct((512, 256), BF16),
            jax.ShapeDtypeStruct((4, 16, 128), F32),
            jax.ShapeDtypeStruct((4, 128, 128), F32),
            jax.ShapeDtypeStruct((4, 256, 128), F32),
            jax.ShapeDtypeStruct((4, 256, 128), F32),
            jax.ShapeDtypeStruct((4, 128, 256), BF16),
        ],
    )(meta, r, prm)


def intra_kernel(x, bc, p, rows_in, cols_in, skip, dx, dbc, e):
    seen = iota((128, 128), 0) >= iota((128, 128), 1)
    lane = iota((128, 128), 1)
    for k in range(4):
        here = slice(128 * k, 128 * k + 128)
        b, c = bc[here, 0:128], bc[here, 128:256]
        rows, cols = rows_in[k], cols_in[k]
        scores = dot_nt(c, b)
        visible = (cols[:, 12:13] == rows[12:13, :]) & seen
        d_scores = jnp.zeros((128, 128), F32)
        by_row = jnp.zeros((128, 128), F32)
        sums = []
        for tile in range(2):
            part = slice(128 * tile, 128 * tile + 128)
            probe = p[k, 0:128, part].astype(F32)
            values = x[here, part].astype(BF16)
            d_values = skip[:, part] * probe
            for a in range(2):
                h = 2 * tile + a
                mine = jnp.where((lane < 64) if a == 0 else (lane >= 64), probe, 0.0).astype(BF16)
                pulled = dot_nt(mine, values)
                decay = jnp.exp(jnp.where(visible, cols[:, h : h + 1] - rows[h : h + 1, :], -1e30))
                steps = rows[4 + h : 5 + h, :]
                weighted = decay * pulled
                decayed = decay * scores
                plain = weighted * scores
                sums.append(jnp.sum(plain, axis=0, keepdims=True))
                by_row = jnp.where(lane == h, jnp.sum(plain * steps, axis=1, keepdims=True), by_row)
                d_scores += weighted * steps
                d_values += dot_tn((decayed * steps).astype(BF16), mine)
            dx[here, part] = d_values
        d_scores = d_scores.astype(BF16)
        dbc[here, 0:128] = dot_tn(d_scores, c)
        dbc[here, 128:256] = dot_nn(d_scores, b)
        sub = iota((8, 128), 0)
        down = jnp.zeros((8, 128), F32)
        for h in range(4):
            down = jnp.where(sub == h, jnp.broadcast_to(sums[h], (8, 128)), down)
        dt = pltpu.roll(rows[0:8], 4, 0)
        e[k, 0:8, :] = down
        e[k, 8:16, :] = by_row.T[0:8] - dt * down


def intra(x, bc, p, rows, cols, skip):
    return pl.pallas_call(
        intra_kernel,
        in_specs=[VMEM] * 6,
        out_specs=[VMEM] * 3,
        out_shape=[
            jax.ShapeDtypeStruct((512, 256), F32),
            jax.ShapeDtypeStruct((512, 256), F32),
            jax.ShapeDtypeStruct((4, 16, 128), F32),
        ],
    )(x, bc, p, rows, cols, skip)


def finish_kernel(meta, r1, r2, r3, x, bc, p, rows_in, cols_in, t_in, q_in, dx, dbc, e, prm, out):
    quarter = meta[2]
    got = (r1, r2, r3)
    parts = [ref[0:256, :].astype(F32) for ref in got]
    decays = [by_head_rows(lanes(ref[256:272, :].astype(F32)[0:1])) for ref in got]

    def total(order):
        out_sum = jnp.zeros((256, 128), F32)
        run = jnp.ones((256, 128), F32)
        for index, valid in order:
            out_sum += jnp.where(valid, run * parts[index], 0.0)
            run = jnp.where(valid, run * decays[index], run)
        return out_sum

    entering = total([(k - 1, quarter - k >= 0) for k in (1, 2, 3)])
    leaving = total([(3 - m, quarter + m <= 3) for m in (1, 2, 3)])
    weights = [weights_of(rows_in[k], cols_in[k]) for k in range(4)]
    through = [by_head_rows(lanes(weights[k][2])) for k in range(4)]
    states, grads = [entering], [leaving]
    for k in range(3):
        states.append(through[k] * states[k] + t_in[k])
        grads.append(through[3 - k] * grads[k] + q_in[3 - k])
    grads = grads[::-1]
    indicator = (iota((8, 256), 1) // 64 == iota((8, 256), 0)).astype(F32)
    lower = (iota((128, 128), 0) >= iota((128, 128), 1)).astype(F32)
    sub, lane = iota((8, 128), 0), iota((8, 128), 1)
    rate = prm[1]

    def by_head(product):
        dims = (((1,), (1,)), ((), ()))
        return lax.dot_general(indicator, product, dims, precision=HIGH, preferred_element_type=F32)

    for k in range(4):
        here = slice(128 * k, 128 * k + 128)
        rows, cols = rows_in[k], cols_in[k]
        carry, tail, thru = weights[k]
        b, c = bc[here, 0:128], bc[here, 128:256]
        carry_x = spread(lanes(carry))
        tail_x = spread(lanes(tail))
        step_x = spread([cols[:, 4 + h : 5 + h] for h in range(4)])
        state, grad = states[k].astype(BF16), grads[k].astype(BF16)
        probe = p[k, 0:128, :].astype(F32) * carry_x
        values = x[here, :] * tail_x
        carried = probe * dot_nt(c, state)
        pulled = dot_nt(b, grad)
        out[here, 0:256] = (dx[here, :] + tail_x * step_x * pulled).astype(BF16)
        d_b = dbc[here, 0:128] + dot_nn((values * step_x).astype(BF16), grad)
        d_c = dbc[here, 128:256] + dot_nn(probe.astype(BF16), state)
        out[here, 256:384] = d_b.astype(BF16)
        out[here, 384:512] = d_c.astype(BF16)
        from_carry = by_head(carried)
        from_tail = by_head(values * pulled)
        dt = pltpu.roll(rows[0:8], 4, 0)
        d_log = e[k, 8:16, :] + from_carry - dt * from_tail
        both = jnp.sum(grads[k] * states[k], axis=1, keepdims=True)
        end = jnp.sum(jnp.where(sub < 4, dt * from_tail, 0.0), axis=1, keepdims=True)
        for h in range(4):
            own = jnp.sum(both[64 * h : 64 * h + 64], axis=0, keepdims=True) * thru[:, h : h + 1]
            end = jnp.where(sub[:, 0:1] == h, end + own, end)
        d_log = jnp.where(lane == 127, d_log + end, d_log)
        d_step = jnp.dot(d_log, lower, precision=HIGH, preferred_element_type=F32)
        d_dt = e[k, 0:8, :] + from_tail - rate * d_step
        z = rows[8:16]
        d_z = jnp.where(sub < 4, d_dt / (1.0 + jnp.exp(-z)), 0.0)
        out[512:528, here] = jnp.concatenate([d_z, jnp.zeros((8, 128), F32)], axis=0).astype(BF16)


def finish(meta, *args):
    return pl.pallas_call(
        finish_kernel,
        in_specs=[SMEM] + [VMEM] * len(args),
        out_specs=VMEM,
        out_shape=jax.ShapeDtypeStruct((528, 512), BF16),
    )(meta, *args)


def pull_half(flip, meta, w, full, out, buf, sems):
    half = lax.rem(meta[0] + flip, 2) * 1024
    copies = []
    for j in range(4):
        here = pl.ds(pl.multiple_of(half + 256 * j, 256), 256)
        copies.append(pltpu.make_async_copy(w.at[here], buf.at[j], sems.at[j]))
    for copy in copies:
        copy.start()
    yield
    for j in range(4):
        copies[j].wait()
        part = dot_nn(buf[j], full[...]).T.astype(BF16)
        for k in range(4):
            out[lax.rem(k + meta[1], 4), :, 256 * j : 256 * j + 256] = part[128 * k : 128 * k + 128]
    yield


def pull_first_kernel(meta, g, w, full, out, buf, sems):
    phases = pull_half(1, meta, w, full, out, buf, sems)
    next(phases)
    shared = g[0, 0:512, 256:512].astype(F32)
    for d in range(4):
        full[256 * d : 256 * d + 256, :] = g[d, 0:512, 0:256].astype(F32).T.astype(BF16)
        if d:
            shared += g[d, 0:512, 256:512].astype(F32)
    full[1024:1280, :] = shared.T.astype(BF16)
    top = iota((8, 512), 0) < 4
    steps = [g[d, 512:528, :].astype(F32)[0:8] for d in range(4)]
    pairs = [jnp.where(top, steps[2 * j], pltpu.roll(steps[2 * j + 1], 4, 0)) for j in range(2)]
    full[1280:1408, :] = jnp.concatenate(pairs + [jnp.zeros((112, 512), F32)], axis=0).astype(BF16)
    next(phases)


def pull_second_kernel(meta, full, w, out, buf, sems):
    for _ in pull_half(0, meta, w, full, out, buf, sems):
        pass


PULL_SCRATCH = [pltpu.VMEM((4, 256, WIDE), BF16), pltpu.SemaphoreType.DMA((4,))]
PULLED = jax.ShapeDtypeStruct((4, 128, 1024), BF16)


def pull_first(meta, g, w):
    return pl.pallas_call(
        pull_first_kernel,
        in_specs=[SMEM, VMEM, ANY],
        out_specs=[VMEM] * 2,
        out_shape=[jax.ShapeDtypeStruct((WIDE, 512), BF16), PULLED],
        scratch_shapes=PULL_SCRATCH,
    )(meta, g, w)


def pull_second(meta, full, w):
    return pl.pallas_call(
        pull_second_kernel,
        in_specs=[SMEM, VMEM, ANY],
        out_specs=VMEM,
        out_shape=PULLED,
        scratch_shapes=PULL_SCRATCH,
    )(meta, full, w)


def to_all(x, axis):
    return lax.all_to_all(jnp.broadcast_to(x[None], (4,) + x.shape), axis, split_axis=0, concat_axis=0)


def shifted(x, axis, k):
    return lax.ppermute(x, axis, [(i, (i + k) % 4) for i in range(4)])


def sum_of_four(x, axis):
    return x + shifted(x, axis, 1) + shifted(x, axis, 2) + shifted(x, axis, 3)


SWAP = [(0, 1), (1, 0)]


def body(tokens, frame_feats, w_proj, frame_pos, segments, signs, w_x, w_bc, w_dt, dt_bias, decay_rate, skip_gain, probe):
    x_at, z_at, core_at = lax.axis_index(X), lax.axis_index("z"), lax.axis_index("core")
    across = lax.rem(z_at, 4)
    origin = 2 * lax.rem(across, 2) + across // 2
    quarter = 2 * lax.rem(origin, 2) + z_at // 4
    meta = jnp.stack([core_at, origin, quarter, z_at]).astype(jnp.int32)
    w_all = pack(w_x, w_bc, w_dt)

    weights = lax.all_gather(w_all, "z", axis=0, tiled=True)

    frame_emb = jnp.dot(frame_feats[0], w_proj, preferred_element_type=F32).astype(BF16)
    slot = frame_pos[0] - CHUNK * (jnp.arange(32, dtype=jnp.int32) // 2)
    tagged = jnp.concatenate([frame_emb, jnp.broadcast_to(slot.astype(BF16)[:, None], (32, 128))], axis=1)
    arrived = lax.all_to_all(tagged, SEQ, split_axis=0, concat_axis=0, tiled=True)
    segment = segments[0]
    before = lax.ppermute(segment[-1:], X + ("z",), [(i, i + 1) for i in range(31)])
    ids = jnp.concatenate([segment[None], jnp.broadcast_to(before[None], (15, CHUNK))]).astype(BF16)
    probe_ids = jnp.concatenate([probe[0], jnp.tile(ids, (1, 8))], axis=0)
    local_pos = arrived[:, 1024].astype(jnp.int32)
    merged = tokens[0].at[local_pos].set(arrived[:, :1024])
    moved = lax.ppermute(merged, AXES, features_route())
    moved, probe_ids = lax.optimization_barrier((moved, probe_ids))
    probe_ids = lax.ppermute(probe_ids, X + ("z",), probe_route())
    own = to_all(moved, "y")
    oth = lax.ppermute(own, "core", SWAP)

    def four(v):
        return lax.dynamic_slice(v, (4 * x_at,), (4,))

    prm = jnp.stack([four(dt_bias), four(decay_rate)])
    prm = jnp.concatenate([prm, jnp.zeros((2, 4), F32)], axis=1)
    prm = jnp.broadcast_to(prm[:, :, None], (2, 8, 128))
    skip = jnp.repeat(four(skip_gain), 64)[None, :]

    partial_proj = project(meta, own, oth, weights, probe_ids)
    received = lax.all_to_all(partial_proj, X, split_axis=0, concat_axis=0)
    pay, values, bc, rows, cols, t_all, q_all, probes = prepare(meta, received, prm)
    got = [lax.ppermute(pay[k - 1], "z", quarter_route(k)) for k in (1, 2, 3)]
    dx, dbc, e = intra(values, bc, probes, rows, cols, skip)
    grads = finish(meta, *got, values, bc, probes, rows, cols, t_all, q_all, dx, dbc, e, prm)
    everyone = to_all(grads, X)
    full, oth_part = pull_first(meta, everyone, weights)
    swapped = lax.ppermute(oth_part, "core", SWAP)
    own_part = pull_second(meta, full, weights)
    both = (own_part.astype(F32) + swapped.astype(F32)).astype(BF16)
    pieces = lax.all_to_all(both, "y", split_axis=0, concat_axis=0)
    away = jnp.sum(pieces.astype(F32), axis=0)
    squares = jnp.broadcast_to(jnp.sum(away * away), (8, 128))
    back = [(b, a) for a, b in features_route()]
    gradient = lax.ppermute(away.astype(BF16), AXES, back)
    squares = squares + lax.ppermute(squares, "core", SWAP)
    squares = sum_of_four(squares, X)
    squares = lax.ppermute(squares, AXES, back)[0, 0]

    direction = (2 * signs[0] - 1).astype(F32)[:, None]
    step = 0.5 * direction * gradient.astype(F32)
    picked = (direction.astype(BF16) * gradient)[local_pos]
    high = squares.astype(BF16)
    low = (squares - high.astype(F32)).astype(BF16)
    lane = jnp.arange(128)[None, :]
    tail = jnp.broadcast_to(jnp.where(lane < 64, high, low), (32, 128))
    returned = lax.all_to_all(jnp.concatenate([picked, tail], axis=1), SEQ, split_axis=0, concat_axis=0, tiled=True)
    sums = returned[::2, 1024:].astype(F32)
    entries = 2048 * 8192
    grad_scale = jnp.sqrt((jnp.sum(sums[:, 0]) + jnp.sum(sums[:, 64])) / entries + 1e-06)
    adv = (merged.astype(F32) + step / grad_scale).astype(BF16)
    adv_frames = (frame_emb.astype(F32) + 0.5 * returned[:, :1024].astype(F32) / grad_scale).astype(BF16)
    return (adv[None], adv_frames[None])


def solution(mesh):
    mesh = Mesh(mesh.devices.reshape(2, 2, 8, 4, 2), AXES)

    return jax.shard_map(
        body,
        mesh=mesh,
        in_specs=(
            P("x_hi", SEQ, TENSOR),
            P("x_hi", SEQ, None),
            P(None, TENSOR),
            P("x_hi", SEQ),
            P("x_hi", SEQ),
            P("x_hi", SEQ),
            P(("x_hi",) + SEQ, TENSOR),
            P(("x_hi",) + SEQ, TENSOR),
            P(("x_hi",) + SEQ, TENSOR),
            P(TENSOR),
            P(TENSOR),
            P(TENSOR),
            P("x_hi", SEQ, TENSOR),
        ),
        out_specs=(P("x_hi", SEQ, TENSOR), P("x_hi", SEQ, TENSOR)),
        check_vma=False,
    )
```

```python
import jax
import jax.numpy as jnp
from jax import lax
from jax.experimental import pallas as pl
from jax.experimental.pallas import tpu as pltpu
from jax.sharding import Mesh, PartitionSpec as P


F32, BF16 = jnp.float32, jnp.bfloat16
AXES = ("x_hi", "x_lo", "z", "y", "core")
X = ("x_hi", "x_lo")
SEQ = ("x_lo", "z")
TENSOR = ("y", "core")
CHUNK = 128
WIDE = 1408
PLACE = (0, 2, 1, 3)
GATHERED = 768
HIGH = lax.Precision.HIGHEST
VMEM = pl.BlockSpec(memory_space=pltpu.VMEM)
SMEM = pl.BlockSpec(memory_space=pltpu.SMEM)


def linear(x, z, y, core):
    return ((x * 8 + z) * 4 + y) * 2 + core


def features_route():
    pairs = []
    for x in range(4):
        for z in range(8):
            for y in range(4):
                for core in range(2):
                    there = linear(y, 4 * (z // 4) + PLACE[x], (z % 4 + x) % 4, core)
                    pairs.append((linear(x, z, y, core), there))
    return pairs


def probe_route():
    pairs = []
    for x in range(4):
        for z in range(8):
            pairs.append((x * 8 + z, (z % 4 + x) % 4 * 8 + 4 * (z // 4) + PLACE[x]))
    return pairs


def quarter_route(k):
    pairs = []
    for z in range(8):
        home = PLACE[z % 4]
        to = (2 * (home % 2) + z // 4 + k) % 4
        pairs.append((z, 4 * (to % 2) + PLACE[home // 2 * 2 + to // 2]))
    return pairs


def dot_nt(a, b):
    return lax.dot_general(a, b, (((1,), (1,)), ((), ())), preferred_element_type=F32)


def dot_tn(a, b):
    return lax.dot_general(a, b, (((0,), (0,)), ((), ())), preferred_element_type=F32)


def dot_nn(a, b):
    return jnp.dot(a, b, preferred_element_type=F32)


def iota(shape, dim):
    return lax.broadcasted_iota(jnp.int32, shape, dim)


def spread(columns):
    left = iota((CHUNK, 128), 1) < 64
    tiles = [
        jnp.where(left, jnp.broadcast_to(columns[2 * i], (CHUNK, 128)), jnp.broadcast_to(columns[2 * i + 1], (CHUNK, 128)))
        for i in range(2)
    ]
    return jnp.concatenate(tiles, axis=1)


def by_head_rows(values):
    rows = iota((256, 128), 0)
    out = jnp.broadcast_to(values[3], (256, 128))
    for h in (2, 1, 0):
        out = jnp.where(rows < 64 * (h + 1), jnp.broadcast_to(values[h], (256, 128)), out)
    return out


def lanes(row):
    return [row[:, h : h + 1] for h in range(4)]


def weights_of(rows, cols):
    seg = cols[:, 12:13]
    prev, last = rows[13:14, 127:128], rows[12:13, 127:128]
    end = cols[127:128, :]
    carry = jnp.where(seg == prev, jnp.exp(cols), 0.0)
    tail = jnp.where(seg == last, jnp.exp(end - cols), 0.0)
    through = jnp.where(last == prev, jnp.exp(end), 0.0)
    return carry, tail, through


def pack_kernel(w_x, w_bc, w_dt, out):
    out[:, 0:256] = w_x[:, GATHERED:1024]
    out[:, 256:512] = w_bc[...]
    out[:, 512:640] = jnp.zeros((256, 128), BF16)
    out[:, 512:528] = w_dt[...]


def pack(*parts):
    return pl.pallas_call(
        pack_kernel, in_specs=[VMEM] * 3, out_specs=VMEM, out_shape=jax.ShapeDtypeStruct((256, WIDE - GATHERED), BF16)
    )(*parts)


TILES = [(256 * t, min(256 * t + 256, WIDE)) for t in range(6)]
ANY = pl.BlockSpec(memory_space=pl.ANY)


def ring_rows(meta, i):
    place = lax.rem(meta[3] + (0, 7, 1, 6, 2, 5, 3, 4)[i], 8)
    row = lax.rem(place // 4 + meta[0], 2) * 1024 + lax.rem(place, 4) * 256
    return pl.multiple_of(row, 256)


def project_kernel(meta, own, oth, probe, w, *rest):
    blocks, (out, kept), (buf, rows, sems, out_sems) = rest[:9], rest[9:11], rest[11:]
    copies = []
    for t, (lo, hi) in enumerate(TILES[:3]):
        for n in range(2):
            here = pl.ds(pl.multiple_of(lax.rem(meta[0] + n, 2) * 1024, 1024), 1024)
            there = buf.at[1024 * n : 1024 * n + 1024, lo:hi]
            copies.append(pltpu.make_async_copy(w.at[here, lo:hi], there, sems.at[2 * t + n]))
    for i in range(7):
        there = buf.at[pl.ds(ring_rows(meta, i), 256), GATHERED:WIDE]
        copies.append(pltpu.make_async_copy(blocks[i], there, sems.at[6 + i]))
    for n in range(2):
        there = buf.at[pl.ds(pl.multiple_of(ring_rows(meta, 7) + 128 * n, 128), 128), GATHERED:WIDE]
        copies.append(pltpu.make_async_copy(blocks[7 + n], there, sems.at[13 + n]))
    stores = [pltpu.make_async_copy(buf.at[:, lo:hi], kept.at[:, lo:hi], out_sems.at[t]) for t, (lo, hi) in enumerate(TILES[:3])]
    stores.append(pltpu.make_async_copy(buf.at[:, GATHERED:WIDE], kept.at[:, GATHERED:WIDE], out_sems.at[3]))
    for copy in copies:
        copy.start()
    for n, ref in enumerate((own, oth)):
        for k in range(4):
            rows[128 * k : 128 * k + 128, 1024 * n : 1024 * n + 1024] = ref[lax.rem(k + meta[1], 4)]
    ids = probe[128:144, 0:512].astype(F32)[0:8]
    for d in range(4):
        part = slice(256 * d, 256 * d + 256)
        out[d, 528:592, 0:256] = probe[0:64, part]
        out[d, 528:592, 256:512] = probe[64:128, part]
    for t, (lo, hi) in enumerate(TILES):
        if t <= 3:
            for copy in copies[2 * t : 2 * t + 2] if t < 3 else copies[6:]:
                copy.wait()
            stores[t].start()
        total = dot_nn(rows[...], buf[:, lo:hi])
        if t < 4:
            out[t, 0:512, 0:256] = total.astype(BF16)
        elif t == 4:
            for d in range(4):
                out[d, 0:512, 256:512] = total.astype(BF16)
        else:
            steps = total.T
            for d in range(4):
                mine = jnp.concatenate([steps[4 * d : 4 * d + 4], jnp.zeros((4, 512), F32), ids], axis=0)
                out[d, 512:528, :] = mine.astype(BF16)
    for store in stores:
        store.wait()


def project(meta, own, oth, probe, w, blocks):
    return pl.pallas_call(
        project_kernel,
        in_specs=[SMEM, VMEM, VMEM, VMEM] + [ANY] * 10,
        out_specs=[VMEM, ANY],
        out_shape=[jax.ShapeDtypeStruct((4, 592, 512), BF16), jax.ShapeDtypeStruct((2048, WIDE), BF16)],
        scratch_shapes=[
            pltpu.VMEM((2048, WIDE), BF16),
            pltpu.VMEM((512, 2048), BF16),
            pltpu.SemaphoreType.DMA((15,)),
            pltpu.SemaphoreType.DMA((4,)),
        ],
    )(meta, own, oth, probe, w, *blocks)


def prepare_kernel(meta, r, prm, pay, x, bc, rows_out, cols_out, t_out, q_out, p):
    total = r[0, 0:512, :].astype(F32)
    raw = r[0, 512:528, :].astype(F32)
    for d in range(1, 4):
        total += r[d, 0:512, :].astype(F32)
        raw += r[d, 512:528, :].astype(F32)
    x[...] = total[:, 0:256]
    bc[...] = total[:, 256:512].astype(BF16)
    upper = (iota((128, 128), 0) <= iota((128, 128), 1)).astype(F32)
    top = iota((8, 128), 0) < 4
    bias, rate = prm[0], prm[1]
    through = []
    for k in range(4):
        here = slice(128 * k, 128 * k + 128)
        z = raw[0:8, here] + bias
        dt = jnp.maximum(z, 0.0) + jnp.log1p(jnp.exp(-jnp.abs(z)))
        logs = jnp.dot(-dt * rate, upper, precision=HIGH, preferred_element_type=F32)
        source = lax.rem(k + meta[1], 4)
        p[k, 0:64, :] = r[source, 528:592, 0:256]
        p[k, 64:128, :] = r[source, 528:592, 256:512]
        seg = r[source, 512:528, 0:128].astype(F32)[8:16]
        rows = jnp.concatenate([jnp.where(top, logs, pltpu.roll(dt, 4, 0)), jnp.where(top, z, pltpu.roll(seg, 4, 0))], axis=0)
        cols = jnp.concatenate([rows, jnp.zeros((112, 128), F32)], axis=0).T
        rows_out[k] = rows
        cols_out[k] = cols
        carry, tail, thru = weights_of(rows, cols)
        through.append(thru)
        carry_x = spread(lanes(carry))
        tail_x = spread([tail[:, h : h + 1] * cols[:, 4 + h : 5 + h] for h in range(4)])
        b, c = bc[here, 0:128], bc[here, 128:256]
        t_out[k] = dot_tn((x[here, :] * tail_x).astype(BF16), b)
        q_out[k] = dot_tn((p[k, 0:128, :].astype(F32) * carry_x).astype(BF16), c)
    state = t_out[0]
    grad = q_out[3]
    whole = through[0]
    for k in range(1, 4):
        state = by_head_rows(lanes(through[k])) * state + t_out[k]
        grad = by_head_rows(lanes(through[3 - k])) * grad + q_out[3 - k]
        whole = whole * through[k]
    for k in range(1, 4):
        pay[k - 1, 0:256, :] = jnp.where(meta[2] + k < 4, state, grad).astype(BF16)
        pay[k - 1, 256:272, :] = jnp.broadcast_to(whole, (16, 128)).astype(BF16)


def prepare(meta, r, prm):
    return pl.pallas_call(
        prepare_kernel,
        in_specs=[SMEM, VMEM, VMEM],
        out_specs=[VMEM] * 8,
        out_shape=[
            jax.ShapeDtypeStruct((3, 272, 128), BF16),
            jax.ShapeDtypeStruct((512, 256), F32),
            jax.ShapeDtypeStruct((512, 256), BF16),
            jax.ShapeDtypeStruct((4, 16, 128), F32),
            jax.ShapeDtypeStruct((4, 128, 128), F32),
            jax.ShapeDtypeStruct((4, 256, 128), F32),
            jax.ShapeDtypeStruct((4, 256, 128), F32),
            jax.ShapeDtypeStruct((4, 128, 256), BF16),
        ],
    )(meta, r, prm)


def intra_kernel(x, bc, p, rows_in, cols_in, skip, dx, dbc, e):
    seen = iota((128, 128), 0) >= iota((128, 128), 1)
    lane = iota((128, 128), 1)
    k, here = 0, slice(0, 128)
    b, c = bc[here, 0:128], bc[here, 128:256]
    rows, cols = rows_in[k], cols_in[k]
    scores = dot_nt(c, b)
    visible = (cols[:, 12:13] == rows[12:13, :]) & seen
    d_scores = jnp.zeros((128, 128), F32)
    by_row = jnp.zeros((128, 128), F32)
    sums = []
    for tile in range(2):
        part = slice(128 * tile, 128 * tile + 128)
        probe = p[k, 0:128, part].astype(F32)
        values = x[here, part].astype(BF16)
        d_values = skip[:, part] * probe
        for a in range(2):
            h = 2 * tile + a
            mine = jnp.where((lane < 64) if a == 0 else (lane >= 64), probe, 0.0).astype(BF16)
            pulled = dot_nt(mine, values)
            decay = jnp.exp(jnp.where(visible, cols[:, h : h + 1] - rows[h : h + 1, :], -1e30))
            steps = rows[4 + h : 5 + h, :]
            weighted = decay * pulled
            decayed = decay * scores
            plain = weighted * scores
            sums.append(jnp.sum(plain, axis=0, keepdims=True))
            by_row = jnp.where(lane == h, jnp.sum(plain * steps, axis=1, keepdims=True), by_row)
            d_scores += weighted * steps
            d_values += dot_tn((decayed * steps).astype(BF16), mine)
        dx[here, part] = d_values
    d_scores = d_scores.astype(BF16)
    dbc[here, 0:128] = dot_tn(d_scores, c)
    dbc[here, 128:256] = dot_nn(d_scores, b)
    sub = iota((8, 128), 0)
    down = jnp.zeros((8, 128), F32)
    for h in range(4):
        down = jnp.where(sub == h, jnp.broadcast_to(sums[h], (8, 128)), down)
    dt = pltpu.roll(rows[0:8], 4, 0)
    e[k, 0:8, :] = down
    e[k, 8:16, :] = by_row.T[0:8] - dt * down


def intra(x, bc, p, rows, cols, skip):
    tall = pl.BlockSpec((128, 256), lambda i: (i, 0))
    flat = lambda *shape: pl.BlockSpec((1,) + shape, lambda i: (i, 0, 0))
    return pl.pallas_call(
        intra_kernel,
        grid=(4,),
        in_specs=[tall, tall, flat(128, 256), flat(16, 128), flat(128, 128), pl.BlockSpec((1, 256), lambda i: (0, 0))],
        out_specs=[tall, tall, flat(16, 128)],
        out_shape=[
            jax.ShapeDtypeStruct((512, 256), F32),
            jax.ShapeDtypeStruct((512, 256), F32),
            jax.ShapeDtypeStruct((4, 16, 128), F32),
        ],
    )(x, bc, p, rows, cols, skip)


def finish_kernel(meta, r1, r2, r3, x, bc, p, rows_in, cols_in, t_in, q_in, dx, dbc, e, prm, out):
    quarter = meta[2]
    got = (r1, r2, r3)
    parts = [ref[0:256, :].astype(F32) for ref in got]
    decays = [by_head_rows(lanes(ref[256:272, :].astype(F32)[0:1])) for ref in got]

    def total(order):
        out_sum = jnp.zeros((256, 128), F32)
        run = jnp.ones((256, 128), F32)
        for index, valid in order:
            out_sum += jnp.where(valid, run * parts[index], 0.0)
            run = jnp.where(valid, run * decays[index], run)
        return out_sum

    entering = total([(k - 1, quarter - k >= 0) for k in (1, 2, 3)])
    leaving = total([(3 - m, quarter + m <= 3) for m in (1, 2, 3)])
    weights = [weights_of(rows_in[k], cols_in[k]) for k in range(4)]
    through = [by_head_rows(lanes(weights[k][2])) for k in range(4)]
    states, grads = [entering], [leaving]
    for k in range(3):
        states.append(through[k] * states[k] + t_in[k])
        grads.append(through[3 - k] * grads[k] + q_in[3 - k])
    grads = grads[::-1]
    indicator = (iota((8, 256), 1) // 64 == iota((8, 256), 0)).astype(F32)
    lower = (iota((128, 128), 0) >= iota((128, 128), 1)).astype(F32)
    sub, lane = iota((8, 128), 0), iota((8, 128), 1)
    rate = prm[1]

    def by_head(product):
        dims = (((1,), (1,)), ((), ()))
        return lax.dot_general(indicator, product, dims, precision=HIGH, preferred_element_type=F32)

    for k in range(4):
        here = slice(128 * k, 128 * k + 128)
        rows, cols = rows_in[k], cols_in[k]
        carry, tail, thru = weights[k]
        b, c = bc[here, 0:128], bc[here, 128:256]
        carry_x = spread(lanes(carry))
        tail_x = spread(lanes(tail))
        step_x = spread([cols[:, 4 + h : 5 + h] for h in range(4)])
        state, grad = states[k].astype(BF16), grads[k].astype(BF16)
        probe = p[k, 0:128, :].astype(F32) * carry_x
        values = x[here, :] * tail_x
        carried = probe * dot_nt(c, state)
        pulled = dot_nt(b, grad)
        out[here, 0:256] = (dx[here, :] + tail_x * step_x * pulled).astype(BF16)
        d_b = dbc[here, 0:128] + dot_nn((values * step_x).astype(BF16), grad)
        d_c = dbc[here, 128:256] + dot_nn(probe.astype(BF16), state)
        out[here, 256:384] = d_b.astype(BF16)
        out[here, 384:512] = d_c.astype(BF16)
        from_carry = by_head(carried)
        from_tail = by_head(values * pulled)
        dt = pltpu.roll(rows[0:8], 4, 0)
        d_log = e[k, 8:16, :] + from_carry - dt * from_tail
        both = jnp.sum(grads[k] * states[k], axis=1, keepdims=True)
        end = jnp.sum(jnp.where(sub < 4, dt * from_tail, 0.0), axis=1, keepdims=True)
        for h in range(4):
            own = jnp.sum(both[64 * h : 64 * h + 64], axis=0, keepdims=True) * thru[:, h : h + 1]
            end = jnp.where(sub[:, 0:1] == h, end + own, end)
        d_log = jnp.where(lane == 127, d_log + end, d_log)
        d_step = jnp.dot(d_log, lower, precision=HIGH, preferred_element_type=F32)
        d_dt = e[k, 0:8, :] + from_tail - rate * d_step
        z = rows[8:16]
        d_z = jnp.where(sub < 4, d_dt / (1.0 + jnp.exp(-z)), 0.0)
        out[512:528, here] = jnp.concatenate([d_z, jnp.zeros((8, 128), F32)], axis=0).astype(BF16)


def finish(meta, *args):
    return pl.pallas_call(
        finish_kernel,
        in_specs=[SMEM] + [VMEM] * len(args),
        out_specs=VMEM,
        out_shape=jax.ShapeDtypeStruct((528, 512), BF16),
    )(meta, *args)


def pull_half(flip, meta, w, full, out, buf, sems):
    copies = []
    for j in range(4):
        row = 1024 * flip + 256 * j
        copies.append(pltpu.make_async_copy(w.at[row : row + 256], buf.at[j], sems.at[j]))
    for copy in copies:
        copy.start()
    yield
    for j in range(4):
        copies[j].wait()
        part = dot_nn(buf[j], full[...]).T.astype(BF16)
        for k in range(4):
            out[lax.rem(k + meta[1], 4), :, 256 * j : 256 * j + 256] = part[128 * k : 128 * k + 128]
    yield


def pull_first_kernel(meta, g, w, full, out, buf, sems):
    phases = pull_half(1, meta, w, full, out, buf, sems)
    next(phases)
    shared = g[0, 0:512, 256:512].astype(F32)
    for d in range(4):
        full[256 * d : 256 * d + 256, :] = g[d, 0:512, 0:256].astype(F32).T.astype(BF16)
        if d:
            shared += g[d, 0:512, 256:512].astype(F32)
    full[1024:1280, :] = shared.T.astype(BF16)
    top = iota((8, 512), 0) < 4
    steps = [g[d, 512:528, :].astype(F32)[0:8] for d in range(4)]
    pairs = [jnp.where(top, steps[2 * j], pltpu.roll(steps[2 * j + 1], 4, 0)) for j in range(2)]
    full[1280:1408, :] = jnp.concatenate(pairs + [jnp.zeros((112, 512), F32)], axis=0).astype(BF16)
    next(phases)


def pull_second_kernel(meta, full, w, out, buf, sems):
    for _ in pull_half(0, meta, w, full, out, buf, sems):
        pass


PULL_SCRATCH = [pltpu.VMEM((4, 256, WIDE), BF16), pltpu.SemaphoreType.DMA((4,))]
PULLED = jax.ShapeDtypeStruct((4, 128, 1024), BF16)


def pull_first(meta, g, w):
    return pl.pallas_call(
        pull_first_kernel,
        in_specs=[SMEM, VMEM, ANY],
        out_specs=[VMEM] * 2,
        out_shape=[jax.ShapeDtypeStruct((WIDE, 512), BF16), PULLED],
        scratch_shapes=PULL_SCRATCH,
    )(meta, g, w)


def pull_second(meta, full, w):
    return pl.pallas_call(
        pull_second_kernel,
        in_specs=[SMEM, VMEM, ANY],
        out_specs=VMEM,
        out_shape=PULLED,
        scratch_shapes=PULL_SCRATCH,
    )(meta, full, w)


def to_all(x, axis):
    return lax.all_to_all(jnp.broadcast_to(x[None], (4,) + x.shape), axis, split_axis=0, concat_axis=0)


def shifted(x, axis, k):
    return lax.ppermute(x, axis, [(i, (i + k) % 4) for i in range(4)])


def sum_of_four(x, axis):
    return x + shifted(x, axis, 1) + shifted(x, axis, 2) + shifted(x, axis, 3)


SWAP = [(0, 1), (1, 0)]


def body(tokens, frame_feats, w_proj, frame_pos, segments, signs, w_x, w_bc, w_dt, dt_bias, decay_rate, skip_gain, probe):
    x_at, z_at, core_at = lax.axis_index(X), lax.axis_index("z"), lax.axis_index("core")
    across = lax.rem(z_at, 4)
    origin = 2 * lax.rem(across, 2) + across // 2
    quarter = 2 * lax.rem(origin, 2) + z_at // 4
    meta = jnp.stack([core_at, origin, quarter, z_at]).astype(jnp.int32)
    gathered = lax.all_gather(w_x[:, :GATHERED], "z", axis=0, tiled=True)
    segment = segments[0]
    before = lax.ppermute(segment[-1:], X + ("z",), [(i, i + 1) for i in range(31)])
    ids = jnp.concatenate([segment[None], jnp.broadcast_to(before[None], (15, CHUNK))]).astype(BF16)
    probe_ids = jnp.concatenate([probe[0], jnp.tile(ids, (1, 8))], axis=0)

    def right(v):
        return lax.ppermute(v, "z", [(i, (i + 1) % 8) for i in range(8)])

    def left(v):
        return lax.ppermute(v, "z", [(i, (i + 7) % 8) for i in range(8)])

    w_ring = pack(w_x, w_bc, w_dt)
    r1, l1 = right(w_ring), left(w_ring)
    frame_emb = jnp.dot(frame_feats[0], w_proj, preferred_element_type=F32).astype(BF16)
    slot = frame_pos[0] - CHUNK * (jnp.arange(32, dtype=jnp.int32) // 2)
    tagged = jnp.concatenate([frame_emb, jnp.broadcast_to(slot.astype(BF16)[:, None], (32, 128))], axis=1)
    arrived = lax.all_to_all(tagged, SEQ, split_axis=0, concat_axis=0, tiled=True)
    local_pos = arrived[:, 1024].astype(jnp.int32)
    merged = tokens[0].at[local_pos].set(arrived[:, :1024])
    merged, r1, l1 = lax.optimization_barrier((merged, r1, l1))
    moved = lax.ppermute(merged, AXES, features_route())
    r2, l2 = right(r1), left(l1)
    moved, r2, l2, probe_ids = lax.optimization_barrier((moved, r2, l2, probe_ids))
    r3, l3 = right(r2), left(l2)
    own = to_all(moved, "y")
    own, r3, l3, probe_ids = lax.optimization_barrier((own, r3, l3, probe_ids))
    r4, l4 = right(r3[:128]), left(l3[128:])
    probe_ids = lax.ppermute(probe_ids, X + ("z",), probe_route())
    oth = lax.ppermute(own, "core", SWAP)

    def four(v):
        return lax.dynamic_slice(v, (4 * x_at,), (4,))

    prm = jnp.stack([four(dt_bias), four(decay_rate)])
    prm = jnp.concatenate([prm, jnp.zeros((2, 4), F32)], axis=1)
    prm = jnp.broadcast_to(prm[:, :, None], (2, 8, 128))
    skip = jnp.repeat(four(skip_gain), 64)[None, :]

    blocks = (w_ring, r1, l1, r2, l2, r3, l3, r4, l4)
    partial_proj, weights = project(meta, own, oth, probe_ids, gathered, blocks)
    received = lax.all_to_all(partial_proj, X, split_axis=0, concat_axis=0)
    pay, values, bc, rows, cols, t_all, q_all, probes = prepare(meta, received, prm)
    got = [lax.ppermute(pay[k - 1], "z", quarter_route(k)) for k in (1, 2, 3)]
    dx, dbc, e = intra(values, bc, probes, rows, cols, skip)
    grads = finish(meta, *got, values, bc, probes, rows, cols, t_all, q_all, dx, dbc, e, prm)
    everyone = to_all(grads, X)
    full, oth_part = pull_first(meta, everyone, weights)
    swapped = lax.ppermute(oth_part, "core", SWAP)
    own_part = pull_second(meta, full, weights)
    both = (own_part.astype(F32) + swapped.astype(F32)).astype(BF16)
    pieces = lax.all_to_all(both, "y", split_axis=0, concat_axis=0)
    away = jnp.sum(pieces.astype(F32), axis=0)
    squares = jnp.broadcast_to(jnp.sum(away * away), (8, 128))
    back = [(b, a) for a, b in features_route()]
    gradient = lax.ppermute(away.astype(BF16), AXES, back)
    squares = squares + lax.ppermute(squares, "core", SWAP)
    squares = sum_of_four(squares, X)
    squares = lax.ppermute(squares, AXES, back)[0, 0]

    direction = (2 * signs[0] - 1).astype(F32)[:, None]
    step = 0.5 * direction * gradient.astype(F32)
    picked = (direction.astype(BF16) * gradient)[local_pos]
    high = squares.astype(BF16)
    low = (squares - high.astype(F32)).astype(BF16)
    lane = jnp.arange(128)[None, :]
    tail = jnp.broadcast_to(jnp.where(lane < 64, high, low), (32, 128))
    returned = lax.all_to_all(jnp.concatenate([picked, tail], axis=1), SEQ, split_axis=0, concat_axis=0, tiled=True)
    sums = returned[::2, 1024:].astype(F32)
    entries = 2048 * 8192
    grad_scale = jnp.sqrt((jnp.sum(sums[:, 0]) + jnp.sum(sums[:, 64])) / entries + 1e-06)
    adv = (merged.astype(F32) + step / grad_scale).astype(BF16)
    adv_frames = (frame_emb.astype(F32) + 0.5 * returned[:, :1024].astype(F32) / grad_scale).astype(BF16)
    return (adv[None], adv_frames[None])


def solution(mesh):
    mesh = Mesh(mesh.devices.reshape(2, 2, 8, 4, 2), AXES)

    return jax.shard_map(
        body,
        mesh=mesh,
        in_specs=(
            P("x_hi", SEQ, TENSOR),
            P("x_hi", SEQ, None),
            P(None, TENSOR),
            P("x_hi", SEQ),
            P("x_hi", SEQ),
            P("x_hi", SEQ),
            P(("x_hi",) + SEQ, TENSOR),
            P(("x_hi",) + SEQ, TENSOR),
            P(("x_hi",) + SEQ, TENSOR),
            P(TENSOR),
            P(TENSOR),
            P(TENSOR),
            P("x_hi", SEQ, TENSOR),
        ),
        out_specs=(P("x_hi", SEQ, TENSOR), P("x_hi", SEQ, TENSOR)),
        check_vma=False,
    )
```

```python
import jax
import jax.numpy as jnp
from jax import lax
from jax.experimental import pallas as pl
from jax.experimental.pallas import tpu as pltpu
from jax.sharding import Mesh, PartitionSpec as P


F32, BF16 = jnp.float32, jnp.bfloat16
AXES = ("x_hi", "x_lo", "z", "y", "core")
X = ("x_hi", "x_lo")
SEQ = ("x_lo", "z")
TENSOR = ("y", "core")
CHUNK = 128
WIDE = 1408
PLACE = (0, 2, 1, 3)
HIGH = lax.Precision.HIGHEST
VMEM = pl.BlockSpec(memory_space=pltpu.VMEM)
SMEM = pl.BlockSpec(memory_space=pltpu.SMEM)


def linear(x, z, y, core):
    return ((x * 8 + z) * 4 + y) * 2 + core


def features_route():
    pairs = []
    for x in range(4):
        for z in range(8):
            for y in range(4):
                for core in range(2):
                    there = linear(y, 4 * (z // 4) + PLACE[x], (z % 4 + x) % 4, core)
                    pairs.append((linear(x, z, y, core), there))
    return pairs


def probe_route():
    pairs = []
    for x in range(4):
        for z in range(8):
            pairs.append((x * 8 + z, (z % 4 + x) % 4 * 8 + 4 * (z // 4) + PLACE[x]))
    return pairs


def quarter_route(k):
    pairs = []
    for z in range(8):
        home = PLACE[z % 4]
        to = (2 * (home % 2) + z // 4 + k) % 4
        pairs.append((z, 4 * (to % 2) + PLACE[home // 2 * 2 + to // 2]))
    return pairs


def dot_nt(a, b):
    return lax.dot_general(a, b, (((1,), (1,)), ((), ())), preferred_element_type=F32)


def dot_tn(a, b):
    return lax.dot_general(a, b, (((0,), (0,)), ((), ())), preferred_element_type=F32)


def dot_nn(a, b):
    return jnp.dot(a, b, preferred_element_type=F32)


def iota(shape, dim):
    return lax.broadcasted_iota(jnp.int32, shape, dim)


def spread(columns):
    left = iota((CHUNK, 128), 1) < 64
    tiles = [
        jnp.where(left, jnp.broadcast_to(columns[2 * i], (CHUNK, 128)), jnp.broadcast_to(columns[2 * i + 1], (CHUNK, 128)))
        for i in range(2)
    ]
    return jnp.concatenate(tiles, axis=1)


def by_head_rows(values):
    rows = iota((256, 128), 0)
    out = jnp.broadcast_to(values[3], (256, 128))
    for h in (2, 1, 0):
        out = jnp.where(rows < 64 * (h + 1), jnp.broadcast_to(values[h], (256, 128)), out)
    return out


def lanes(row):
    return [row[:, h : h + 1] for h in range(4)]


def weights_of(rows, cols):
    seg = cols[:, 12:13]
    prev, last = rows[13:14, 127:128], rows[12:13, 127:128]
    end = cols[127:128, :]
    carry = jnp.where(seg == prev, jnp.exp(cols), 0.0)
    tail = jnp.where(seg == last, jnp.exp(end - cols), 0.0)
    through = jnp.where(last == prev, jnp.exp(end), 0.0)
    return carry, tail, through


def pack_kernel(w_x, w_bc, w_dt, out):
    out[:, 0:1024] = w_x[...]
    out[:, 1024:1280] = w_bc[...]
    out[:, 1280:1408] = jnp.zeros((256, 128), BF16)
    out[:, 1280:1296] = w_dt[...]


def pack(*parts):
    return pl.pallas_call(
        pack_kernel, in_specs=[VMEM] * 3, out_specs=VMEM, out_shape=jax.ShapeDtypeStruct((256, WIDE), BF16)
    )(*parts)


TILES = [(256 * t, min(256 * t + 256, WIDE)) for t in range(6)]
ANY = pl.BlockSpec(memory_space=pl.ANY)


def ring_rows(meta, i):
    place = lax.rem(meta[3] + (0, 7, 1, 6, 2, 5, 3, 4)[i], 8)
    row = lax.rem(place // 4 + meta[0], 2) * 1024 + lax.rem(place, 4) * 256
    return pl.multiple_of(row, 256)


def project_kernel(meta, own, oth, probe, *rest):
    blocks, (out, kept), (buf, rows, sems, out_sem) = rest[:9], rest[9:11], rest[11:]
    copies = []
    for i in range(7):
        there = buf.at[pl.ds(ring_rows(meta, i), 256)]
        copies.append(pltpu.make_async_copy(blocks[i], there, sems.at[i]))
    for n in range(2):
        there = buf.at[pl.ds(pl.multiple_of(ring_rows(meta, 7) + 128 * n, 128), 128)]
        copies.append(pltpu.make_async_copy(blocks[7 + n], there, sems.at[7 + n]))
    store = pltpu.make_async_copy(buf, kept, out_sem)
    for copy in copies:
        copy.start()
    for n, ref in enumerate((own, oth)):
        for k in range(4):
            rows[128 * k : 128 * k + 128, 1024 * n : 1024 * n + 1024] = ref[lax.rem(k + meta[1], 4)]
    ids = probe[128:144, 0:512].astype(F32)[0:8]
    for d in range(4):
        part = slice(256 * d, 256 * d + 256)
        out[d, 528:592, 0:256] = probe[0:64, part]
        out[d, 528:592, 256:512] = probe[64:128, part]
    for copy in copies:
        copy.wait()
    store.start()
    for t, (lo, hi) in enumerate(TILES):
        total = dot_nn(rows[...], buf[:, lo:hi])
        if t < 4:
            out[t, 0:512, 0:256] = total.astype(BF16)
        elif t == 4:
            for d in range(4):
                out[d, 0:512, 256:512] = total.astype(BF16)
        else:
            steps = total.T
            for d in range(4):
                mine = jnp.concatenate([steps[4 * d : 4 * d + 4], jnp.zeros((4, 512), F32), ids], axis=0)
                out[d, 512:528, :] = mine.astype(BF16)
    store.wait()


def project(meta, own, oth, probe, blocks):
    return pl.pallas_call(
        project_kernel,
        in_specs=[SMEM, VMEM, VMEM, VMEM] + [ANY] * 9,
        out_specs=[VMEM, ANY],
        out_shape=[jax.ShapeDtypeStruct((4, 592, 512), BF16), jax.ShapeDtypeStruct((2048, WIDE), BF16)],
        scratch_shapes=[
            pltpu.VMEM((2048, WIDE), BF16),
            pltpu.VMEM((512, 2048), BF16),
            pltpu.SemaphoreType.DMA((9,)),
            pltpu.SemaphoreType.DMA,
        ],
    )(meta, own, oth, probe, *blocks)


def prepare_kernel(meta, r, prm, pay, x, bc, rows_out, cols_out, t_out, q_out, p):
    total = r[0, 0:512, :].astype(F32)
    raw = r[0, 512:528, :].astype(F32)
    for d in range(1, 4):
        total += r[d, 0:512, :].astype(F32)
        raw += r[d, 512:528, :].astype(F32)
    x[...] = total[:, 0:256]
    bc[...] = total[:, 256:512].astype(BF16)
    upper = (iota((128, 128), 0) <= iota((128, 128), 1)).astype(F32)
    top = iota((8, 128), 0) < 4
    bias, rate = prm[0], prm[1]
    through = []
    for k in range(4):
        here = slice(128 * k, 128 * k + 128)
        z = raw[0:8, here] + bias
        dt = jnp.maximum(z, 0.0) + jnp.log1p(jnp.exp(-jnp.abs(z)))
        logs = jnp.dot(-dt * rate, upper, precision=HIGH, preferred_element_type=F32)
        source = lax.rem(k + meta[1], 4)
        p[k, 0:64, :] = r[source, 528:592, 0:256]
        p[k, 64:128, :] = r[source, 528:592, 256:512]
        seg = r[source, 512:528, 0:128].astype(F32)[8:16]
        rows = jnp.concatenate([jnp.where(top, logs, pltpu.roll(dt, 4, 0)), jnp.where(top, z, pltpu.roll(seg, 4, 0))], axis=0)
        cols = jnp.concatenate([rows, jnp.zeros((112, 128), F32)], axis=0).T
        rows_out[k] = rows
        cols_out[k] = cols
        carry, tail, thru = weights_of(rows, cols)
        through.append(thru)
        carry_x = spread(lanes(carry))
        tail_x = spread([tail[:, h : h + 1] * cols[:, 4 + h : 5 + h] for h in range(4)])
        b, c = bc[here, 0:128], bc[here, 128:256]
        t_out[k] = dot_tn((x[here, :] * tail_x).astype(BF16), b)
        q_out[k] = dot_tn((p[k, 0:128, :].astype(F32) * carry_x).astype(BF16), c)
    state = t_out[0]
    grad = q_out[3]
    whole = through[0]
    for k in range(1, 4):
        state = by_head_rows(lanes(through[k])) * state + t_out[k]
        grad = by_head_rows(lanes(through[3 - k])) * grad + q_out[3 - k]
        whole = whole * through[k]
    for k in range(1, 4):
        pay[k - 1, 0:256, :] = jnp.where(meta[2] + k < 4, state, grad).astype(BF16)
        pay[k - 1, 256:272, :] = jnp.broadcast_to(whole, (16, 128)).astype(BF16)


def prepare(meta, r, prm):
    return pl.pallas_call(
        prepare_kernel,
        in_specs=[SMEM, VMEM, VMEM],
        out_specs=[VMEM] * 8,
        out_shape=[
            jax.ShapeDtypeStruct((3, 272, 128), BF16),
            jax.ShapeDtypeStruct((512, 256), F32),
            jax.ShapeDtypeStruct((512, 256), BF16),
            jax.ShapeDtypeStruct((4, 16, 128), F32),
            jax.ShapeDtypeStruct((4, 128, 128), F32),
            jax.ShapeDtypeStruct((4, 256, 128), F32),
            jax.ShapeDtypeStruct((4, 256, 128), F32),
            jax.ShapeDtypeStruct((4, 128, 256), BF16),
        ],
    )(meta, r, prm)


def intra_kernel(x, bc, p, rows_in, cols_in, skip, dx, dbc, e):
    seen = iota((128, 128), 0) >= iota((128, 128), 1)
    lane = iota((128, 128), 1)
    k, here = 0, slice(0, 128)
    b, c = bc[here, 0:128], bc[here, 128:256]
    rows, cols = rows_in[k], cols_in[k]
    scores = dot_nt(c, b)
    visible = (cols[:, 12:13] == rows[12:13, :]) & seen
    d_scores = jnp.zeros((128, 128), F32)
    by_row = jnp.zeros((128, 128), F32)
    sums = []
    for tile in range(2):
        part = slice(128 * tile, 128 * tile + 128)
        probe = p[k, 0:128, part].astype(F32)
        values = x[here, part].astype(BF16)
        d_values = skip[:, part] * probe
        for a in range(2):
            h = 2 * tile + a
            mine = jnp.where((lane < 64) if a == 0 else (lane >= 64), probe, 0.0).astype(BF16)
            pulled = dot_nt(mine, values)
            decay = jnp.exp(jnp.where(visible, cols[:, h : h + 1] - rows[h : h + 1, :], -1e30))
            steps = rows[4 + h : 5 + h, :]
            weighted = decay * pulled
            decayed = decay * scores
            plain = weighted * scores
            sums.append(jnp.sum(plain, axis=0, keepdims=True))
            by_row = jnp.where(lane == h, jnp.sum(plain * steps, axis=1, keepdims=True), by_row)
            d_scores += weighted * steps
            d_values += dot_tn((decayed * steps).astype(BF16), mine)
        dx[here, part] = d_values
    d_scores = d_scores.astype(BF16)
    dbc[here, 0:128] = dot_tn(d_scores, c)
    dbc[here, 128:256] = dot_nn(d_scores, b)
    sub = iota((8, 128), 0)
    down = jnp.zeros((8, 128), F32)
    for h in range(4):
        down = jnp.where(sub == h, jnp.broadcast_to(sums[h], (8, 128)), down)
    dt = pltpu.roll(rows[0:8], 4, 0)
    e[k, 0:8, :] = down
    e[k, 8:16, :] = by_row.T[0:8] - dt * down


def intra(x, bc, p, rows, cols, skip):
    tall = pl.BlockSpec((128, 256), lambda i: (i, 0))
    flat = lambda *shape: pl.BlockSpec((1,) + shape, lambda i: (i, 0, 0))
    return pl.pallas_call(
        intra_kernel,
        grid=(4,),
        in_specs=[tall, tall, flat(128, 256), flat(16, 128), flat(128, 128), pl.BlockSpec((1, 256), lambda i: (0, 0))],
        out_specs=[tall, tall, flat(16, 128)],
        out_shape=[
            jax.ShapeDtypeStruct((512, 256), F32),
            jax.ShapeDtypeStruct((512, 256), F32),
            jax.ShapeDtypeStruct((4, 16, 128), F32),
        ],
    )(x, bc, p, rows, cols, skip)


def finish_kernel(meta, r1, r2, r3, x, bc, p, rows_in, cols_in, t_in, q_in, dx, dbc, e, prm, out):
    quarter = meta[2]
    got = (r1, r2, r3)
    parts = [ref[0:256, :].astype(F32) for ref in got]
    decays = [by_head_rows(lanes(ref[256:272, :].astype(F32)[0:1])) for ref in got]

    def total(order):
        out_sum = jnp.zeros((256, 128), F32)
        run = jnp.ones((256, 128), F32)
        for index, valid in order:
            out_sum += jnp.where(valid, run * parts[index], 0.0)
            run = jnp.where(valid, run * decays[index], run)
        return out_sum

    entering = total([(k - 1, quarter - k >= 0) for k in (1, 2, 3)])
    leaving = total([(3 - m, quarter + m <= 3) for m in (1, 2, 3)])
    weights = [weights_of(rows_in[k], cols_in[k]) for k in range(4)]
    through = [by_head_rows(lanes(weights[k][2])) for k in range(4)]
    states, grads = [entering], [leaving]
    for k in range(3):
        states.append(through[k] * states[k] + t_in[k])
        grads.append(through[3 - k] * grads[k] + q_in[3 - k])
    grads = grads[::-1]
    indicator = (iota((8, 256), 1) // 64 == iota((8, 256), 0)).astype(F32)
    lower = (iota((128, 128), 0) >= iota((128, 128), 1)).astype(F32)
    sub, lane = iota((8, 128), 0), iota((8, 128), 1)
    rate = prm[1]

    def by_head(product):
        dims = (((1,), (1,)), ((), ()))
        return lax.dot_general(indicator, product, dims, precision=HIGH, preferred_element_type=F32)

    for k in range(4):
        here = slice(128 * k, 128 * k + 128)
        rows, cols = rows_in[k], cols_in[k]
        carry, tail, thru = weights[k]
        b, c = bc[here, 0:128], bc[here, 128:256]
        carry_x = spread(lanes(carry))
        tail_x = spread(lanes(tail))
        step_x = spread([cols[:, 4 + h : 5 + h] for h in range(4)])
        state, grad = states[k].astype(BF16), grads[k].astype(BF16)
        probe = p[k, 0:128, :].astype(F32) * carry_x
        values = x[here, :] * tail_x
        carried = probe * dot_nt(c, state)
        pulled = dot_nt(b, grad)
        out[here, 0:256] = (dx[here, :] + tail_x * step_x * pulled).astype(BF16)
        d_b = dbc[here, 0:128] + dot_nn((values * step_x).astype(BF16), grad)
        d_c = dbc[here, 128:256] + dot_nn(probe.astype(BF16), state)
        out[here, 256:384] = d_b.astype(BF16)
        out[here, 384:512] = d_c.astype(BF16)
        from_carry = by_head(carried)
        from_tail = by_head(values * pulled)
        dt = pltpu.roll(rows[0:8], 4, 0)
        d_log = e[k, 8:16, :] + from_carry - dt * from_tail
        both = jnp.sum(grads[k] * states[k], axis=1, keepdims=True)
        end = jnp.sum(jnp.where(sub < 4, dt * from_tail, 0.0), axis=1, keepdims=True)
        for h in range(4):
            own = jnp.sum(both[64 * h : 64 * h + 64], axis=0, keepdims=True) * thru[:, h : h + 1]
            end = jnp.where(sub[:, 0:1] == h, end + own, end)
        d_log = jnp.where(lane == 127, d_log + end, d_log)
        d_step = jnp.dot(d_log, lower, precision=HIGH, preferred_element_type=F32)
        d_dt = e[k, 0:8, :] + from_tail - rate * d_step
        z = rows[8:16]
        d_z = jnp.where(sub < 4, d_dt / (1.0 + jnp.exp(-z)), 0.0)
        out[512:528, here] = jnp.concatenate([d_z, jnp.zeros((8, 128), F32)], axis=0).astype(BF16)


def finish(meta, *args):
    return pl.pallas_call(
        finish_kernel,
        in_specs=[SMEM] + [VMEM] * len(args),
        out_specs=VMEM,
        out_shape=jax.ShapeDtypeStruct((528, 512), BF16),
    )(meta, *args)


def pull_half(flip, meta, w, full, out, buf, sems):
    copies = []
    for j in range(4):
        row = 1024 * flip + 256 * j
        copies.append(pltpu.make_async_copy(w.at[row : row + 256], buf.at[j], sems.at[j]))
    for copy in copies:
        copy.start()
    yield
    for j in range(4):
        copies[j].wait()
        part = dot_nn(buf[j], full[...]).T.astype(BF16)
        for k in range(4):
            out[lax.rem(k + meta[1], 4), :, 256 * j : 256 * j + 256] = part[128 * k : 128 * k + 128]
    yield


def pull_first_kernel(meta, g, w, full, out, buf, sems):
    phases = pull_half(1, meta, w, full, out, buf, sems)
    next(phases)
    shared = g[0, 0:512, 256:512].astype(F32)
    for d in range(4):
        full[256 * d : 256 * d + 256, :] = g[d, 0:512, 0:256].astype(F32).T.astype(BF16)
        if d:
            shared += g[d, 0:512, 256:512].astype(F32)
    full[1024:1280, :] = shared.T.astype(BF16)
    top = iota((8, 512), 0) < 4
    steps = [g[d, 512:528, :].astype(F32)[0:8] for d in range(4)]
    pairs = [jnp.where(top, steps[2 * j], pltpu.roll(steps[2 * j + 1], 4, 0)) for j in range(2)]
    full[1280:1408, :] = jnp.concatenate(pairs + [jnp.zeros((112, 512), F32)], axis=0).astype(BF16)
    next(phases)


def pull_second_kernel(meta, full, w, out, buf, sems):
    for _ in pull_half(0, meta, w, full, out, buf, sems):
        pass


PULL_SCRATCH = [pltpu.VMEM((4, 256, WIDE), BF16), pltpu.SemaphoreType.DMA((4,))]
PULLED = jax.ShapeDtypeStruct((4, 128, 1024), BF16)


def pull_first(meta, g, w):
    return pl.pallas_call(
        pull_first_kernel,
        in_specs=[SMEM, VMEM, ANY],
        out_specs=[VMEM] * 2,
        out_shape=[jax.ShapeDtypeStruct((WIDE, 512), BF16), PULLED],
        scratch_shapes=PULL_SCRATCH,
    )(meta, g, w)


def pull_second(meta, full, w):
    return pl.pallas_call(
        pull_second_kernel,
        in_specs=[SMEM, VMEM, ANY],
        out_specs=VMEM,
        out_shape=PULLED,
        scratch_shapes=PULL_SCRATCH,
    )(meta, full, w)


def to_all(x, axis):
    return lax.all_to_all(jnp.broadcast_to(x[None], (4,) + x.shape), axis, split_axis=0, concat_axis=0)


def shifted(x, axis, k):
    return lax.ppermute(x, axis, [(i, (i + k) % 4) for i in range(4)])


def sum_of_four(x, axis):
    return x + shifted(x, axis, 1) + shifted(x, axis, 2) + shifted(x, axis, 3)


SWAP = [(0, 1), (1, 0)]


def body(tokens, frame_feats, w_proj, frame_pos, segments, signs, w_x, w_bc, w_dt, dt_bias, decay_rate, skip_gain, probe):
    x_at, z_at, core_at = lax.axis_index(X), lax.axis_index("z"), lax.axis_index("core")
    across = lax.rem(z_at, 4)
    origin = 2 * lax.rem(across, 2) + across // 2
    quarter = 2 * lax.rem(origin, 2) + z_at // 4
    meta = jnp.stack([core_at, origin, quarter, z_at]).astype(jnp.int32)
    segment = segments[0]
    before = lax.ppermute(segment[-1:], X + ("z",), [(i, i + 1) for i in range(31)])
    ids = jnp.concatenate([segment[None], jnp.broadcast_to(before[None], (15, CHUNK))]).astype(BF16)
    probe_ids = jnp.concatenate([probe[0], jnp.tile(ids, (1, 8))], axis=0)

    def right(v):
        return lax.ppermute(v, "z", [(i, (i + 1) % 8) for i in range(8)])

    def left(v):
        return lax.ppermute(v, "z", [(i, (i + 7) % 8) for i in range(8)])

    w_ring = pack(w_x, w_bc, w_dt)
    r1, l1 = right(w_ring), left(w_ring)
    probe_ids = lax.ppermute(probe_ids, X + ("z",), probe_route())
    frame_emb = jnp.dot(frame_feats[0], w_proj, preferred_element_type=F32).astype(BF16)
    slot = frame_pos[0] - CHUNK * (jnp.arange(32, dtype=jnp.int32) // 2)
    tagged = jnp.concatenate([frame_emb, jnp.broadcast_to(slot.astype(BF16)[:, None], (32, 128))], axis=1)
    arrived = lax.all_to_all(tagged, SEQ, split_axis=0, concat_axis=0, tiled=True)
    local_pos = arrived[:, 1024].astype(jnp.int32)
    merged = tokens[0].at[local_pos].set(arrived[:, :1024])
    moved = lax.ppermute(merged, AXES, features_route())
    r2, l2 = right(r1), left(l1)
    r3, l3 = right(r2), left(l2)
    own = to_all(moved, "y")
    r4, l4 = right(r3[:128]), left(l3[128:])
    oth = lax.ppermute(own, "core", SWAP)

    def four(v):
        return lax.dynamic_slice(v, (4 * x_at,), (4,))

    prm = jnp.stack([four(dt_bias), four(decay_rate)])
    prm = jnp.concatenate([prm, jnp.zeros((2, 4), F32)], axis=1)
    prm = jnp.broadcast_to(prm[:, :, None], (2, 8, 128))
    skip = jnp.repeat(four(skip_gain), 64)[None, :]

    blocks = (w_ring, r1, l1, r2, l2, r3, l3, r4, l4)
    partial_proj, weights = project(meta, own, oth, probe_ids, blocks)
    received = lax.all_to_all(partial_proj, X, split_axis=0, concat_axis=0)
    pay, values, bc, rows, cols, t_all, q_all, probes = prepare(meta, received, prm)
    got = [lax.ppermute(pay[k - 1], "z", quarter_route(k)) for k in (1, 2, 3)]
    dx, dbc, e = intra(values, bc, probes, rows, cols, skip)
    grads = finish(meta, *got, values, bc, probes, rows, cols, t_all, q_all, dx, dbc, e, prm)
    everyone = to_all(grads, X)
    full, oth_part = pull_first(meta, everyone, weights)
    swapped = lax.ppermute(oth_part, "core", SWAP)
    own_part = pull_second(meta, full, weights)
    both = (own_part.astype(F32) + swapped.astype(F32)).astype(BF16)
    pieces = lax.all_to_all(both, "y", split_axis=0, concat_axis=0)
    away = jnp.sum(pieces.astype(F32), axis=0)
    squares = jnp.broadcast_to(jnp.sum(away * away), (8, 128))
    back = [(b, a) for a, b in features_route()]
    gradient = lax.ppermute(away.astype(BF16), AXES, back)
    squares = squares + lax.ppermute(squares, "core", SWAP)
    squares = sum_of_four(squares, X)
    squares = lax.ppermute(squares, AXES, back)[0, 0]

    direction = (2 * signs[0] - 1).astype(F32)[:, None]
    step = 0.5 * direction * gradient.astype(F32)
    picked = (direction.astype(BF16) * gradient)[local_pos]
    high = squares.astype(BF16)
    low = (squares - high.astype(F32)).astype(BF16)
    lane = jnp.arange(128)[None, :]
    tail = jnp.broadcast_to(jnp.where(lane < 64, high, low), (32, 128))
    returned = lax.all_to_all(jnp.concatenate([picked, tail], axis=1), SEQ, split_axis=0, concat_axis=0, tiled=True)
    sums = returned[::2, 1024:].astype(F32)
    entries = 2048 * 8192
    grad_scale = jnp.sqrt((jnp.sum(sums[:, 0]) + jnp.sum(sums[:, 64])) / entries + 1e-06)
    adv = (merged.astype(F32) + step / grad_scale).astype(BF16)
    adv_frames = (frame_emb.astype(F32) + 0.5 * returned[:, :1024].astype(F32) / grad_scale).astype(BF16)
    return (adv[None], adv_frames[None])


def solution(mesh):
    mesh = Mesh(mesh.devices.reshape(2, 2, 8, 4, 2), AXES)

    return jax.shard_map(
        body,
        mesh=mesh,
        in_specs=(
            P("x_hi", SEQ, TENSOR),
            P("x_hi", SEQ, None),
            P(None, TENSOR),
            P("x_hi", SEQ),
            P("x_hi", SEQ),
            P("x_hi", SEQ),
            P(("x_hi",) + SEQ, TENSOR),
            P(("x_hi",) + SEQ, TENSOR),
            P(("x_hi",) + SEQ, TENSOR),
            P(TENSOR),
            P(TENSOR),
            P(TENSOR),
            P("x_hi", SEQ, TENSOR),
        ),
        out_specs=(P("x_hi", SEQ, TENSOR), P("x_hi", SEQ, TENSOR)),
        check_vma=False,
    )
```

```python
import jax
import jax.numpy as jnp
from jax import lax
from jax.experimental import pallas as pl
from jax.experimental.pallas import tpu as pltpu
from jax.sharding import Mesh, PartitionSpec as P


F32, BF16 = jnp.float32, jnp.bfloat16
AXES = ("x_hi", "x_lo", "z", "y", "core")
X = ("x_hi", "x_lo")
SEQ = ("x_lo", "z")
TENSOR = ("y", "core")
CHUNK = 128
WIDE = 1408
PLACE = (0, 2, 1, 3)
HIGH = lax.Precision.HIGHEST
VMEM = pl.BlockSpec(memory_space=pltpu.VMEM)
SMEM = pl.BlockSpec(memory_space=pltpu.SMEM)


def linear(x, z, y, core):
    return ((x * 8 + z) * 4 + y) * 2 + core


def features_route():
    pairs = []
    for x in range(4):
        for z in range(8):
            for y in range(4):
                for core in range(2):
                    there = linear(y, 4 * (z // 4) + PLACE[x], (z % 4 + x) % 4, core)
                    pairs.append((linear(x, z, y, core), there))
    return pairs


def probe_route():
    pairs = []
    for x in range(4):
        for z in range(8):
            pairs.append((x * 8 + z, (z % 4 + x) % 4 * 8 + 4 * (z // 4) + PLACE[x]))
    return pairs


def quarter_route(k):
    pairs = []
    for z in range(8):
        home = PLACE[z % 4]
        to = (2 * (home % 2) + z // 4 + k) % 4
        pairs.append((z, 4 * (to % 2) + PLACE[home // 2 * 2 + to // 2]))
    return pairs


def dot_nt(a, b):
    return lax.dot_general(a, b, (((1,), (1,)), ((), ())), preferred_element_type=F32)


def dot_tn(a, b):
    return lax.dot_general(a, b, (((0,), (0,)), ((), ())), preferred_element_type=F32)


def dot_nn(a, b):
    return jnp.dot(a, b, preferred_element_type=F32)


def iota(shape, dim):
    return lax.broadcasted_iota(jnp.int32, shape, dim)


def spread(columns):
    left = iota((CHUNK, 128), 1) < 64
    tiles = [
        jnp.where(left, jnp.broadcast_to(columns[2 * i], (CHUNK, 128)), jnp.broadcast_to(columns[2 * i + 1], (CHUNK, 128)))
        for i in range(2)
    ]
    return jnp.concatenate(tiles, axis=1)


def by_head_rows(values):
    rows = iota((256, 128), 0)
    out = jnp.broadcast_to(values[3], (256, 128))
    for h in (2, 1, 0):
        out = jnp.where(rows < 64 * (h + 1), jnp.broadcast_to(values[h], (256, 128)), out)
    return out


def lanes(row):
    return [row[:, h : h + 1] for h in range(4)]


def weights_of(rows, cols):
    seg = cols[:, 12:13]
    prev, last = rows[13:14, 127:128], rows[12:13, 127:128]
    end = cols[127:128, :]
    carry = jnp.where(seg == prev, jnp.exp(cols), 0.0)
    tail = jnp.where(seg == last, jnp.exp(end - cols), 0.0)
    through = jnp.where(last == prev, jnp.exp(end), 0.0)
    return carry, tail, through


def pack_kernel(w_x, w_bc, w_dt, out):
    out[:, 0:1024] = w_x[...]
    out[:, 1024:1280] = w_bc[...]
    out[:, 1280:1408] = jnp.zeros((256, 128), BF16)
    out[:, 1280:1296] = w_dt[...]


def pack(*parts):
    return pl.pallas_call(
        pack_kernel, in_specs=[VMEM] * 3, out_specs=VMEM, out_shape=jax.ShapeDtypeStruct((256, WIDE), BF16)
    )(*parts)


TILES = [(256 * t, min(256 * t + 256, WIDE)) for t in range(6)]
ANY = pl.BlockSpec(memory_space=pl.ANY)


def ring_rows(meta, i):
    place = lax.rem(meta[3] + (0, 7, 1, 6, 2, 5, 3, 4)[i], 8)
    row = lax.rem(place // 4 + meta[0], 2) * 1024 + lax.rem(place, 4) * 256
    return pl.multiple_of(row, 256)


def project_kernel(meta, own, oth, probe, ids_in, *rest):
    blocks, (out, kept), (buf, rows, sems, out_sem) = rest[:9], rest[9:11], rest[11:]
    copies = []
    for i in range(7):
        there = buf.at[pl.ds(ring_rows(meta, i), 256)]
        copies.append(pltpu.make_async_copy(blocks[i], there, sems.at[i]))
    for n in range(2):
        there = buf.at[pl.ds(pl.multiple_of(ring_rows(meta, 7) + 128 * n, 128), 128)]
        copies.append(pltpu.make_async_copy(blocks[7 + n], there, sems.at[7 + n]))
    store = pltpu.make_async_copy(buf, kept, out_sem)
    for copy in copies:
        copy.start()
    for n, ref in enumerate((own, oth)):
        for k in range(4):
            rows[128 * k : 128 * k + 128, 1024 * n : 1024 * n + 1024] = ref[lax.rem(k + meta[1], 4)]
    ids = jnp.concatenate([ids_in[...]] * 4, axis=1)
    for d in range(4):
        part = slice(256 * d, 256 * d + 256)
        out[d, 528:592, 0:256] = probe[0:64, part]
        out[d, 528:592, 256:512] = probe[64:128, part]
    for copy in copies:
        copy.wait()
    store.start()
    for t, (lo, hi) in enumerate(TILES):
        total = dot_nn(rows[...], buf[:, lo:hi])
        if t < 4:
            out[t, 0:512, 0:256] = total.astype(BF16)
        elif t == 4:
            for d in range(4):
                out[d, 0:512, 256:512] = total.astype(BF16)
        else:
            steps = total.T
            for d in range(4):
                mine = jnp.concatenate([steps[4 * d : 4 * d + 4], jnp.zeros((4, 512), F32), ids], axis=0)
                out[d, 512:528, :] = mine.astype(BF16)
    store.wait()


def project(meta, own, oth, probe, ids, blocks):
    return pl.pallas_call(
        project_kernel,
        in_specs=[SMEM, VMEM, VMEM, VMEM, VMEM] + [ANY] * 9,
        out_specs=[VMEM, ANY],
        out_shape=[jax.ShapeDtypeStruct((4, 592, 512), BF16), jax.ShapeDtypeStruct((2048, WIDE), BF16)],
        scratch_shapes=[
            pltpu.VMEM((2048, WIDE), BF16),
            pltpu.VMEM((512, 2048), BF16),
            pltpu.SemaphoreType.DMA((9,)),
            pltpu.SemaphoreType.DMA,
        ],
    )(meta, own, oth, probe, ids, *blocks)


def prepare_kernel(meta, r, prm, pay, x, bc, rows_out, cols_out, t_out, q_out, p):
    total = r[0, 0:512, :].astype(F32)
    raw = r[0, 512:528, :].astype(F32)
    for d in range(1, 4):
        total += r[d, 0:512, :].astype(F32)
        raw += r[d, 512:528, :].astype(F32)
    x[...] = total[:, 0:256]
    bc[...] = total[:, 256:512].astype(BF16)
    upper = (iota((128, 128), 0) <= iota((128, 128), 1)).astype(F32)
    top = iota((8, 128), 0) < 4
    bias, rate = prm[0], prm[1]
    through = []
    for k in range(4):
        here = slice(128 * k, 128 * k + 128)
        z = raw[0:8, here] + bias
        dt = jnp.maximum(z, 0.0) + jnp.log1p(jnp.exp(-jnp.abs(z)))
        logs = jnp.dot(-dt * rate, upper, precision=HIGH, preferred_element_type=F32)
        source = lax.rem(k + meta[1], 4)
        p[k, 0:64, :] = r[source, 528:592, 0:256]
        p[k, 64:128, :] = r[source, 528:592, 256:512]
        seg = r[source, 512:528, 0:128].astype(F32)[8:16]
        rows = jnp.concatenate([jnp.where(top, logs, pltpu.roll(dt, 4, 0)), jnp.where(top, z, pltpu.roll(seg, 4, 0))], axis=0)
        cols = jnp.concatenate([rows, jnp.zeros((112, 128), F32)], axis=0).T
        rows_out[k] = rows
        cols_out[k] = cols
        carry, tail, thru = weights_of(rows, cols)
        through.append(thru)
        carry_x = spread(lanes(carry))
        tail_x = spread([tail[:, h : h + 1] * cols[:, 4 + h : 5 + h] for h in range(4)])
        b, c = bc[here, 0:128], bc[here, 128:256]
        t_out[k] = dot_tn((x[here, :] * tail_x).astype(BF16), b)
        q_out[k] = dot_tn((p[k, 0:128, :].astype(F32) * carry_x).astype(BF16), c)
    state = t_out[0]
    grad = q_out[3]
    whole = through[0]
    for k in range(1, 4):
        state = by_head_rows(lanes(through[k])) * state + t_out[k]
        grad = by_head_rows(lanes(through[3 - k])) * grad + q_out[3 - k]
        whole = whole * through[k]
    for k in range(1, 4):
        pay[k - 1, 0:256, :] = jnp.where(meta[2] + k < 4, state, grad).astype(BF16)
        pay[k - 1, 256:272, :] = jnp.broadcast_to(whole, (16, 128)).astype(BF16)


def prepare(meta, r, prm):
    return pl.pallas_call(
        prepare_kernel,
        in_specs=[SMEM, VMEM, VMEM],
        out_specs=[VMEM] * 8,
        out_shape=[
            jax.ShapeDtypeStruct((3, 272, 128), BF16),
            jax.ShapeDtypeStruct((512, 256), F32),
            jax.ShapeDtypeStruct((512, 256), BF16),
            jax.ShapeDtypeStruct((4, 16, 128), F32),
            jax.ShapeDtypeStruct((4, 128, 128), F32),
            jax.ShapeDtypeStruct((4, 256, 128), F32),
            jax.ShapeDtypeStruct((4, 256, 128), F32),
            jax.ShapeDtypeStruct((4, 128, 256), BF16),
        ],
    )(meta, r, prm)


def intra_kernel(x, bc, p, rows_in, cols_in, skip, dx, dbc, e):
    seen = iota((128, 128), 0) >= iota((128, 128), 1)
    lane = iota((128, 128), 1)
    k, here = 0, slice(0, 128)
    b, c = bc[here, 0:128], bc[here, 128:256]
    rows, cols = rows_in[k], cols_in[k]
    scores = dot_nt(c, b)
    visible = (cols[:, 12:13] == rows[12:13, :]) & seen
    d_scores = jnp.zeros((128, 128), F32)
    by_row = jnp.zeros((128, 128), F32)
    sums = []
    for tile in range(2):
        part = slice(128 * tile, 128 * tile + 128)
        probe = p[k, 0:128, part].astype(F32)
        values = x[here, part].astype(BF16)
        d_values = skip[:, part] * probe
        for a in range(2):
            h = 2 * tile + a
            mine = jnp.where((lane < 64) if a == 0 else (lane >= 64), probe, 0.0).astype(BF16)
            pulled = dot_nt(mine, values)
            decay = jnp.exp(jnp.where(visible, cols[:, h : h + 1] - rows[h : h + 1, :], -1e30))
            steps = rows[4 + h : 5 + h, :]
            weighted = decay * pulled
            decayed = decay * scores
            plain = weighted * scores
            sums.append(jnp.sum(plain, axis=0, keepdims=True))
            by_row = jnp.where(lane == h, jnp.sum(plain * steps, axis=1, keepdims=True), by_row)
            d_scores += weighted * steps
            d_values += dot_tn((decayed * steps).astype(BF16), mine)
        dx[here, part] = d_values
    d_scores = d_scores.astype(BF16)
    dbc[here, 0:128] = dot_tn(d_scores, c)
    dbc[here, 128:256] = dot_nn(d_scores, b)
    sub = iota((8, 128), 0)
    down = jnp.zeros((8, 128), F32)
    for h in range(4):
        down = jnp.where(sub == h, jnp.broadcast_to(sums[h], (8, 128)), down)
    dt = pltpu.roll(rows[0:8], 4, 0)
    e[k, 0:8, :] = down
    e[k, 8:16, :] = by_row.T[0:8] - dt * down


def intra(x, bc, p, rows, cols, skip):
    tall = pl.BlockSpec((128, 256), lambda i: (i, 0))
    flat = lambda *shape: pl.BlockSpec((1,) + shape, lambda i: (i, 0, 0))
    return pl.pallas_call(
        intra_kernel,
        grid=(4,),
        in_specs=[tall, tall, flat(128, 256), flat(16, 128), flat(128, 128), pl.BlockSpec((1, 256), lambda i: (0, 0))],
        out_specs=[tall, tall, flat(16, 128)],
        out_shape=[
            jax.ShapeDtypeStruct((512, 256), F32),
            jax.ShapeDtypeStruct((512, 256), F32),
            jax.ShapeDtypeStruct((4, 16, 128), F32),
        ],
    )(x, bc, p, rows, cols, skip)


def finish_kernel(meta, r1, r2, r3, x, bc, p, rows_in, cols_in, t_in, q_in, dx, dbc, e, prm, out):
    quarter = meta[2]
    got = (r1, r2, r3)
    parts = [ref[0:256, :].astype(F32) for ref in got]
    decays = [by_head_rows(lanes(ref[256:272, :].astype(F32)[0:1])) for ref in got]

    def total(order):
        out_sum = jnp.zeros((256, 128), F32)
        run = jnp.ones((256, 128), F32)
        for index, valid in order:
            out_sum += jnp.where(valid, run * parts[index], 0.0)
            run = jnp.where(valid, run * decays[index], run)
        return out_sum

    entering = total([(k - 1, quarter - k >= 0) for k in (1, 2, 3)])
    leaving = total([(3 - m, quarter + m <= 3) for m in (1, 2, 3)])
    weights = [weights_of(rows_in[k], cols_in[k]) for k in range(4)]
    through = [by_head_rows(lanes(weights[k][2])) for k in range(4)]
    states, grads = [entering], [leaving]
    for k in range(3):
        states.append(through[k] * states[k] + t_in[k])
        grads.append(through[3 - k] * grads[k] + q_in[3 - k])
    grads = grads[::-1]
    indicator = (iota((8, 256), 1) // 64 == iota((8, 256), 0)).astype(F32)
    lower = (iota((128, 128), 0) >= iota((128, 128), 1)).astype(F32)
    sub, lane = iota((8, 128), 0), iota((8, 128), 1)
    rate = prm[1]

    def by_head(product):
        dims = (((1,), (1,)), ((), ()))
        return lax.dot_general(indicator, product, dims, precision=HIGH, preferred_element_type=F32)

    for k in range(4):
        here = slice(128 * k, 128 * k + 128)
        rows, cols = rows_in[k], cols_in[k]
        carry, tail, thru = weights[k]
        b, c = bc[here, 0:128], bc[here, 128:256]
        carry_x = spread(lanes(carry))
        tail_x = spread(lanes(tail))
        step_x = spread([cols[:, 4 + h : 5 + h] for h in range(4)])
        state, grad = states[k].astype(BF16), grads[k].astype(BF16)
        probe = p[k, 0:128, :].astype(F32) * carry_x
        values = x[here, :] * tail_x
        carried = probe * dot_nt(c, state)
        pulled = dot_nt(b, grad)
        out[here, 0:256] = (dx[here, :] + tail_x * step_x * pulled).astype(BF16)
        d_b = dbc[here, 0:128] + dot_nn((values * step_x).astype(BF16), grad)
        d_c = dbc[here, 128:256] + dot_nn(probe.astype(BF16), state)
        out[here, 256:384] = d_b.astype(BF16)
        out[here, 384:512] = d_c.astype(BF16)
        from_carry = by_head(carried)
        from_tail = by_head(values * pulled)
        dt = pltpu.roll(rows[0:8], 4, 0)
        d_log = e[k, 8:16, :] + from_carry - dt * from_tail
        both = jnp.sum(grads[k] * states[k], axis=1, keepdims=True)
        end = jnp.sum(jnp.where(sub < 4, dt * from_tail, 0.0), axis=1, keepdims=True)
        for h in range(4):
            own = jnp.sum(both[64 * h : 64 * h + 64], axis=0, keepdims=True) * thru[:, h : h + 1]
            end = jnp.where(sub[:, 0:1] == h, end + own, end)
        d_log = jnp.where(lane == 127, d_log + end, d_log)
        d_step = jnp.dot(d_log, lower, precision=HIGH, preferred_element_type=F32)
        d_dt = e[k, 0:8, :] + from_tail - rate * d_step
        z = rows[8:16]
        d_z = jnp.where(sub < 4, d_dt / (1.0 + jnp.exp(-z)), 0.0)
        out[512:528, here] = jnp.concatenate([d_z, jnp.zeros((8, 128), F32)], axis=0).astype(BF16)


def finish(meta, *args):
    return pl.pallas_call(
        finish_kernel,
        in_specs=[SMEM] + [VMEM] * len(args),
        out_specs=VMEM,
        out_shape=jax.ShapeDtypeStruct((528, 512), BF16),
    )(meta, *args)


def pull_half(flip, meta, w, full, out, buf, sems):
    copies = []
    for j in range(4):
        row = 1024 * flip + 256 * j
        copies.append(pltpu.make_async_copy(w.at[row : row + 256], buf.at[j], sems.at[j]))
    for copy in copies:
        copy.start()
    yield
    for j in range(4):
        copies[j].wait()
        part = dot_nn(buf[j], full[...]).T.astype(BF16)
        for k in range(4):
            out[lax.rem(k + meta[1], 4), :, 256 * j : 256 * j + 256] = part[128 * k : 128 * k + 128]
    yield


def pull_first_kernel(meta, g, w, full, out, buf, sems):
    phases = pull_half(1, meta, w, full, out, buf, sems)
    next(phases)
    shared = g[0, 0:512, 256:512].astype(F32)
    for d in range(4):
        full[256 * d : 256 * d + 256, :] = g[d, 0:512, 0:256].astype(F32).T.astype(BF16)
        if d:
            shared += g[d, 0:512, 256:512].astype(F32)
    full[1024:1280, :] = shared.T.astype(BF16)
    top = iota((8, 512), 0) < 4
    steps = [g[d, 512:528, :].astype(F32)[0:8] for d in range(4)]
    pairs = [jnp.where(top, steps[2 * j], pltpu.roll(steps[2 * j + 1], 4, 0)) for j in range(2)]
    full[1280:1408, :] = jnp.concatenate(pairs + [jnp.zeros((112, 512), F32)], axis=0).astype(BF16)
    next(phases)


def pull_second_kernel(meta, full, w, out, buf, sems):
    for _ in pull_half(0, meta, w, full, out, buf, sems):
        pass


PULL_SCRATCH = [pltpu.VMEM((4, 256, WIDE), BF16), pltpu.SemaphoreType.DMA((4,))]
PULLED = jax.ShapeDtypeStruct((4, 128, 1024), BF16)


def pull_first(meta, g, w):
    return pl.pallas_call(
        pull_first_kernel,
        in_specs=[SMEM, VMEM, ANY],
        out_specs=[VMEM] * 2,
        out_shape=[jax.ShapeDtypeStruct((WIDE, 512), BF16), PULLED],
        scratch_shapes=PULL_SCRATCH,
    )(meta, g, w)


def pull_second(meta, full, w):
    return pl.pallas_call(
        pull_second_kernel,
        in_specs=[SMEM, VMEM, ANY],
        out_specs=VMEM,
        out_shape=PULLED,
        scratch_shapes=PULL_SCRATCH,
    )(meta, full, w)


def to_all(x, axis):
    return lax.all_to_all(jnp.broadcast_to(x[None], (4,) + x.shape), axis, split_axis=0, concat_axis=0)


def shifted(x, axis, k):
    return lax.ppermute(x, axis, [(i, (i + k) % 4) for i in range(4)])


def sum_of_four(x, axis):
    return x + shifted(x, axis, 1) + shifted(x, axis, 2) + shifted(x, axis, 3)


SWAP = [(0, 1), (1, 0)]


def body(tokens, frame_feats, w_proj, frame_pos, segments, signs, w_x, w_bc, w_dt, dt_bias, decay_rate, skip_gain, probe):
    x_at, z_at, core_at = lax.axis_index(X), lax.axis_index("z"), lax.axis_index("core")
    across = lax.rem(z_at, 4)
    origin = 2 * lax.rem(across, 2) + across // 2
    quarter = 2 * lax.rem(origin, 2) + z_at // 4
    meta = jnp.stack([core_at, origin, quarter, z_at]).astype(jnp.int32)
    segment = segments[0]
    before = lax.ppermute(segment[-1:], X + ("z",), [(i, i + 1) for i in range(31)])
    ids = jnp.concatenate([segment[None], jnp.broadcast_to(before[None], (7, CHUNK))]).astype(F32)
    ids = lax.ppermute(ids, X + ("z",), probe_route())

    def right(v):
        return lax.ppermute(v, "z", [(i, (i + 1) % 8) for i in range(8)])

    def left(v):
        return lax.ppermute(v, "z", [(i, (i + 7) % 8) for i in range(8)])

    w_ring = pack(w_x, w_bc, w_dt)
    r1, l1 = right(w_ring), left(w_ring)
    probe_moved = lax.ppermute(probe[0], X + ("z",), probe_route())
    frame_emb = jnp.dot(frame_feats[0], w_proj, preferred_element_type=F32).astype(BF16)
    slot = frame_pos[0] - CHUNK * (jnp.arange(32, dtype=jnp.int32) // 2)
    tagged = jnp.concatenate([frame_emb, jnp.broadcast_to(slot.astype(BF16)[:, None], (32, 128))], axis=1)
    arrived = lax.all_to_all(tagged, SEQ, split_axis=0, concat_axis=0, tiled=True)
    local_pos = arrived[:, 1024].astype(jnp.int32)
    merged = tokens[0].at[local_pos].set(arrived[:, :1024])
    moved = lax.ppermute(merged, AXES, features_route())
    r2, l2 = right(r1), left(l1)
    r3, l3 = right(r2), left(l2)
    own = to_all(moved, "y")
    r4, l4 = right(r3[:128]), left(l3[128:])
    oth = lax.ppermute(own, "core", SWAP)

    def four(v):
        return lax.dynamic_slice(v, (4 * x_at,), (4,))

    prm = jnp.stack([four(dt_bias), four(decay_rate)])
    prm = jnp.concatenate([prm, jnp.zeros((2, 4), F32)], axis=1)
    prm = jnp.broadcast_to(prm[:, :, None], (2, 8, 128))
    skip = jnp.repeat(four(skip_gain), 64)[None, :]

    blocks = (w_ring, r1, l1, r2, l2, r3, l3, r4, l4)
    partial_proj, weights = project(meta, own, oth, probe_moved, ids, blocks)
    received = lax.all_to_all(partial_proj, X, split_axis=0, concat_axis=0)
    pay, values, bc, rows, cols, t_all, q_all, probes = prepare(meta, received, prm)
    got = [lax.ppermute(pay[k - 1], "z", quarter_route(k)) for k in (1, 2, 3)]
    dx, dbc, e = intra(values, bc, probes, rows, cols, skip)
    grads = finish(meta, *got, values, bc, probes, rows, cols, t_all, q_all, dx, dbc, e, prm)
    everyone = to_all(grads, X)
    full, oth_part = pull_first(meta, everyone, weights)
    swapped = lax.ppermute(oth_part, "core", SWAP)
    own_part = pull_second(meta, full, weights)
    both = (own_part.astype(F32) + swapped.astype(F32)).astype(BF16)
    pieces = lax.all_to_all(both, "y", split_axis=0, concat_axis=0)
    away = jnp.sum(pieces.astype(F32), axis=0)
    squares = jnp.broadcast_to(jnp.sum(away * away), (8, 128))
    back = [(b, a) for a, b in features_route()]
    gradient = lax.ppermute(away.astype(BF16), AXES, back)
    squares = squares + lax.ppermute(squares, "core", SWAP)
    squares = sum_of_four(squares, X)
    squares = lax.ppermute(squares, AXES, back)[0, 0]

    direction = (2 * signs[0] - 1).astype(F32)[:, None]
    step = 0.5 * direction * gradient.astype(F32)
    picked = (direction.astype(BF16) * gradient)[local_pos]
    high = squares.astype(BF16)
    low = (squares - high.astype(F32)).astype(BF16)
    lane = jnp.arange(128)[None, :]
    tail = jnp.broadcast_to(jnp.where(lane < 64, high, low), (32, 128))
    returned = lax.all_to_all(jnp.concatenate([picked, tail], axis=1), SEQ, split_axis=0, concat_axis=0, tiled=True)
    sums = returned[::2, 1024:].astype(F32)
    entries = 2048 * 8192
    grad_scale = jnp.sqrt((jnp.sum(sums[:, 0]) + jnp.sum(sums[:, 64])) / entries + 1e-06)
    adv = (merged.astype(F32) + step / grad_scale).astype(BF16)
    adv_frames = (frame_emb.astype(F32) + 0.5 * returned[:, :1024].astype(F32) / grad_scale).astype(BF16)
    return (adv[None], adv_frames[None])


def solution(mesh):
    mesh = Mesh(mesh.devices.reshape(2, 2, 8, 4, 2), AXES)

    return jax.shard_map(
        body,
        mesh=mesh,
        in_specs=(
            P("x_hi", SEQ, TENSOR),
            P("x_hi", SEQ, None),
            P(None, TENSOR),
            P("x_hi", SEQ),
            P("x_hi", SEQ),
            P("x_hi", SEQ),
            P(("x_hi",) + SEQ, TENSOR),
            P(("x_hi",) + SEQ, TENSOR),
            P(("x_hi",) + SEQ, TENSOR),
            P(TENSOR),
            P(TENSOR),
            P(TENSOR),
            P("x_hi", SEQ, TENSOR),
        ),
        out_specs=(P("x_hi", SEQ, TENSOR), P("x_hi", SEQ, TENSOR)),
        check_vma=False,
    )
```

```python
import jax
import jax.numpy as jnp
from jax import lax
from jax.experimental import pallas as pl
from jax.experimental.pallas import tpu as pltpu
from jax.sharding import Mesh, PartitionSpec as P


F32, BF16 = jnp.float32, jnp.bfloat16
AXES = ("x_hi", "x_lo", "z", "y", "core")
X = ("x_hi", "x_lo")
SEQ = ("x_lo", "z")
TENSOR = ("y", "core")
CHUNK = 128
WIDE = 1408
PLACE = (0, 2, 1, 3)
HIGH = lax.Precision.HIGHEST
VMEM = pl.BlockSpec(memory_space=pltpu.VMEM)
SMEM = pl.BlockSpec(memory_space=pltpu.SMEM)


def linear(x, z, y, core):
    return ((x * 8 + z) * 4 + y) * 2 + core


def features_route():
    pairs = []
    for x in range(4):
        for z in range(8):
            for y in range(4):
                for core in range(2):
                    there = linear(y, 4 * (z // 4) + PLACE[x], (z % 4 + x) % 4, core)
                    pairs.append((linear(x, z, y, core), there))
    return pairs


def probe_route():
    pairs = []
    for x in range(4):
        for z in range(8):
            pairs.append((x * 8 + z, (z % 4 + x) % 4 * 8 + 4 * (z // 4) + PLACE[x]))
    return pairs


def quarter_route(k):
    pairs = []
    for z in range(8):
        home = PLACE[z % 4]
        to = (2 * (home % 2) + z // 4 + k) % 4
        pairs.append((z, 4 * (to % 2) + PLACE[home // 2 * 2 + to // 2]))
    return pairs


def dot_nt(a, b):
    return lax.dot_general(a, b, (((1,), (1,)), ((), ())), preferred_element_type=F32)


def dot_tn(a, b):
    return lax.dot_general(a, b, (((0,), (0,)), ((), ())), preferred_element_type=F32)


def dot_nn(a, b):
    return jnp.dot(a, b, preferred_element_type=F32)


def iota(shape, dim):
    return lax.broadcasted_iota(jnp.int32, shape, dim)


def spread(columns):
    left = iota((CHUNK, 128), 1) < 64
    tiles = [
        jnp.where(left, jnp.broadcast_to(columns[2 * i], (CHUNK, 128)), jnp.broadcast_to(columns[2 * i + 1], (CHUNK, 128)))
        for i in range(2)
    ]
    return jnp.concatenate(tiles, axis=1)


def by_head_rows(values):
    rows = iota((256, 128), 0)
    out = jnp.broadcast_to(values[3], (256, 128))
    for h in (2, 1, 0):
        out = jnp.where(rows < 64 * (h + 1), jnp.broadcast_to(values[h], (256, 128)), out)
    return out


def lanes(row):
    return [row[:, h : h + 1] for h in range(4)]


def weights_of(rows, cols):
    seg = cols[:, 12:13]
    prev, last = rows[13:14, 127:128], rows[12:13, 127:128]
    end = cols[127:128, :]
    carry = jnp.where(seg == prev, jnp.exp(cols), 0.0)
    tail = jnp.where(seg == last, jnp.exp(end - cols), 0.0)
    through = jnp.where(last == prev, jnp.exp(end), 0.0)
    return carry, tail, through


def pack_kernel(w_x, w_bc, w_dt, out):
    out[:, 0:1024] = w_x[...]
    out[:, 1024:1280] = w_bc[...]
    out[:, 1280:1408] = jnp.zeros((256, 128), BF16)
    out[:, 1280:1296] = w_dt[...]


def pack(*parts):
    return pl.pallas_call(
        pack_kernel, in_specs=[VMEM] * 3, out_specs=VMEM, out_shape=jax.ShapeDtypeStruct((256, WIDE), BF16)
    )(*parts)


TILES = [(256 * t, min(256 * t + 256, WIDE)) for t in range(6)]
ANY = pl.BlockSpec(memory_space=pl.ANY)


def ring_rows(meta, i):
    place = lax.rem(meta[3] + (0, 7, 1, 6, 2, 5, 3, 4)[i], 8)
    row = lax.rem(place // 4 + meta[0], 2) * 1024 + lax.rem(place, 4) * 256
    return pl.multiple_of(row, 256)


def project_kernel(meta, own, oth, probe, ids_in, *rest):
    blocks, (out, kept), (buf, rows, sems, out_sem) = rest[:9], rest[9:11], rest[11:]
    copies = []
    for i in range(7):
        there = buf.at[pl.ds(ring_rows(meta, i), 256)]
        copies.append(pltpu.make_async_copy(blocks[i], there, sems.at[i]))
    for n in range(2):
        there = buf.at[pl.ds(pl.multiple_of(ring_rows(meta, 7) + 128 * n, 128), 128)]
        copies.append(pltpu.make_async_copy(blocks[7 + n], there, sems.at[7 + n]))
    store = pltpu.make_async_copy(buf, kept, out_sem)
    for copy in copies:
        copy.start()
    for n, ref in enumerate((own, oth)):
        for k in range(4):
            rows[128 * k : 128 * k + 128, 1024 * n : 1024 * n + 1024] = ref[lax.rem(k + meta[1], 4)]
    ids = jnp.concatenate([ids_in[...]] * 4, axis=1)
    for d in range(4):
        part = slice(256 * d, 256 * d + 256)
        out[d, 528:592, 0:256] = probe[0:64, part]
        out[d, 528:592, 256:512] = probe[64:128, part]
    for copy in copies:
        copy.wait()
    store.start()
    for t, (lo, hi) in enumerate(TILES):
        total = dot_nn(rows[...], buf[:, lo:hi])
        if t < 4:
            out[t, 0:512, 0:256] = total.astype(BF16)
        elif t == 4:
            for d in range(4):
                out[d, 0:512, 256:512] = total.astype(BF16)
        else:
            steps = total.T
            for d in range(4):
                mine = jnp.concatenate([steps[4 * d : 4 * d + 4], jnp.zeros((4, 512), F32), ids], axis=0)
                out[d, 512:528, :] = mine.astype(BF16)
    store.wait()


def project(meta, own, oth, probe, ids, blocks):
    return pl.pallas_call(
        project_kernel,
        in_specs=[SMEM, VMEM, VMEM, VMEM, VMEM] + [ANY] * 9,
        out_specs=[VMEM, ANY],
        out_shape=[jax.ShapeDtypeStruct((4, 592, 512), BF16), jax.ShapeDtypeStruct((2048, WIDE), BF16)],
        scratch_shapes=[
            pltpu.VMEM((2048, WIDE), BF16),
            pltpu.VMEM((512, 2048), BF16),
            pltpu.SemaphoreType.DMA((9,)),
            pltpu.SemaphoreType.DMA,
        ],
    )(meta, own, oth, probe, ids, *blocks)


def prepare_kernel(meta, r, prm, pay1, pay2, pay3, x, bc, rows_out, cols_out, t_out, q_out, p):
    total = r[0, 0:512, :].astype(F32)
    raw = r[0, 512:528, :].astype(F32)
    for d in range(1, 4):
        total += r[d, 0:512, :].astype(F32)
        raw += r[d, 512:528, :].astype(F32)
    x[...] = total[:, 0:256]
    bc[...] = total[:, 256:512].astype(BF16)
    upper = (iota((128, 128), 0) <= iota((128, 128), 1)).astype(F32)
    top = iota((8, 128), 0) < 4
    bias, rate = prm[0], prm[1]
    through = []
    for k in range(4):
        here = slice(128 * k, 128 * k + 128)
        z = raw[0:8, here] + bias
        dt = jnp.maximum(z, 0.0) + jnp.log1p(jnp.exp(-jnp.abs(z)))
        logs = jnp.dot(-dt * rate, upper, precision=HIGH, preferred_element_type=F32)
        source = lax.rem(k + meta[1], 4)
        p[k, 0:64, :] = r[source, 528:592, 0:256]
        p[k, 64:128, :] = r[source, 528:592, 256:512]
        seg = r[source, 512:528, 0:128].astype(F32)[8:16]
        rows = jnp.concatenate([jnp.where(top, logs, pltpu.roll(dt, 4, 0)), jnp.where(top, z, pltpu.roll(seg, 4, 0))], axis=0)
        cols = jnp.concatenate([rows, jnp.zeros((112, 128), F32)], axis=0).T
        rows_out[k] = rows
        cols_out[k] = cols
        carry, tail, thru = weights_of(rows, cols)
        through.append(thru)
        carry_x = spread(lanes(carry))
        tail_x = spread([tail[:, h : h + 1] * cols[:, 4 + h : 5 + h] for h in range(4)])
        b, c = bc[here, 0:128], bc[here, 128:256]
        t_out[k] = dot_tn((x[here, :] * tail_x).astype(BF16), b)
        q_out[k] = dot_tn((p[k, 0:128, :].astype(F32) * carry_x).astype(BF16), c)
    state = t_out[0]
    grad = q_out[3]
    whole = through[0]
    for k in range(1, 4):
        state = by_head_rows(lanes(through[k])) * state + t_out[k]
        grad = by_head_rows(lanes(through[3 - k])) * grad + q_out[3 - k]
        whole = whole * through[k]
    for k in range(1, 4):
        pay = (pay1, pay2, pay3)[k - 1]
        pay[0:256, :] = jnp.where(meta[2] + k < 4, state, grad).astype(BF16)
        pay[256:272, :] = jnp.broadcast_to(whole, (16, 128)).astype(BF16)


def prepare(meta, r, prm):
    return pl.pallas_call(
        prepare_kernel,
        in_specs=[SMEM, VMEM, VMEM],
        out_specs=[VMEM] * 10,
        out_shape=[
            jax.ShapeDtypeStruct((272, 128), BF16),
            jax.ShapeDtypeStruct((272, 128), BF16),
            jax.ShapeDtypeStruct((272, 128), BF16),
            jax.ShapeDtypeStruct((512, 256), F32),
            jax.ShapeDtypeStruct((512, 256), BF16),
            jax.ShapeDtypeStruct((4, 16, 128), F32),
            jax.ShapeDtypeStruct((4, 128, 128), F32),
            jax.ShapeDtypeStruct((4, 256, 128), F32),
            jax.ShapeDtypeStruct((4, 256, 128), F32),
            jax.ShapeDtypeStruct((4, 128, 256), BF16),
        ],
    )(meta, r, prm)


def intra_kernel(x, bc, p, rows_in, cols_in, skip, dx, dbc, e):
    seen = iota((128, 128), 0) >= iota((128, 128), 1)
    lane = iota((128, 128), 1)
    k, here = 0, slice(0, 128)
    b, c = bc[here, 0:128], bc[here, 128:256]
    rows, cols = rows_in[k], cols_in[k]
    scores = dot_nt(c, b)
    visible = (cols[:, 12:13] == rows[12:13, :]) & seen
    d_scores = jnp.zeros((128, 128), F32)
    by_row = jnp.zeros((128, 128), F32)
    sums = []
    for tile in range(2):
        part = slice(128 * tile, 128 * tile + 128)
        probe = p[k, 0:128, part].astype(F32)
        values = x[here, part].astype(BF16)
        d_values = skip[:, part] * probe
        for a in range(2):
            h = 2 * tile + a
            mine = jnp.where((lane < 64) if a == 0 else (lane >= 64), probe, 0.0).astype(BF16)
            pulled = dot_nt(mine, values)
            decay = jnp.exp(jnp.where(visible, cols[:, h : h + 1] - rows[h : h + 1, :], -1e30))
            steps = rows[4 + h : 5 + h, :]
            weighted = decay * pulled
            decayed = decay * scores
            plain = weighted * scores
            sums.append(jnp.sum(plain, axis=0, keepdims=True))
            by_row = jnp.where(lane == h, jnp.sum(plain * steps, axis=1, keepdims=True), by_row)
            d_scores += weighted * steps
            d_values += dot_tn((decayed * steps).astype(BF16), mine)
        dx[here, part] = d_values
    d_scores = d_scores.astype(BF16)
    dbc[here, 0:128] = dot_tn(d_scores, c)
    dbc[here, 128:256] = dot_nn(d_scores, b)
    sub = iota((8, 128), 0)
    down = jnp.zeros((8, 128), F32)
    for h in range(4):
        down = jnp.where(sub == h, jnp.broadcast_to(sums[h], (8, 128)), down)
    dt = pltpu.roll(rows[0:8], 4, 0)
    e[k, 0:8, :] = down
    e[k, 8:16, :] = by_row.T[0:8] - dt * down


def intra(x, bc, p, rows, cols, skip):
    tall = pl.BlockSpec((128, 256), lambda i: (i, 0))
    flat = lambda *shape: pl.BlockSpec((1,) + shape, lambda i: (i, 0, 0))
    return pl.pallas_call(
        intra_kernel,
        grid=(4,),
        in_specs=[tall, tall, flat(128, 256), flat(16, 128), flat(128, 128), pl.BlockSpec((1, 256), lambda i: (0, 0))],
        out_specs=[tall, tall, flat(16, 128)],
        out_shape=[
            jax.ShapeDtypeStruct((512, 256), F32),
            jax.ShapeDtypeStruct((512, 256), F32),
            jax.ShapeDtypeStruct((4, 16, 128), F32),
        ],
    )(x, bc, p, rows, cols, skip)


def finish_kernel(meta, r1, r2, r3, x, bc, p, rows_in, cols_in, t_in, q_in, dx, dbc, e, prm, copies):
    out = copies.at[0]
    quarter = meta[2]
    got = (r1, r2, r3)
    parts = [ref[0:256, :].astype(F32) for ref in got]
    decays = [by_head_rows(lanes(ref[256:272, :].astype(F32)[0:1])) for ref in got]

    def total(order):
        out_sum = jnp.zeros((256, 128), F32)
        run = jnp.ones((256, 128), F32)
        for index, valid in order:
            out_sum += jnp.where(valid, run * parts[index], 0.0)
            run = jnp.where(valid, run * decays[index], run)
        return out_sum

    entering = total([(k - 1, quarter - k >= 0) for k in (1, 2, 3)])
    leaving = total([(3 - m, quarter + m <= 3) for m in (1, 2, 3)])
    weights = [weights_of(rows_in[k], cols_in[k]) for k in range(4)]
    through = [by_head_rows(lanes(weights[k][2])) for k in range(4)]
    states, grads = [entering], [leaving]
    for k in range(3):
        states.append(through[k] * states[k] + t_in[k])
        grads.append(through[3 - k] * grads[k] + q_in[3 - k])
    grads = grads[::-1]
    indicator = (iota((8, 256), 1) // 64 == iota((8, 256), 0)).astype(F32)
    lower = (iota((128, 128), 0) >= iota((128, 128), 1)).astype(F32)
    sub, lane = iota((8, 128), 0), iota((8, 128), 1)
    rate = prm[1]

    def by_head(product):
        dims = (((1,), (1,)), ((), ()))
        return lax.dot_general(indicator, product, dims, precision=HIGH, preferred_element_type=F32)

    for k in range(4):
        here = slice(128 * k, 128 * k + 128)
        rows, cols = rows_in[k], cols_in[k]
        carry, tail, thru = weights[k]
        b, c = bc[here, 0:128], bc[here, 128:256]
        carry_x = spread(lanes(carry))
        tail_x = spread(lanes(tail))
        step_x = spread([cols[:, 4 + h : 5 + h] for h in range(4)])
        state, grad = states[k].astype(BF16), grads[k].astype(BF16)
        probe = p[k, 0:128, :].astype(F32) * carry_x
        values = x[here, :] * tail_x
        carried = probe * dot_nt(c, state)
        pulled = dot_nt(b, grad)
        out[here, 0:256] = (dx[here, :] + tail_x * step_x * pulled).astype(BF16)
        d_b = dbc[here, 0:128] + dot_nn((values * step_x).astype(BF16), grad)
        d_c = dbc[here, 128:256] + dot_nn(probe.astype(BF16), state)
        out[here, 256:384] = d_b.astype(BF16)
        out[here, 384:512] = d_c.astype(BF16)
        from_carry = by_head(carried)
        from_tail = by_head(values * pulled)
        dt = pltpu.roll(rows[0:8], 4, 0)
        d_log = e[k, 8:16, :] + from_carry - dt * from_tail
        both = jnp.sum(grads[k] * states[k], axis=1, keepdims=True)
        end = jnp.sum(jnp.where(sub < 4, dt * from_tail, 0.0), axis=1, keepdims=True)
        for h in range(4):
            own = jnp.sum(both[64 * h : 64 * h + 64], axis=0, keepdims=True) * thru[:, h : h + 1]
            end = jnp.where(sub[:, 0:1] == h, end + own, end)
        d_log = jnp.where(lane == 127, d_log + end, d_log)
        d_step = jnp.dot(d_log, lower, precision=HIGH, preferred_element_type=F32)
        d_dt = e[k, 0:8, :] + from_tail - rate * d_step
        z = rows[8:16]
        d_z = jnp.where(sub < 4, d_dt / (1.0 + jnp.exp(-z)), 0.0)
        out[512:528, here] = jnp.concatenate([d_z, jnp.zeros((8, 128), F32)], axis=0).astype(BF16)
    for d in range(1, 4):
        copies[d] = copies[0]


def finish(meta, *args):
    return pl.pallas_call(
        finish_kernel,
        in_specs=[SMEM] + [VMEM] * len(args),
        out_specs=VMEM,
        out_shape=jax.ShapeDtypeStruct((4, 528, 512), BF16),
    )(meta, *args)


def pull_half(flip, meta, w, full, out, buf, sems):
    copies = []
    for j in range(4):
        row = 1024 * flip + 256 * j
        copies.append(pltpu.make_async_copy(w.at[row : row + 256], buf.at[j], sems.at[j]))
    for copy in copies:
        copy.start()
    yield
    for j in range(4):
        copies[j].wait()
        part = dot_nn(buf[j], full[...]).T.astype(BF16)
        for k in range(4):
            out[lax.rem(k + meta[1], 4), :, 256 * j : 256 * j + 256] = part[128 * k : 128 * k + 128]
    yield


def pull_first_kernel(meta, g, w, full, out, buf, sems):
    phases = pull_half(1, meta, w, full, out, buf, sems)
    next(phases)
    shared = g[0, 0:512, 256:512].astype(F32)
    for d in range(4):
        full[256 * d : 256 * d + 256, :] = g[d, 0:512, 0:256].astype(F32).T.astype(BF16)
        if d:
            shared += g[d, 0:512, 256:512].astype(F32)
    full[1024:1280, :] = shared.T.astype(BF16)
    top = iota((8, 512), 0) < 4
    steps = [g[d, 512:528, :].astype(F32)[0:8] for d in range(4)]
    pairs = [jnp.where(top, steps[2 * j], pltpu.roll(steps[2 * j + 1], 4, 0)) for j in range(2)]
    full[1280:1408, :] = jnp.concatenate(pairs + [jnp.zeros((112, 512), F32)], axis=0).astype(BF16)
    next(phases)


def pull_second_kernel(meta, full, w, out, buf, sems):
    for _ in pull_half(0, meta, w, full, out, buf, sems):
        pass


PULL_SCRATCH = [pltpu.VMEM((4, 256, WIDE), BF16), pltpu.SemaphoreType.DMA((4,))]
PULLED = jax.ShapeDtypeStruct((4, 128, 1024), BF16)


def pull_first(meta, g, w):
    return pl.pallas_call(
        pull_first_kernel,
        in_specs=[SMEM, VMEM, ANY],
        out_specs=[VMEM] * 2,
        out_shape=[jax.ShapeDtypeStruct((WIDE, 512), BF16), PULLED],
        scratch_shapes=PULL_SCRATCH,
    )(meta, g, w)


def pull_second(meta, full, w):
    return pl.pallas_call(
        pull_second_kernel,
        in_specs=[SMEM, VMEM, ANY],
        out_specs=VMEM,
        out_shape=PULLED,
        scratch_shapes=PULL_SCRATCH,
    )(meta, full, w)


def to_all(x, axis):
    return lax.all_to_all(jnp.broadcast_to(x[None], (4,) + x.shape), axis, split_axis=0, concat_axis=0)


def shifted(x, axis, k):
    return lax.ppermute(x, axis, [(i, (i + k) % 4) for i in range(4)])


def sum_of_four(x, axis):
    return x + shifted(x, axis, 1) + shifted(x, axis, 2) + shifted(x, axis, 3)


SWAP = [(0, 1), (1, 0)]


def body(tokens, frame_feats, w_proj, frame_pos, segments, signs, w_x, w_bc, w_dt, dt_bias, decay_rate, skip_gain, probe):
    x_at, z_at, core_at = lax.axis_index(X), lax.axis_index("z"), lax.axis_index("core")
    across = lax.rem(z_at, 4)
    origin = 2 * lax.rem(across, 2) + across // 2
    quarter = 2 * lax.rem(origin, 2) + z_at // 4
    meta = jnp.stack([core_at, origin, quarter, z_at]).astype(jnp.int32)
    segment = segments[0]
    before = lax.ppermute(segment[-1:], X + ("z",), [(i, i + 1) for i in range(31)])
    ids = jnp.concatenate([segment[None], jnp.broadcast_to(before[None], (7, CHUNK))]).astype(F32)
    ids = lax.ppermute(ids, X + ("z",), probe_route())

    def right(v):
        return lax.ppermute(v, "z", [(i, (i + 1) % 8) for i in range(8)])

    def left(v):
        return lax.ppermute(v, "z", [(i, (i + 7) % 8) for i in range(8)])

    w_ring = pack(w_x, w_bc, w_dt)
    r1, l1 = right(w_ring), left(w_ring)
    probe_moved = lax.ppermute(probe[0], X + ("z",), probe_route())
    frame_emb = jnp.dot(frame_feats[0], w_proj, preferred_element_type=F32).astype(BF16)
    slot = frame_pos[0] - CHUNK * (jnp.arange(32, dtype=jnp.int32) // 2)
    tagged = jnp.concatenate([frame_emb, jnp.broadcast_to(slot.astype(BF16)[:, None], (32, 128))], axis=1)
    arrived = lax.all_to_all(tagged, SEQ, split_axis=0, concat_axis=0, tiled=True)
    local_pos = arrived[:, 1024].astype(jnp.int32)
    merged = tokens[0].at[local_pos].set(arrived[:, :1024])
    moved = lax.ppermute(merged, AXES, features_route())
    r2, l2 = right(r1), left(l1)
    r3, l3 = right(r2), left(l2)
    own = to_all(moved, "y")
    r4, l4 = right(r3[:128]), left(l3[128:])
    oth = lax.ppermute(own, "core", SWAP)

    def four(v):
        return lax.dynamic_slice(v, (4 * x_at,), (4,))

    prm = jnp.stack([four(dt_bias), four(decay_rate)])
    prm = jnp.concatenate([prm, jnp.zeros((2, 4), F32)], axis=1)
    prm = jnp.broadcast_to(prm[:, :, None], (2, 8, 128))
    skip = jnp.repeat(four(skip_gain), 64)[None, :]

    blocks = (w_ring, r1, l1, r2, l2, r3, l3, r4, l4)
    partial_proj, weights = project(meta, own, oth, probe_moved, ids, blocks)
    received = lax.all_to_all(partial_proj, X, split_axis=0, concat_axis=0)
    *pay, values, bc, rows, cols, t_all, q_all, probes = prepare(meta, received, prm)
    got = [lax.ppermute(pay[k - 1], "z", quarter_route(k)) for k in (1, 2, 3)]
    dx, dbc, e = intra(values, bc, probes, rows, cols, skip)
    grads = finish(meta, *got, values, bc, probes, rows, cols, t_all, q_all, dx, dbc, e, prm)
    everyone = lax.all_to_all(grads, X, split_axis=0, concat_axis=0)
    full, oth_part = pull_first(meta, everyone, weights)
    swapped = lax.ppermute(oth_part, "core", SWAP)
    own_part = pull_second(meta, full, weights)
    both = (own_part.astype(F32) + swapped.astype(F32)).astype(BF16)
    pieces = lax.all_to_all(both, "y", split_axis=0, concat_axis=0)
    away = jnp.sum(pieces.astype(F32), axis=0)
    squares = jnp.broadcast_to(jnp.sum(away * away), (8, 128))
    back = [(b, a) for a, b in features_route()]
    gradient = lax.ppermute(away.astype(BF16), AXES, back)
    squares = squares + lax.ppermute(squares, "core", SWAP)
    squares = sum_of_four(squares, X)
    squares = lax.ppermute(squares, AXES, back)[0, 0]

    direction = (2 * signs[0] - 1).astype(F32)[:, None]
    step = 0.5 * direction * gradient.astype(F32)
    picked = (direction.astype(BF16) * gradient)[local_pos]
    high = squares.astype(BF16)
    low = (squares - high.astype(F32)).astype(BF16)
    lane = jnp.arange(128)[None, :]
    tail = jnp.broadcast_to(jnp.where(lane < 64, high, low), (32, 128))
    returned = lax.all_to_all(jnp.concatenate([picked, tail], axis=1), SEQ, split_axis=0, concat_axis=0, tiled=True)
    sums = returned[::2, 1024:].astype(F32)
    entries = 2048 * 8192
    grad_scale = jnp.sqrt((jnp.sum(sums[:, 0]) + jnp.sum(sums[:, 64])) / entries + 1e-06)
    adv = (merged.astype(F32) + step / grad_scale).astype(BF16)
    adv_frames = (frame_emb.astype(F32) + 0.5 * returned[:, :1024].astype(F32) / grad_scale).astype(BF16)
    return (adv[None], adv_frames[None])


def solution(mesh):
    mesh = Mesh(mesh.devices.reshape(2, 2, 8, 4, 2), AXES)

    return jax.shard_map(
        body,
        mesh=mesh,
        in_specs=(
            P("x_hi", SEQ, TENSOR),
            P("x_hi", SEQ, None),
            P(None, TENSOR),
            P("x_hi", SEQ),
            P("x_hi", SEQ),
            P("x_hi", SEQ),
            P(("x_hi",) + SEQ, TENSOR),
            P(("x_hi",) + SEQ, TENSOR),
            P(("x_hi",) + SEQ, TENSOR),
            P(TENSOR),
            P(TENSOR),
            P(TENSOR),
            P("x_hi", SEQ, TENSOR),
        ),
        out_specs=(P("x_hi", SEQ, TENSOR), P("x_hi", SEQ, TENSOR)),
        check_vma=False,
    )
```
